256 devices in a mesh: dp: 4 (over y), tensor: 16 (over z, core), owner: 4 (over x).
Axes of the slice: x: 4, y: 4, z: 8, core: 2. Of those that a mesh axis runs over, the one named last changes fastest.
Arguments:
- queries: bfloat16 [512, 8192], P(('dp', 'tensor'), 'owner'), may hold values from -360 to 360
- cached_key_rows: bfloat16 [512, 512, 8, 128], P(('dp', 'tensor'), None, 'owner'), may hold values from -6 to 6
- cached_value_rows: bfloat16 [512, 512, 8, 128], P(('dp', 'tensor'), None, 'owner'), may hold values from -6 to 6
- newest_key: bfloat16 [512, 8, 128], P(('dp', 'tensor'), 'owner'), may hold values from -6 to 6
- newest_value: bfloat16 [512, 8, 128], P(('dp', 'tensor'), 'owner'), may hold values from -6 to 6
- output_weight: bfloat16 [8, 1024, 8192], P('owner', 'tensor'), may hold values from -0.75 to 0.75
- adapter_down_weight: bfloat16 [128, 8, 1024, 64], P('owner', None, 'tensor'), may hold values from -0.5 to 0.5
- adapter_up_weight: bfloat16 [128, 64, 8192], P('owner', None, 'tensor'), may hold values from -0.75 to 0.75
- adapter_store_row: int32 [128], replicated, may hold values from 0 to 127, each once
- adapters_by_group: int32 [4, 16], P('dp'), may hold values from 0 to 127, as said below
- adapter_per_row: int32 [512], P('dp'), may hold values from 0 to 127, as said below
Outputs:
- output: bfloat16 [512, 8192], P('dp', ('tensor', 'owner'))
The draws below stay inside these ranges and needn't reach their ends.
Inputs may be any that keep to these rules, and one draw needn't show every extreme that they name: `adapter_per_row`: the rows g * 128 to (g + 1) * 128 - 1 form dp group g; each row's adapter is one of its group's listed adapters, and each listed one is used by some row of the group. `adapters_by_group`: the 16 adapters of a group are distinct.
All inputs are finite; a program needn't handle non-finite values.
Results may differ from the reference program's by a relative error of at most 0.015.
Values may be sent and summed in bfloat16 or wider, within the bound.
No kernel may reach another device: no remote copies, remote signals or barrier semaphores. Data moves between devices by JAX's collectives and lax.ppermute only.
A program may use at most 128 MiB of HBM per device.

```python
import jax
import jax.numpy as jnp
from jax import lax

KEY_HEADS = 8
HEAD_SIZE = 128
ADAPTER_RANK = 64
CTX = 512
SLOTS = 16
MODEL_WIDTH = 8192
QUERY_PER_KEY = 8
ADAPTER_COUNT = 128
ROWS_DEV = 128
ROWS = 512
GROUPS = 4


def assignment(key):
    inner_key = jax.random.fold_in(key, 11)

    def one_group(group_index):
        return jax.random.permutation(jax.random.fold_in(inner_key, group_index), ADAPTER_COUNT)[:SLOTS]
    listing = jax.vmap(one_group)(jnp.arange(GROUPS, dtype=jnp.int32))
    slot_pick = jax.random.randint(jax.random.fold_in(inner_key, 5000), (GROUPS, ROWS_DEV), 0, SLOTS)
    positions = jnp.arange(ROWS_DEV, dtype=jnp.int32)[None, :]
    slot_pick = jnp.where(positions < SLOTS, positions % SLOTS, slot_pick)
    picked = jnp.take_along_axis(listing, slot_pick, axis=1)
    return (listing.astype(jnp.int32), picked.reshape(ROWS).astype(jnp.int32))


def draw_adapters_by_group(key, part):
    return assignment(key)[0]


def draw_adapter_per_row(key, part):
    return assignment(key)[1]


def draw_queries(key, part):
    drawn = jax.random.truncated_normal(key, -6.0, 6.0, (ROWS, MODEL_WIDTH), jnp.float32)
    return drawn.astype(jnp.bfloat16)


def raised(values, rng, source, target, blocks, factor):
    def block_of(position):
        return (jnp.arange(values.shape[position]) // (values.shape[position] // blocks)).reshape((-1,) + (1,) * (values.ndim - 1 - position))

    first = jax.random.permutation(rng, blocks)[block_of(target)]
    second = (block_of(target) + blocks // 2) % blocks
    return jnp.where((block_of(source) == first) | (block_of(source) == second), factor * values, values)


def block_scale(rng, dims, cuts, smallest, largest):
    level, own = 1.0, jax.random.fold_in(rng, 6)
    for axis_at, shards_of in cuts:
        heights = jnp.exp(jax.random.uniform(jax.random.fold_in(own, axis_at), (shards_of,), jnp.float32, smallest / len(cuts), largest / len(cuts)))
        level = level * jnp.repeat(heights, dims[axis_at] // shards_of).reshape([-1 if axis == axis_at else 1 for axis in range(len(dims))])
    return level


def bell_draw(rng, shape, deviation, limit, cuts=(), held_as=jnp.bfloat16):
    entries = deviation * jax.random.normal(rng, shape, jnp.float32)
    if cuts:
        entries = entries * block_scale(rng, shape, cuts, -0.22, 0.18)
    return jnp.clip(entries, -limit, limit).astype(held_as)


def heavy_noise(stream_key, dims, deviation, reach, cuts, heavy, held_as=jnp.bfloat16):
    array = deviation * jax.random.normal(stream_key, dims, jnp.float32)
    if cuts:
        array = array * block_scale(stream_key, dims, cuts, -0.22, 0.18)
    return jnp.clip(raised(array, jax.random.fold_in(stream_key, 3), *heavy), -reach, reach).astype(held_as)


def setup_inputs(seed: int = 0) -> dict:
    arg_keys = jax.random.split(jax.random.key(seed), 12)
    queries = draw_queries(jax.random.fold_in(arg_keys[11], 71), 0)
    cached_key_rows = bell_draw(arg_keys[1], (ROWS, CTX, KEY_HEADS, HEAD_SIZE), 1.0, 6.0, ((0, 64), (2, 4)))
    cached_value_rows = bell_draw(arg_keys[2], (ROWS, CTX, KEY_HEADS, HEAD_SIZE), 1.0, 6.0, ((0, 64), (2, 4)))
    newest_key = bell_draw(arg_keys[3], (ROWS, KEY_HEADS, HEAD_SIZE), 1.0, 6.0, ((0, 64), (1, 4)))
    newest_value = bell_draw(arg_keys[4], (ROWS, KEY_HEADS, HEAD_SIZE), 1.0, 6.0, ((0, 64), (1, 4)))
    output_weight = heavy_noise(arg_keys[5], (KEY_HEADS, QUERY_PER_KEY * HEAD_SIZE, MODEL_WIDTH), HEAD_SIZE ** -0.5, 0.75, ((0, 4), (1, 16)), (1, 2, 16, 2.0))
    adapter_down_weight = bell_draw(arg_keys[6], (ADAPTER_COUNT, KEY_HEADS, QUERY_PER_KEY * HEAD_SIZE, ADAPTER_RANK), HEAD_SIZE ** -0.5, 0.5, ((0, 4), (2, 16)))
    adapter_up_weight = bell_draw(arg_keys[7], (ADAPTER_COUNT, ADAPTER_RANK, MODEL_WIDTH), ADAPTER_RANK ** -0.5, 0.75, ((0, 4), (2, 16)))
    adapter_store_row = jax.random.permutation(arg_keys[8], ADAPTER_COUNT).astype(jnp.int32)
    adapters_by_group = draw_adapters_by_group(jax.random.fold_in(arg_keys[11], 71), 0)
    adapter_per_row = draw_adapter_per_row(jax.random.fold_in(arg_keys[11], 71), 0)
    return dict(queries=queries, cached_key_rows=cached_key_rows, cached_value_rows=cached_value_rows, newest_key=newest_key, newest_value=newest_value, output_weight=output_weight, adapter_down_weight=adapter_down_weight, adapter_up_weight=adapter_up_weight, adapter_store_row=adapter_store_row, adapters_by_group=adapters_by_group, adapter_per_row=adapter_per_row)


ADAPTER_SCALE = 2.0


def attend(query_rows, key_rows, value_rows, fresh_key, fresh_value):
    row_total = query_rows.shape[0]
    heads = query_rows.astype(jnp.float32).reshape(row_total, KEY_HEADS, QUERY_PER_KEY, HEAD_SIZE)
    inverse_root = HEAD_SIZE ** -0.5
    scores = jnp.einsum("rkgh,rckh->rkgc", heads, key_rows.astype(jnp.float32)) * inverse_root
    fresh_score = jnp.einsum("rkgh,rkh->rkg", heads, fresh_key.astype(jnp.float32)) * inverse_root
    overall = jnp.maximum(jnp.max(scores, axis=-1), fresh_score)
    weights_exp = jnp.exp(scores - overall[..., None])
    fresh_weight = jnp.exp(fresh_score - overall)
    denominator = jnp.sum(weights_exp, axis=-1) + fresh_weight
    mixed = jnp.einsum("rkgc,rckh->rkgh", weights_exp, value_rows.astype(jnp.float32))
    mixed = mixed + fresh_weight[..., None] * fresh_value.astype(jnp.float32)[:, :, None, :]
    return (mixed / denominator[..., None]).astype(jnp.bfloat16).reshape(row_total, MODEL_WIDTH)


def reference(queries, cached_key_rows, cached_value_rows, newest_key, newest_value, output_weight, adapter_down_weight, adapter_up_weight, adapter_store_row, adapters_by_group, adapter_per_row):
    weight_matrix = output_weight.reshape(MODEL_WIDTH, MODEL_WIDTH)

    def per_group(inputs):
        query_rows, key_rows, value_rows, fresh_key, fresh_value, row_ids, slot_ids = inputs
        attention = attend(query_rows, key_rows, value_rows, fresh_key, fresh_value)
        base_output = jnp.dot(attention, weight_matrix, preferred_element_type=jnp.float32)
        slot_home = adapter_store_row[slot_ids].astype(jnp.int32)

        def down_step(carry, item):
            slot_id, found_position = item
            weight_table = lax.dynamic_index_in_dim(adapter_down_weight, found_position, 0, keepdims=False).reshape(MODEL_WIDTH, ADAPTER_RANK)
            chosen = (row_ids == slot_id).astype(jnp.float32)
            return carry + chosen[:, None] * jnp.dot(attention, weight_table, preferred_element_type=jnp.float32), None

        rank_sum = lax.scan(down_step, jnp.zeros((ROWS_DEV, ADAPTER_RANK), jnp.float32), (slot_ids, slot_home))[0]
        rank_code = rank_sum.astype(jnp.bfloat16)

        def up_step(carry, item):
            slot_id, found_position = item
            weight_table = lax.dynamic_index_in_dim(adapter_up_weight, found_position, 0, keepdims=False)
            chosen = (row_ids == slot_id).astype(jnp.float32)
            return carry + chosen[:, None] * jnp.dot(rank_code, weight_table, preferred_element_type=jnp.float32), None

        adapter_delta = lax.scan(up_step, jnp.zeros((ROWS_DEV, MODEL_WIDTH), jnp.float32), (slot_ids, slot_home))[0]
        return (base_output + ADAPTER_SCALE * adapter_delta).astype(jnp.bfloat16)

    result = lax.map(per_group, (
        queries.reshape(GROUPS, ROWS_DEV, MODEL_WIDTH),
        cached_key_rows.reshape(GROUPS, ROWS_DEV, CTX, KEY_HEADS, HEAD_SIZE),
        cached_value_rows.reshape(GROUPS, ROWS_DEV, CTX, KEY_HEADS, HEAD_SIZE),
        newest_key.reshape(GROUPS, ROWS_DEV, KEY_HEADS, HEAD_SIZE),
        newest_value.reshape(GROUPS, ROWS_DEV, KEY_HEADS, HEAD_SIZE),
        adapter_per_row.reshape(GROUPS, ROWS_DEV),
        adapters_by_group))
    return result.reshape(ROWS, MODEL_WIDTH)
```

```python
import jax
import jax.numpy as jnp
from jax import lax
from jax.experimental import pallas as pl
from jax.experimental.pallas import tpu as pltpu
from jax.sharding import PartitionSpec as P

ADAPTER_SCALE = 2.0
BF16 = jnp.bfloat16
F32 = jnp.float32

VMEM = pl.BlockSpec(memory_space=pltpu.VMEM)
SMEM = pl.BlockSpec(memory_space=pltpu.SMEM)
ANY = pl.BlockSpec(memory_space=pl.ANY)


def slot_position(slot, group_ref, store_ref, stored):
    spot = store_ref[group_ref[0, slot]] - lax.axis_index("owner") * stored
    here = jnp.logical_and(spot >= 0, spot < stored)
    return jnp.clip(spot, 0, stored - 1), here


def row_adapters(rows_ref, width):
    rows = rows_ref.shape[1]
    return jnp.transpose(jnp.broadcast_to(rows_ref[...], (rows, rows)))[:, :width]


def project_kernel(
    group_ref, store_ref, rows_ref, att_ref, w_ref, down_ref, keep_ref, send_ref, dbuf, acc, sems
):
    slots = dbuf.shape[0]
    stored = down_ref.shape[0]
    copies = []
    for s in range(slots):
        spot, _ = slot_position(s, group_ref, store_ref, stored)
        copy = pltpu.make_async_copy(down_ref.at[spot], dbuf.at[s], sems.at[s])
        copy.start()
        copies.append(copy)
    owners, rows, feats = att_ref.shape
    att = jnp.concatenate([att_ref[o] for o in range(owners)], axis=1)
    weight = w_ref[...].reshape(owners * feats, w_ref.shape[2])
    first = lax.rem(lax.axis_index("tensor"), 2) == 0
    planes = w_ref.shape[2] // 256
    for z in range(planes):
        part = jnp.dot(att, weight[:, 256 * z : 256 * z + 256], preferred_element_type=F32)
        even, odd = part[:, :128], part[:, 128:]
        keep_ref[z * rows : (z + 1) * rows, :] = jnp.where(first, even, odd)
        send_ref[z * rows : (z + 1) * rows, :] = jnp.where(first, odd, even).astype(BF16)
    rank = dbuf.shape[-1]
    ids = row_adapters(rows_ref, rank)
    acc[...] = jnp.zeros_like(acc)
    for s in range(slots):
        copies[s].wait()
        _, here = slot_position(s, group_ref, store_ref, stored)

        @pl.when(here)
        def _(s=s):
            table = dbuf[s].reshape(owners * feats, rank)
            code = jnp.dot(att, table, preferred_element_type=F32)
            acc[...] += jnp.where(ids == group_ref[0, s], code, 0.0)

    half = rows // 2
    code = jnp.concatenate([acc[:half, :], acc[half:, :]], axis=1)
    keep_ref[planes * rows :, :] = code
    send_ref[planes * rows :, :] = code.astype(BF16)


def pair_kernel(keep_ref, got_ref, out_ref):
    planes, total, _ = out_ref.shape
    rows = (keep_ref.shape[0] - total) // (planes - 1)
    code = (keep_ref[planes * rows :, :] + got_ref[planes * rows :, :].astype(F32)).astype(BF16)
    for z in range(planes):
        span = pl.ds(z * rows, rows)
        out_ref[z, :rows, :] = (keep_ref[span, :] + got_ref[span, :].astype(F32)).astype(BF16)
        out_ref[z, rows:, :] = code


def update_kernel(
    group_ref, store_ref, rows_ref, parts_ref, up_ref, base_ref, send_ref, ubuf, acc, sems
):
    slots = ubuf.shape[0]
    stored = up_ref.shape[0]
    copies = []
    for s in range(slots):
        spot, _ = slot_position(s, group_ref, store_ref, stored)
        copy = pltpu.make_async_copy(up_ref.at[spot], ubuf.at[s], sems.at[s])
        copy.start()
        copies.append(copy)
    total = parts_ref[0].astype(F32)
    for z in range(1, parts_ref.shape[0]):
        total = total + parts_ref[z].astype(F32)
    rows = base_ref.shape[0]
    base_ref[...] = total[:rows]
    rank = ubuf.shape[1]
    packed = total[rows:]
    code = jnp.concatenate([packed[:, :rank], packed[:, rank:]], axis=0).astype(BF16)
    ids = row_adapters(rows_ref, rank)
    acc[...] = jnp.zeros_like(acc)
    for s in range(slots):
        copies[s].wait()
        _, here = slot_position(s, group_ref, store_ref, stored)

        @pl.when(here)
        def _(s=s):
            chosen = jnp.where(ids == group_ref[0, s], code.astype(F32), 0.0).astype(BF16)
            acc[...] += jnp.dot(chosen, ubuf[s], preferred_element_type=F32)

    width = send_ref.shape[2]
    for o in range(send_ref.shape[0]):
        send_ref[o] = acc[:, o * width : (o + 1) * width].astype(BF16)


def final_kernel(base_ref, got_ref, out_ref):
    update = got_ref[0].astype(F32)
    for o in range(1, got_ref.shape[0]):
        update = update + got_ref[o].astype(F32)
    out_ref[...] = (base_ref[...] + ADAPTER_SCALE * update).astype(BF16)


def attend(queries, cached_key_rows, cached_value_rows, newest_key, newest_value):
    row_count = queries.shape[0]
    local_heads = newest_key.shape[1]
    head_width = newest_key.shape[2]
    group_width = queries.shape[1] // local_heads
    query_heads = queries.reshape(row_count, local_heads, group_width // head_width, head_width)
    inverse_root = head_width ** (-0.5)
    scores = (
        jnp.einsum(
            "rkgh,rckh->rkgc", query_heads, cached_key_rows, preferred_element_type=jnp.float32
        )
        * inverse_root
    )
    fresh_score = (
        jnp.einsum("rkgh,rkh->rkg", query_heads, newest_key, preferred_element_type=jnp.float32)
        * inverse_root
    )
    overall = jnp.maximum(jnp.max(scores, axis=-1), fresh_score)
    weights_exp = jnp.exp(scores - overall[..., None])
    fresh_weight = jnp.exp(fresh_score - overall)
    denominator = jnp.sum(weights_exp, axis=-1) + fresh_weight
    mixed = jnp.einsum(
        "rkgc,rckh->rkgh", weights_exp, cached_value_rows, preferred_element_type=jnp.float32
    )
    mixed = mixed + fresh_weight[..., None] * newest_value.astype(jnp.float32)[:, :, None, :]
    return (mixed / denominator[..., None]).astype(jnp.bfloat16)


def shards(
    queries,
    cached_key_rows,
    cached_value_rows,
    newest_key,
    newest_value,
    output_weight,
    adapter_down_weight,
    adapter_up_weight,
    adapter_store_row,
    adapters_by_group,
    adapter_per_row,
):
    owners = lax.axis_size("owner")
    tensors = lax.axis_size("tensor")
    planes = tensors // 2
    slots = adapters_by_group.shape[1]
    row_count, local_heads, head_width = newest_key.shape
    rows = adapter_per_row.shape[0]
    feats = local_heads * output_weight.shape[1]
    columns = output_weight.shape[2]
    block = columns // (tensors * owners)
    rank = adapter_down_weight.shape[-1]
    row_ids = adapter_per_row.reshape(1, rows)

    weight = output_weight.reshape(feats, tensors, owners, block).transpose(2, 0, 1, 3)
    weight = weight.reshape(owners, feats, tensors * block)
    weight = lax.all_to_all(weight, "owner", split_axis=0, concat_axis=0, tiled=True)

    mixed = attend(queries, cached_key_rows, cached_value_rows, newest_key, newest_value)
    part = output_weight.shape[1]
    outgoing = mixed.reshape(row_count, local_heads, tensors, part).transpose(2, 0, 1, 3)
    outgoing = outgoing.reshape(1, tensors, row_count, feats)
    outgoing = jnp.broadcast_to(outgoing, (owners, tensors, row_count, feats))
    outgoing = outgoing.reshape(owners * tensors, row_count, feats)
    attention = lax.all_to_all(
        outgoing, ("owner", "tensor"), split_axis=0, concat_axis=0, tiled=True
    )
    attention = attention.reshape(owners, rows, feats)

    tall = planes * rows + rows // 2
    keep, send = pl.pallas_call(
        project_kernel,
        name="project",
        out_shape=(
            jax.ShapeDtypeStruct((tall, block), F32),
            jax.ShapeDtypeStruct((tall, block), BF16),
        ),
        in_specs=[SMEM, SMEM, VMEM, VMEM, VMEM, ANY],
        out_specs=(VMEM, VMEM),
        scratch_shapes=[
            pltpu.VMEM((slots,) + adapter_down_weight.shape[1:], BF16),
            pltpu.VMEM((rows, rank), F32),
            pltpu.SemaphoreType.DMA((slots,)),
        ],
    )(adapters_by_group, adapter_store_row, row_ids, attention, weight, adapter_down_weight)
    got = lax.ppermute(send, "tensor", [(t, t ^ 1) for t in range(tensors)])
    pieces = pl.pallas_call(
        pair_kernel,
        name="pair",
        out_shape=jax.ShapeDtypeStruct((planes, rows + rows // 2, block), BF16),
        in_specs=[VMEM, VMEM],
        out_specs=VMEM,
    )(keep, got)
    groups = [[2 * z + c for z in range(planes)] for c in range(2)]
    parts = lax.all_to_all(
        pieces, "tensor", split_axis=0, concat_axis=0, tiled=True, axis_index_groups=groups
    )
    base, update = pl.pallas_call(
        update_kernel,
        name="update",
        out_shape=(
            jax.ShapeDtypeStruct((rows, block), F32),
            jax.ShapeDtypeStruct((owners, rows, block), BF16),
        ),
        in_specs=[SMEM, SMEM, VMEM, VMEM, ANY],
        out_specs=(VMEM, VMEM),
        scratch_shapes=[
            pltpu.VMEM((slots,) + adapter_up_weight.shape[1:], BF16),
            pltpu.VMEM((rows, owners * block), F32),
            pltpu.SemaphoreType.DMA((slots,)),
        ],
    )(adapters_by_group, adapter_store_row, row_ids, parts, adapter_up_weight)
    update = lax.all_to_all(update, "owner", split_axis=0, concat_axis=0, tiled=True)
    return pl.pallas_call(
        final_kernel,
        name="final",
        out_shape=jax.ShapeDtypeStruct((rows, block), BF16),
        in_specs=[VMEM, VMEM],
        out_specs=VMEM,
    )(base, update)


def solution(mesh):
    return jax.shard_map(
        shards,
        mesh=mesh,
        in_specs=(
            P(("dp", "tensor"), "owner"),
            P(("dp", "tensor"), None, "owner", None),
            P(("dp", "tensor"), None, "owner", None),
            P(("dp", "tensor"), "owner", None),
            P(("dp", "tensor"), "owner", None),
            P("owner", "tensor", None),
            P("owner", None, "tensor", None),
            P("owner", None, "tensor"),
            P(),
            P("dp", None),
            P("dp"),
        ),
        out_specs=P("dp", ("tensor", "owner")),
        check_vma=False,
    )
```

```python
import jax
import jax.numpy as jnp
from jax import lax
from jax.experimental import pallas as pl
from jax.experimental.pallas import tpu as pltpu
from jax.sharding import PartitionSpec as P

ADAPTER_SCALE = 2.0
BF16 = jnp.bfloat16
F32 = jnp.float32

VMEM = pl.BlockSpec(memory_space=pltpu.VMEM)
SMEM = pl.BlockSpec(memory_space=pltpu.SMEM)
ANY = pl.BlockSpec(memory_space=pl.ANY)
LIMIT = pltpu.CompilerParams(vmem_limit_bytes=16 * 1024 * 1024)


def near(array):
    return pltpu.with_memory_space_constraint(array, pltpu.VMEM)


def slot_position(slot, group_ref, store_ref, stored):
    spot = store_ref[group_ref[0, slot]] - lax.axis_index("owner") * stored
    here = jnp.logical_and(spot >= 0, spot < stored)
    return jnp.clip(spot, 0, stored - 1), here


def row_adapters(rows_ref, width):
    rows = rows_ref.shape[1]
    return jnp.transpose(jnp.broadcast_to(rows_ref[...], (rows, rows)))[:, :width]


def project_kernel(
    group_ref, store_ref, rows_ref, att_ref, w_ref, down_ref, keep_ref, send_ref, dbuf, acc, sems
):
    slots = dbuf.shape[0]
    stored = down_ref.shape[0]
    copies = []
    for s in range(slots):
        spot, _ = slot_position(s, group_ref, store_ref, stored)
        copy = pltpu.make_async_copy(down_ref.at[spot], dbuf.at[s], sems.at[s])
        copy.start()
        copies.append(copy)
    owners, rows, feats = att_ref.shape
    mine = att_ref[lax.axis_index("owner")]
    first = lax.rem(lax.axis_index("tensor"), 2) == 0
    rank = dbuf.shape[-1]
    block = keep_ref.shape[1]
    planes = w_ref.shape[1] // (2 * owners * block)
    wide = owners * block
    for z in range(planes):
        columns = w_ref[:, 2 * wide * z : 2 * wide * (z + 1)]
        part = jnp.dot(mine, columns, preferred_element_type=F32)
        for o in range(owners):
            even = part[:, o * block : (o + 1) * block]
            odd = part[:, wide + o * block : wide + (o + 1) * block]
            span = pl.ds((z * owners + o) * rows, rows)
            keep_ref[span, :] = jnp.where(first, even, odd)
            send_ref[span, :] = jnp.where(first, odd, even).astype(BF16)
    att = jnp.concatenate([att_ref[o] for o in range(owners)], axis=1)
    ids = row_adapters(rows_ref, rank)
    acc[...] = jnp.zeros_like(acc)
    for s in range(slots):
        copies[s].wait()
        _, here = slot_position(s, group_ref, store_ref, stored)

        @pl.when(here)
        def _(s=s):
            table = dbuf[s].reshape(owners * feats, rank)
            code = jnp.dot(att, table, preferred_element_type=F32)
            acc[...] += jnp.where(ids == group_ref[0, s], code, 0.0)

    half = rows // 2
    code = jnp.concatenate([acc[:half, :], acc[half:, :]], axis=1)
    keep_ref[planes * owners * rows :, :] = code
    send_ref[planes * owners * rows :, :] = code.astype(BF16)


def pair_kernel(keep_ref, got_ref, out_ref):
    planes, total, _ = out_ref.shape
    tall = (keep_ref.shape[0] - total) // (planes - 1)
    code = keep_ref[planes * tall :, :] + got_ref[planes * tall :, :].astype(F32)
    code = code.astype(BF16)
    for z in range(planes):
        span = pl.ds(z * tall, tall)
        out_ref[z, :tall, :] = (keep_ref[span, :] + got_ref[span, :].astype(F32)).astype(BF16)
        out_ref[z, tall:, :] = code


def update_kernel(group_ref, store_ref, rows_ref, parts_ref, up_ref, send_ref, ubuf, acc, sems):
    slots = ubuf.shape[0]
    stored = up_ref.shape[0]
    copies = []
    for s in range(slots):
        spot, _ = slot_position(s, group_ref, store_ref, stored)
        copy = pltpu.make_async_copy(up_ref.at[spot], ubuf.at[s], sems.at[s])
        copy.start()
        copies.append(copy)
    owners, rows, block = send_ref.shape
    rank = ubuf.shape[1]
    tall = owners * rows

    def total(start, size):
        part = parts_ref[0, start : start + size, :].astype(F32)
        for z in range(1, parts_ref.shape[0]):
            part = part + parts_ref[z, start : start + size, :].astype(F32)
        return part

    packed = total(tall, rows // 2)
    code = jnp.concatenate([packed[:, :rank], packed[:, rank:]], axis=0).astype(BF16).astype(F32)
    ids = row_adapters(rows_ref, rank)
    acc[...] = jnp.zeros_like(acc)
    for s in range(slots):
        copies[s].wait()
        _, here = slot_position(s, group_ref, store_ref, stored)

        @pl.when(here)
        def _(s=s):
            chosen = jnp.where(ids == group_ref[0, s], code, 0.0).astype(BF16)
            acc[...] += jnp.dot(chosen, ubuf[s], preferred_element_type=F32)

    for o in range(owners):
        update = acc[:, o * block : (o + 1) * block]
        send_ref[o] = (total(o * rows, rows) + ADAPTER_SCALE * update).astype(BF16)


def final_kernel(got_ref, out_ref):
    total = got_ref[0].astype(F32)
    for o in range(1, got_ref.shape[0]):
        total = total + got_ref[o].astype(F32)
    out_ref[...] = total.astype(BF16)


def attend(queries, cached_key_rows, cached_value_rows, newest_key, newest_value):
    row_count = queries.shape[0]
    local_heads = newest_key.shape[1]
    head_width = newest_key.shape[2]
    group_width = queries.shape[1] // local_heads
    query_heads = queries.reshape(row_count, local_heads, group_width // head_width, head_width)
    inverse_root = head_width ** (-0.5)
    scores = (
        jnp.einsum(
            "rkgh,rckh->rkgc", query_heads, cached_key_rows, preferred_element_type=jnp.float32
        )
        * inverse_root
    )
    fresh_score = (
        jnp.einsum("rkgh,rkh->rkg", query_heads, newest_key, preferred_element_type=jnp.float32)
        * inverse_root
    )
    overall = jnp.maximum(jnp.max(scores, axis=-1), fresh_score)
    weights_exp = jnp.exp(scores - overall[..., None])
    fresh_weight = jnp.exp(fresh_score - overall)
    denominator = jnp.sum(weights_exp, axis=-1) + fresh_weight
    mixed = jnp.einsum(
        "rkgc,rckh->rkgh", weights_exp, cached_value_rows, preferred_element_type=jnp.float32
    )
    mixed = mixed + fresh_weight[..., None] * newest_value.astype(jnp.float32)[:, :, None, :]
    return (mixed / denominator[..., None]).astype(jnp.bfloat16)


def shards(
    queries,
    cached_key_rows,
    cached_value_rows,
    newest_key,
    newest_value,
    output_weight,
    adapter_down_weight,
    adapter_up_weight,
    adapter_store_row,
    adapters_by_group,
    adapter_per_row,
):
    owners = lax.axis_size("owner")
    tensors = lax.axis_size("tensor")
    planes = tensors // 2
    slots = adapters_by_group.shape[1]
    row_count, local_heads, head_width = newest_key.shape
    rows = adapter_per_row.shape[0]
    feats = local_heads * output_weight.shape[1]
    columns = output_weight.shape[2]
    block = columns // (tensors * owners)
    rank = adapter_down_weight.shape[-1]
    row_ids = adapter_per_row.reshape(1, rows)

    mixed = attend(queries, cached_key_rows, cached_value_rows, newest_key, newest_value)
    part = output_weight.shape[1]
    outgoing = mixed.reshape(row_count, local_heads, tensors, part).transpose(2, 0, 1, 3)
    outgoing = outgoing.reshape(1, tensors, row_count, feats)
    outgoing = jnp.broadcast_to(outgoing, (owners, tensors, row_count, feats))
    outgoing = outgoing.reshape(owners * tensors, row_count, feats)
    attention = lax.all_to_all(
        outgoing, ("owner", "tensor"), split_axis=0, concat_axis=0, tiled=True
    )
    attention = attention.reshape(owners, rows, feats)

    weight = output_weight.reshape(feats, columns)
    tall = planes * owners * rows + rows // 2
    keep, send = pl.pallas_call(
        project_kernel,
        name="project",
        out_shape=(pltpu.VMEM((tall, block), F32), pltpu.VMEM((tall, block), BF16)),
        in_specs=[SMEM, SMEM, VMEM, VMEM, VMEM, ANY],
        out_specs=(VMEM, VMEM),
        scratch_shapes=[
            pltpu.VMEM((slots,) + adapter_down_weight.shape[1:], BF16),
            pltpu.VMEM((rows, rank), F32),
            pltpu.SemaphoreType.DMA((slots,)),
        ],
        compiler_params=LIMIT,
    )(
        adapters_by_group,
        adapter_store_row,
        row_ids,
        near(attention),
        near(weight),
        adapter_down_weight,
    )
    got = lax.ppermute(send, "tensor", [(t, t ^ 1) for t in range(tensors)])
    pieces = pl.pallas_call(
        pair_kernel,
        name="pair",
        out_shape=pltpu.VMEM((planes, owners * rows + rows // 2, block), BF16),
        in_specs=[VMEM, VMEM],
        out_specs=VMEM,
        compiler_params=LIMIT,
    )(near(keep), near(got))
    groups = [[2 * z + c for z in range(planes)] for c in range(2)]
    parts = lax.all_to_all(
        pieces, "tensor", split_axis=0, concat_axis=0, tiled=True, axis_index_groups=groups
    )
    sums = pl.pallas_call(
        update_kernel,
        name="update",
        out_shape=pltpu.VMEM((owners, rows, block), BF16),
        in_specs=[SMEM, SMEM, VMEM, VMEM, ANY],
        out_specs=VMEM,
        scratch_shapes=[
            pltpu.VMEM((slots,) + adapter_up_weight.shape[1:], BF16),
            pltpu.VMEM((rows, owners * block), F32),
            pltpu.SemaphoreType.DMA((slots,)),
        ],
        compiler_params=LIMIT,
    )(adapters_by_group, adapter_store_row, row_ids, near(parts), adapter_up_weight)
    sums = lax.all_to_all(sums, "owner", split_axis=0, concat_axis=0, tiled=True)
    return pl.pallas_call(
        final_kernel,
        name="final",
        out_shape=jax.ShapeDtypeStruct((rows, block), BF16),
        in_specs=[VMEM],
        out_specs=VMEM,
        compiler_params=LIMIT,
    )(near(sums))


def solution(mesh):
    return jax.shard_map(
        shards,
        mesh=mesh,
        in_specs=(
            P(("dp", "tensor"), "owner"),
            P(("dp", "tensor"), None, "owner", None),
            P(("dp", "tensor"), None, "owner", None),
            P(("dp", "tensor"), "owner", None),
            P(("dp", "tensor"), "owner", None),
            P("owner", "tensor", None),
            P("owner", None, "tensor", None),
            P("owner", None, "tensor"),
            P(),
            P("dp", None),
            P("dp"),
        ),
        out_specs=P("dp", ("tensor", "owner")),
        check_vma=False,
    )
```

```python
import jax
import jax.numpy as jnp
from jax import lax
from jax.experimental import pallas as pl
from jax.experimental.pallas import tpu as pltpu
from jax.sharding import PartitionSpec as P

ADAPTER_SCALE = 2.0
BF16 = jnp.bfloat16
F32 = jnp.float32

VMEM = pl.BlockSpec(memory_space=pltpu.VMEM)
SMEM = pl.BlockSpec(memory_space=pltpu.SMEM)
HBM = pl.BlockSpec(memory_space=pltpu.HBM)
LIMIT = pltpu.CompilerParams(vmem_limit_bytes=16 * 1024 * 1024)


def near(array):
    return pltpu.with_memory_space_constraint(array, pltpu.VMEM)


def far(array):
    return pltpu.with_memory_space_constraint(array, pltpu.HBM)


def slot_position(slot, group_ref, store_ref, stored):
    spot = store_ref[group_ref[0, slot]] - lax.axis_index("owner") * stored
    here = jnp.logical_and(spot >= 0, spot < stored)
    return jnp.clip(spot, 0, stored - 1), here


def row_adapters(rows_ref, width):
    rows = rows_ref.shape[1]
    return jnp.transpose(jnp.broadcast_to(rows_ref[...], (rows, rows)))[:, :width]


def column_copies(w_ref, out_ref, step, sems, base):
    owners = lax.axis_size("owner")
    target = lax.rem(lax.axis_index("owner") + step, owners)
    copies = []
    for block in range(out_ref.shape[1] // 128):
        at = pl.multiple_of((block * owners + target) * 128, 128)
        copies.append(
            pltpu.make_async_copy(
                w_ref.at[:, pl.ds(at, 128)],
                out_ref.at[:, pl.ds(block * 128, 128)],
                sems.at[base + block],
            )
        )
    return copies


def slab_kernel(w_ref, right_ref, left_ref, sems):
    owners = lax.axis_size("owner")
    blocks = right_ref.shape[1] // 128
    copies = column_copies(w_ref, right_ref, 1, sems, 0)
    copies += column_copies(w_ref, left_ref, owners - 1, sems, blocks)
    for copy in copies:
        copy.start()
    for copy in copies:
        copy.wait()


def attend_kernel(
    group_ref,
    store_ref,
    queries_ref,
    keys_ref,
    values_hbm_ref,
    key_ref,
    value_ref,
    w_ref,
    down_ref,
    out_ref,
    mine_ref,
    across_ref,
    slots_ref,
    values_ref,
    value_sems,
    sems,
):
    stored = down_ref.shape[0]
    blocks = mine_ref.shape[1] // 128
    value_copies = [
        pltpu.make_async_copy(values_hbm_ref.at[r], values_ref.at[r], value_sems.at[r])
        for r in range(values_ref.shape[0])
    ]
    for copy in value_copies:
        copy.start()
    copies = column_copies(w_ref, mine_ref, 0, sems, 0)
    copies += column_copies(w_ref, across_ref, 2, sems, blocks)
    for s in range(slots_ref.shape[0]):
        spot, _ = slot_position(s, group_ref, store_ref, stored)
        copies.append(
            pltpu.make_async_copy(down_ref.at[spot], slots_ref.at[s], sems.at[2 * blocks + s])
        )
    for copy in copies:
        copy.start()

    heads, rows, width = queries_ref.shape
    _, local, _ = key_ref.shape
    grouped = heads // local
    positions = keys_ref.shape[1]
    scale = width ** (-0.5)
    queries = jnp.swapaxes(queries_ref[...].astype(F32), 0, 1)
    row_head = lax.broadcasted_iota(jnp.int32, (heads, positions), 0) // grouped
    place_head = lax.broadcasted_iota(jnp.int32, (heads, positions), 1) % local
    same = row_head == place_head

    def spread(ref, r):
        fresh = ref[r].astype(F32)
        parts = [jnp.broadcast_to(fresh[k : k + 1], (grouped, width)) for k in range(local)]
        return jnp.concatenate(parts, axis=0)

    mixed = []
    for r in range(rows):
        query = queries[r]
        scores = lax.dot_general(
            query.astype(BF16), keys_ref[r], (((1,), (1,)), ((), ())), preferred_element_type=F32
        )
        scores = jnp.where(same, scores * scale, -jnp.inf)
        fresh_score = jnp.sum(query * spread(key_ref, r), axis=1, keepdims=True) * scale
        overall = jnp.maximum(jnp.max(scores, axis=1, keepdims=True), fresh_score)
        weights = jnp.exp(scores - overall)
        fresh_weight = jnp.exp(fresh_score - overall)
        denominator = jnp.sum(weights, axis=1, keepdims=True) + fresh_weight
        value_copies[r].wait()
        total = jnp.dot(weights.astype(BF16), values_ref[r], preferred_element_type=F32)
        total = total + fresh_weight * spread(value_ref, r)
        mixed.append(total / denominator)
    mixed = jnp.swapaxes(jnp.stack(mixed), 0, 1)

    half = width // 2
    low = lax.broadcasted_iota(jnp.int32, (rows, width), 1) < half
    for g in range(grouped):
        one, two = mixed[g], mixed[grouped + g]
        pair = (
            jnp.where(low, one, pltpu.roll(two, half, 1)),
            jnp.where(low, pltpu.roll(one, half, 1), two),
        )
        for i, part in enumerate(pair):
            for o in range(out_ref.shape[0]):
                out_ref[o, 2 * g + i] = part.astype(BF16)
    for copy in copies:
        copy.wait()


def project_kernel(
    group_ref,
    store_ref,
    rows_ref,
    att_ref,
    mine_ref,
    across_ref,
    before_ref,
    after_ref,
    slots_ref,
    keep_ref,
    send_ref,
    acc,
):
    slots, _, _, rank = slots_ref.shape
    stored = store_ref.shape[0] // lax.axis_size("owner")
    owners, rows, feats = att_ref.shape
    owner = lax.axis_index("owner")
    mine = att_ref[owner]
    beside = jnp.concatenate(
        [att_ref[lax.rem(owner + owners - 1, owners)], att_ref[lax.rem(owner + 1, owners)]], axis=1
    )
    first = lax.rem(lax.axis_index("tensor"), 2) == 0
    block = keep_ref.shape[1]
    planes = before_ref.shape[1] // (2 * block)

    for z in range(planes):
        span = pl.ds(z * 2 * block, 2 * block)
        near_rows = jnp.concatenate([before_ref[:, span], after_ref[:, span]], axis=0)
        here = jnp.dot(beside, near_rows, preferred_element_type=F32)
        here = here + jnp.dot(mine, mine_ref[:, span], preferred_element_type=F32)
        there = jnp.dot(mine, across_ref[:, span], preferred_element_type=F32)
        for i, part in enumerate((here, there)):
            even, odd = part[:, :block], part[:, block:]
            rows_span = pl.ds((2 * z + i) * rows, rows)
            keep_ref[rows_span, :] = jnp.where(first, even, odd)
            send_ref[rows_span, :] = jnp.where(first, odd, even).astype(BF16)
    att = jnp.concatenate([att_ref[o] for o in range(owners)], axis=1)
    ids = row_adapters(rows_ref, rank)
    acc[...] = jnp.zeros_like(acc)
    for s in range(slots):
        _, here = slot_position(s, group_ref, store_ref, stored)

        @pl.when(here)
        def _(s=s):
            table = slots_ref[s].reshape(owners * feats, rank)
            code = jnp.dot(att, table, preferred_element_type=F32)
            acc[...] += jnp.where(ids == group_ref[0, s], code, 0.0)

    half = rows // 2
    code = jnp.concatenate([acc[:half, :], acc[half:, :]], axis=1)
    keep_ref[2 * planes * rows :, :] = code
    send_ref[2 * planes * rows :, :] = code.astype(BF16)


def pair_kernel(keep_ref, got_ref, out_ref):
    planes, total, _ = out_ref.shape
    tall = (keep_ref.shape[0] - total) // (planes - 1)
    code = keep_ref[planes * tall :, :] + got_ref[planes * tall :, :].astype(F32)
    code = code.astype(BF16)
    for z in range(planes):
        span = pl.ds(z * tall, tall)
        out_ref[z, :tall, :] = (keep_ref[span, :] + got_ref[span, :].astype(F32)).astype(BF16)
        out_ref[z, tall:, :] = code


def update_kernel(group_ref, store_ref, rows_ref, parts_ref, up_ref, send_ref, acc):
    slots = group_ref.shape[1]
    stored, rank, _ = up_ref.shape
    owners, rows, block = send_ref.shape
    owner = lax.axis_index("owner")

    def total(start, size):
        part = parts_ref[0, start : start + size, :].astype(F32)
        for z in range(1, parts_ref.shape[0]):
            part = part + parts_ref[z, start : start + size, :].astype(F32)
        return part

    packed = total(2 * rows, rows // 2)
    code = jnp.concatenate([packed[:, :rank], packed[:, rank:]], axis=0).astype(BF16).astype(F32)
    ids = row_adapters(rows_ref, rank)
    acc[...] = jnp.zeros_like(acc)
    for s in range(slots):
        spot, here = slot_position(s, group_ref, store_ref, stored)

        @pl.when(here)
        def _(s=s, spot=spot):
            chosen = jnp.where(ids == group_ref[0, s], code, 0.0).astype(BF16)
            acc[...] += jnp.dot(chosen, up_ref[spot], preferred_element_type=F32)

    own, across = total(0, rows), total(rows, rows)
    for o in range(owners):
        update = ADAPTER_SCALE * acc[:, o * block : (o + 1) * block]
        base = jnp.where(owner == o, own, jnp.where(owner == (o + 2) % owners, across, 0.0))
        send_ref[o] = (base + update).astype(BF16)


def final_kernel(got_ref, out_ref):
    total = got_ref[0].astype(F32)
    for o in range(1, got_ref.shape[0]):
        total = total + got_ref[o].astype(F32)
    out_ref[...] = total.astype(BF16)


def shards(
    queries,
    cached_key_rows,
    cached_value_rows,
    newest_key,
    newest_value,
    output_weight,
    adapter_down_weight,
    adapter_up_weight,
    adapter_store_row,
    adapters_by_group,
    adapter_per_row,
):
    owners = lax.axis_size("owner")
    tensors = lax.axis_size("tensor")
    planes = tensors // 2
    slots = adapters_by_group.shape[1]
    row_count, local_heads, head_width = newest_key.shape
    rows = adapter_per_row.shape[0]
    feats = local_heads * output_weight.shape[1]
    columns = output_weight.shape[2]
    block = columns // (tensors * owners)
    rank = adapter_down_weight.shape[-1]
    row_ids = adapter_per_row.reshape(1, rows)

    weight = far(output_weight.reshape(feats, columns))
    slab = pltpu.VMEM((feats, columns // owners), BF16)
    blocks = columns // owners // 128
    right, left = pl.pallas_call(
        slab_kernel,
        name="slabs",
        out_shape=(slab, slab),
        in_specs=[HBM],
        out_specs=(VMEM, VMEM),
        scratch_shapes=[pltpu.SemaphoreType.DMA((2 * blocks,))],
        compiler_params=LIMIT,
    )(weight)
    before = lax.ppermute(right, "owner", [(o, (o + 1) % owners) for o in range(owners)])
    after = lax.ppermute(left, "owner", [(o, (o - 1) % owners) for o in range(owners)])

    heads = queries.shape[1] // head_width
    grouped = queries.reshape(row_count, heads, head_width).transpose(1, 0, 2)
    outgoing, mine, across, tables = pl.pallas_call(
        attend_kernel,
        name="attend",
        out_shape=(
            pltpu.VMEM((owners, tensors, row_count, feats), BF16),
            slab,
            slab,
            pltpu.VMEM((slots,) + adapter_down_weight.shape[1:], BF16),
        ),
        in_specs=[SMEM, SMEM, VMEM, VMEM, HBM, VMEM, VMEM, HBM, HBM],
        out_specs=(VMEM, VMEM, VMEM, VMEM),
        scratch_shapes=[
            pltpu.VMEM((row_count, cached_value_rows.shape[1] * local_heads, head_width), BF16),
            pltpu.SemaphoreType.DMA((row_count,)),
            pltpu.SemaphoreType.DMA((2 * blocks + slots,)),
        ],
        compiler_params=LIMIT,
    )(
        adapters_by_group,
        adapter_store_row,
        grouped,
        near(cached_key_rows.reshape(row_count, -1, head_width)),
        far(cached_value_rows.reshape(row_count, -1, head_width)),
        newest_key,
        newest_value,
        weight,
        far(adapter_down_weight),
    )
    outgoing = outgoing.reshape(owners * tensors, row_count, feats)
    attention = lax.all_to_all(
        outgoing, ("owner", "tensor"), split_axis=0, concat_axis=0, tiled=True
    )
    attention = attention.reshape(owners, rows, feats)

    tall = 2 * planes * rows + rows // 2
    keep, send = pl.pallas_call(
        project_kernel,
        name="project",
        out_shape=(pltpu.VMEM((tall, block), F32), pltpu.VMEM((tall, block), BF16)),
        in_specs=[SMEM, SMEM] + [VMEM] * 7,
        out_specs=(VMEM, VMEM),
        scratch_shapes=[pltpu.VMEM((rows, rank), F32)],
        compiler_params=LIMIT,
    )(
        adapters_by_group,
        adapter_store_row,
        row_ids,
        near(attention),
        near(mine),
        near(across),
        near(before),
        near(after),
        near(tables),
    )
    got = lax.ppermute(send, "tensor", [(t, t ^ 1) for t in range(tensors)])
    pieces = pl.pallas_call(
        pair_kernel,
        name="pair",
        out_shape=pltpu.VMEM((planes, 2 * rows + rows // 2, block), BF16),
        in_specs=[VMEM, VMEM],
        out_specs=VMEM,
        compiler_params=LIMIT,
    )(near(keep), near(got))
    groups = [[2 * z + c for z in range(planes)] for c in range(2)]
    parts = lax.all_to_all(
        pieces, "tensor", split_axis=0, concat_axis=0, tiled=True, axis_index_groups=groups
    )
    sums = pl.pallas_call(
        update_kernel,
        name="update",
        out_shape=pltpu.VMEM((owners, rows, block), BF16),
        in_specs=[SMEM, SMEM, VMEM, VMEM, VMEM],
        out_specs=VMEM,
        scratch_shapes=[pltpu.VMEM((rows, owners * block), F32)],
        compiler_params=LIMIT,
    )(adapters_by_group, adapter_store_row, row_ids, near(parts), near(adapter_up_weight))
    sums = lax.all_to_all(sums, "owner", split_axis=0, concat_axis=0, tiled=True)
    return pl.pallas_call(
        final_kernel,
        name="final",
        out_shape=jax.ShapeDtypeStruct((rows, block), BF16),
        in_specs=[VMEM],
        out_specs=VMEM,
        compiler_params=LIMIT,
    )(near(sums))


def solution(mesh):
    return jax.shard_map(
        shards,
        mesh=mesh,
        in_specs=(
            P(("dp", "tensor"), "owner"),
            P(("dp", "tensor"), None, "owner", None),
            P(("dp", "tensor"), None, "owner", None),
            P(("dp", "tensor"), "owner", None),
            P(("dp", "tensor"), "owner", None),
            P("owner", "tensor", None),
            P("owner", None, "tensor", None),
            P("owner", None, "tensor"),
            P(),
            P("dp", None),
            P("dp"),
        ),
        out_specs=P("dp", ("tensor", "owner")),
        check_vma=False,
    )
```

```python
import jax
import jax.numpy as jnp
from jax import lax
from jax.experimental import pallas as pl
from jax.experimental.pallas import tpu as pltpu
from jax.sharding import PartitionSpec as P

ADAPTER_SCALE = 2.0
BF16 = jnp.bfloat16
F32 = jnp.float32

VMEM = pl.BlockSpec(memory_space=pltpu.VMEM)
SMEM = pl.BlockSpec(memory_space=pltpu.SMEM)
HBM = pl.BlockSpec(memory_space=pltpu.HBM)
LIMIT = pltpu.CompilerParams(vmem_limit_bytes=16 * 1024 * 1024)


def near(array):
    return pltpu.with_memory_space_constraint(array, pltpu.VMEM)


def far(array):
    return pltpu.with_memory_space_constraint(array, pltpu.HBM)


def slot_position(slot, group_ref, store_ref, stored):
    spot = store_ref[group_ref[0, slot]] - lax.axis_index("owner") * stored
    here = jnp.logical_and(spot >= 0, spot < stored)
    return jnp.clip(spot, 0, stored - 1), here


def row_adapters(rows_ref, width):
    rows = rows_ref.shape[1]
    return jnp.transpose(jnp.broadcast_to(rows_ref[...], (rows, rows)))[:, :width]


def slab_kernel(w_hbm_ref, queries_hbm_ref, w_ref, queries_ref, right_ref, left_ref, sems):
    chunks = sems.shape[0] - 1
    step = w_ref.shape[0] // chunks
    copies = [
        pltpu.make_async_copy(
            w_hbm_ref.at[pl.ds(i * step, step)], w_ref.at[pl.ds(i * step, step)], sems.at[i]
        )
        for i in range(chunks)
    ]
    copies.append(pltpu.make_async_copy(queries_hbm_ref, queries_ref, sems.at[chunks]))
    for copy in copies:
        copy.start()
    owner, owners = lax.axis_index("owner"), lax.axis_size("owner")
    targets = [lax.rem(owner + 1, owners), lax.rem(owner + owners - 1, owners)]
    for i in range(chunks):
        copies[i].wait()
        rows = pl.ds(i * step, step)
        for out_ref, target in zip((right_ref, left_ref), targets):
            for block in range(out_ref.shape[1] // 128):
                at = pl.multiple_of((block * owners + target) * 128, 128)
                out_ref[rows, block * 128 : (block + 1) * 128] = w_ref[rows, pl.ds(at, 128)]
    copies[chunks].wait()


def attend_kernel(
    group_ref,
    store_ref,
    queries_ref,
    keys_ref,
    values_hbm_ref,
    key_ref,
    value_ref,
    down_ref,
    out_ref,
    slots_ref,
    values_ref,
    value_sem,
    sems,
):
    stored = down_ref.shape[0]
    values_copy = pltpu.make_async_copy(values_hbm_ref, values_ref, value_sem)
    values_copy.start()
    copies = []
    for s in range(slots_ref.shape[0]):
        spot, _ = slot_position(s, group_ref, store_ref, stored)
        copies.append(pltpu.make_async_copy(down_ref.at[spot], slots_ref.at[s], sems.at[s]))
    for copy in copies:
        copy.start()

    rows, local, width = key_ref.shape
    heads = queries_ref.shape[1] // width
    grouped = heads // local
    positions = keys_ref.shape[1]
    scale = width ** (-0.5)
    queries = [queries_ref[:, h * width : (h + 1) * width].astype(F32) for h in range(heads)]
    queries = jnp.swapaxes(jnp.stack(queries), 0, 1)
    row_head = lax.broadcasted_iota(jnp.int32, (heads, positions), 0) // grouped
    place_head = lax.broadcasted_iota(jnp.int32, (heads, positions), 1) % local
    same = row_head == place_head

    def spread(ref, r):
        fresh = ref[r].astype(F32)
        parts = [jnp.broadcast_to(fresh[k : k + 1], (grouped, width)) for k in range(local)]
        return jnp.concatenate(parts, axis=0)

    weights, fresh_weights, denominators = [], [], []
    for r in range(rows):
        query = queries[r]
        scores = lax.dot_general(
            query.astype(BF16), keys_ref[r], (((1,), (1,)), ((), ())), preferred_element_type=F32
        )
        scores = jnp.where(same, scores * scale, -jnp.inf)
        fresh_score = jnp.sum(query * spread(key_ref, r), axis=1, keepdims=True) * scale
        overall = jnp.maximum(jnp.max(scores, axis=1, keepdims=True), fresh_score)
        weight = jnp.exp(scores - overall)
        fresh_weight = jnp.exp(fresh_score - overall)
        denominators.append(jnp.sum(weight, axis=1, keepdims=True) + fresh_weight)
        weights.append(weight.astype(BF16))
        fresh_weights.append(fresh_weight)
    values_copy.wait()
    mixed = []
    for r in range(rows):
        total = jnp.dot(weights[r], values_ref[r], preferred_element_type=F32)
        total = total + fresh_weights[r] * spread(value_ref, r)
        mixed.append(total / denominators[r])
    mixed = jnp.swapaxes(jnp.stack(mixed), 0, 1)

    half = width // 2
    low = lax.broadcasted_iota(jnp.int32, (rows, width), 1) < half
    for g in range(grouped):
        one, two = mixed[g], mixed[grouped + g]
        pair = (
            jnp.where(low, one, pltpu.roll(two, half, 1)),
            jnp.where(low, pltpu.roll(one, half, 1), two),
        )
        for i, part in enumerate(pair):
            part = part.astype(BF16)
            for o in range(out_ref.shape[0]):
                out_ref[o, 2 * g + i] = part
    for copy in copies:
        copy.wait()


def project_kernel(
    group_ref,
    store_ref,
    rows_ref,
    att_ref,
    w_ref,
    before_ref,
    after_ref,
    slots_ref,
    keep_ref,
    send_ref,
    acc,
):
    slots, _, _, rank = slots_ref.shape
    stored = store_ref.shape[0] // lax.axis_size("owner")
    owners, rows, feats = att_ref.shape
    owner = lax.axis_index("owner")
    mine = att_ref[owner]
    beside = jnp.concatenate(
        [att_ref[lax.rem(owner + owners - 1, owners)], att_ref[lax.rem(owner + 1, owners)]], axis=1
    )
    first = lax.rem(lax.axis_index("tensor"), 2) == 0
    block = keep_ref.shape[1]
    planes = before_ref.shape[1] // (2 * block)

    across = lax.rem(owner + 2, owners)

    def columns(z, target):
        at = [pl.multiple_of(((2 * z + c) * owners + target) * block, block) for c in range(2)]
        return jnp.concatenate([w_ref[:, pl.ds(a, block)] for a in at], axis=1)

    for z in range(planes):
        span = pl.ds(z * 2 * block, 2 * block)
        near_rows = jnp.concatenate([before_ref[:, span], after_ref[:, span]], axis=0)
        here = jnp.dot(beside, near_rows, preferred_element_type=F32)
        here = here + jnp.dot(mine, columns(z, owner), preferred_element_type=F32)
        there = jnp.dot(mine, columns(z, across), preferred_element_type=F32)
        for i, part in enumerate((here, there)):
            even, odd = part[:, :block], part[:, block:]
            rows_span = pl.ds((2 * z + i) * rows, rows)
            keep_ref[rows_span, :] = jnp.where(first, even, odd)
            send_ref[rows_span, :] = jnp.where(first, odd, even).astype(BF16)
    att = jnp.concatenate([att_ref[o] for o in range(owners)], axis=1)
    ids = row_adapters(rows_ref, rank)
    acc[...] = jnp.zeros_like(acc)
    for s in range(slots):
        _, here = slot_position(s, group_ref, store_ref, stored)

        @pl.when(here)
        def _(s=s):
            table = slots_ref[s].reshape(owners * feats, rank)
            code = jnp.dot(att, table, preferred_element_type=F32)
            acc[...] += jnp.where(ids == group_ref[0, s], code, 0.0)

    half = rows // 2
    code = jnp.concatenate([acc[:half, :], acc[half:, :]], axis=1)
    keep_ref[2 * planes * rows :, :] = code
    send_ref[2 * planes * rows :, :] = code.astype(BF16)


def pair_kernel(keep_ref, got_ref, out_ref):
    planes, total, _ = out_ref.shape
    tall = (keep_ref.shape[0] - total) // (planes - 1)
    code = keep_ref[planes * tall :, :] + got_ref[planes * tall :, :].astype(F32)
    code = code.astype(BF16)
    for z in range(planes):
        span = pl.ds(z * tall, tall)
        out_ref[z, :tall, :] = (keep_ref[span, :] + got_ref[span, :].astype(F32)).astype(BF16)
        out_ref[z, tall:, :] = code


def update_kernel(group_ref, store_ref, rows_ref, parts_ref, up_ref, send_ref, acc):
    slots = group_ref.shape[1]
    stored, rank, _ = up_ref.shape
    owners, rows, block = send_ref.shape
    owner = lax.axis_index("owner")

    def total(start, size):
        part = parts_ref[0, start : start + size, :].astype(F32)
        for z in range(1, parts_ref.shape[0]):
            part = part + parts_ref[z, start : start + size, :].astype(F32)
        return part

    packed = total(2 * rows, rows // 2)
    code = jnp.concatenate([packed[:, :rank], packed[:, rank:]], axis=0).astype(BF16).astype(F32)
    ids = row_adapters(rows_ref, rank)
    acc[...] = jnp.zeros_like(acc)
    for s in range(slots):
        spot, here = slot_position(s, group_ref, store_ref, stored)

        @pl.when(here)
        def _(s=s, spot=spot):
            chosen = jnp.where(ids == group_ref[0, s], code, 0.0).astype(BF16)
            acc[...] += jnp.dot(chosen, up_ref[spot], preferred_element_type=F32)

    own, across = total(0, rows), total(rows, rows)
    for o in range(owners):
        update = ADAPTER_SCALE * acc[:, o * block : (o + 1) * block]
        base = jnp.where(owner == o, own, jnp.where(owner == (o + 2) % owners, across, 0.0))
        send_ref[o] = (base + update).astype(BF16)


def final_kernel(got_ref, out_ref):
    total = got_ref[0].astype(F32)
    for o in range(1, got_ref.shape[0]):
        total = total + got_ref[o].astype(F32)
    out_ref[...] = total.astype(BF16)


def shards(
    queries,
    cached_key_rows,
    cached_value_rows,
    newest_key,
    newest_value,
    output_weight,
    adapter_down_weight,
    adapter_up_weight,
    adapter_store_row,
    adapters_by_group,
    adapter_per_row,
):
    owners = lax.axis_size("owner")
    tensors = lax.axis_size("tensor")
    planes = tensors // 2
    slots = adapters_by_group.shape[1]
    row_count, local_heads, head_width = newest_key.shape
    rows = adapter_per_row.shape[0]
    feats = local_heads * output_weight.shape[1]
    columns = output_weight.shape[2]
    block = columns // (tensors * owners)
    rank = adapter_down_weight.shape[-1]
    row_ids = adapter_per_row.reshape(1, rows)

    slab = pltpu.VMEM((feats, columns // owners), BF16)
    weight, local_queries, right, left = pl.pallas_call(
        slab_kernel,
        name="slabs",
        out_shape=(
            pltpu.VMEM((feats, columns), BF16),
            pltpu.VMEM(queries.shape, BF16),
            slab,
            slab,
        ),
        in_specs=[HBM, HBM],
        out_specs=(VMEM, VMEM, VMEM, VMEM),
        scratch_shapes=[pltpu.SemaphoreType.DMA((5,))],
        compiler_params=LIMIT,
    )(far(output_weight.reshape(feats, columns)), far(queries))
    before = lax.ppermute(right, "owner", [(o, (o + 1) % owners) for o in range(owners)])
    after = lax.ppermute(left, "owner", [(o, (o - 1) % owners) for o in range(owners)])

    outgoing, tables = pl.pallas_call(
        attend_kernel,
        name="attend",
        out_shape=(
            pltpu.VMEM((owners, tensors, row_count, feats), BF16),
            pltpu.VMEM((slots,) + adapter_down_weight.shape[1:], BF16),
        ),
        in_specs=[SMEM, SMEM, VMEM, VMEM, HBM, VMEM, VMEM, HBM],
        out_specs=(VMEM, VMEM),
        scratch_shapes=[
            pltpu.VMEM((row_count, cached_value_rows.shape[1] * local_heads, head_width), BF16),
            pltpu.SemaphoreType.DMA,
            pltpu.SemaphoreType.DMA((slots,)),
        ],
        compiler_params=LIMIT,
    )(
        adapters_by_group,
        adapter_store_row,
        near(local_queries),
        near(cached_key_rows.reshape(row_count, -1, head_width)),
        far(cached_value_rows.reshape(row_count, -1, head_width)),
        newest_key,
        newest_value,
        far(adapter_down_weight),
    )
    outgoing = outgoing.reshape(owners * tensors, row_count, feats)
    attention = lax.all_to_all(
        outgoing, ("owner", "tensor"), split_axis=0, concat_axis=0, tiled=True
    )
    attention = attention.reshape(owners, rows, feats)

    tall = 2 * planes * rows + rows // 2
    keep, send = pl.pallas_call(
        project_kernel,
        name="project",
        out_shape=(pltpu.VMEM((tall, block), F32), pltpu.VMEM((tall, block), BF16)),
        in_specs=[SMEM, SMEM] + [VMEM] * 6,
        out_specs=(VMEM, VMEM),
        scratch_shapes=[pltpu.VMEM((rows, rank), F32)],
        compiler_params=LIMIT,
    )(
        adapters_by_group,
        adapter_store_row,
        row_ids,
        near(attention),
        near(weight),
        near(before),
        near(after),
        near(tables),
    )
    got = lax.ppermute(send, "tensor", [(t, t ^ 1) for t in range(tensors)])
    pieces = pl.pallas_call(
        pair_kernel,
        name="pair",
        out_shape=pltpu.VMEM((planes, 2 * rows + rows // 2, block), BF16),
        in_specs=[VMEM, VMEM],
        out_specs=VMEM,
        compiler_params=LIMIT,
    )(near(keep), near(got))
    groups = [[2 * z + c for z in range(planes)] for c in range(2)]
    parts = lax.all_to_all(
        pieces, "tensor", split_axis=0, concat_axis=0, tiled=True, axis_index_groups=groups
    )
    sums = pl.pallas_call(
        update_kernel,
        name="update",
        out_shape=pltpu.VMEM((owners, rows, block), BF16),
        in_specs=[SMEM, SMEM, VMEM, VMEM, VMEM],
        out_specs=VMEM,
        scratch_shapes=[pltpu.VMEM((rows, owners * block), F32)],
        compiler_params=LIMIT,
    )(adapters_by_group, adapter_store_row, row_ids, near(parts), near(adapter_up_weight))
    sums = lax.all_to_all(sums, "owner", split_axis=0, concat_axis=0, tiled=True)
    return pl.pallas_call(
        final_kernel,
        name="final",
        out_shape=jax.ShapeDtypeStruct((rows, block), BF16),
        in_specs=[VMEM],
        out_specs=VMEM,
        compiler_params=LIMIT,
    )(near(sums))


def solution(mesh):
    return jax.shard_map(
        shards,
        mesh=mesh,
        in_specs=(
            P(("dp", "tensor"), "owner"),
            P(("dp", "tensor"), None, "owner", None),
            P(("dp", "tensor"), None, "owner", None),
            P(("dp", "tensor"), "owner", None),
            P(("dp", "tensor"), "owner", None),
            P("owner", "tensor", None),
            P("owner", None, "tensor", None),
            P("owner", None, "tensor"),
            P(),
            P("dp", None),
            P("dp"),
        ),
        out_specs=P("dp", ("tensor", "owner")),
        check_vma=False,
    )
```

```python
import jax
import jax.numpy as jnp
from jax import lax
from jax.experimental import pallas as pl
from jax.experimental.pallas import tpu as pltpu
from jax.sharding import PartitionSpec as P

ADAPTER_SCALE = 2.0
BF16 = jnp.bfloat16
F32 = jnp.float32

VMEM = pl.BlockSpec(memory_space=pltpu.VMEM)
SMEM = pl.BlockSpec(memory_space=pltpu.SMEM)
HBM = pl.BlockSpec(memory_space=pltpu.HBM)
LIMIT = pltpu.CompilerParams(vmem_limit_bytes=16 * 1024 * 1024)


def near(array):
    return pltpu.with_memory_space_constraint(array, pltpu.VMEM)


def far(array):
    return pltpu.with_memory_space_constraint(array, pltpu.HBM)


def slot_position(slot, group_ref, store_ref, stored):
    spot = store_ref[group_ref[0, slot]] - lax.axis_index("owner") * stored
    here = jnp.logical_and(spot >= 0, spot < stored)
    return jnp.clip(spot, 0, stored - 1), here


def row_adapters(rows_ref, width):
    rows = rows_ref.shape[1]
    return jnp.transpose(jnp.broadcast_to(rows_ref[...], (rows, rows)))[:, :width]


def slab_kernel(w_hbm_ref, queries_hbm_ref, w_ref, queries_ref, right_ref, left_ref, sems):
    chunks = sems.shape[0] - 1
    step = w_ref.shape[0] // chunks
    copies = [
        pltpu.make_async_copy(
            w_hbm_ref.at[pl.ds(i * step, step)], w_ref.at[pl.ds(i * step, step)], sems.at[i]
        )
        for i in range(chunks)
    ]
    copies.append(pltpu.make_async_copy(queries_hbm_ref, queries_ref, sems.at[chunks]))
    for copy in copies:
        copy.start()
    owner, owners = lax.axis_index("owner"), lax.axis_size("owner")
    targets = [lax.rem(owner + 1, owners), lax.rem(owner + owners - 1, owners)]
    for i in range(chunks):
        copies[i].wait()
        rows = pl.ds(i * step, step)
        for out_ref, target in zip((right_ref, left_ref), targets):
            for block in range(out_ref.shape[1] // 128):
                at = pl.multiple_of((block * owners + target) * 128, 128)
                out_ref[rows, block * 128 : (block + 1) * 128] = w_ref[rows, pl.ds(at, 128)]
    copies[chunks].wait()


def attend_kernel(
    group_ref,
    store_ref,
    queries_ref,
    keys_ref,
    values_hbm_ref,
    key_ref,
    value_ref,
    down_ref,
    out_ref,
    slots_ref,
    values_ref,
    value_sem,
    sems,
):
    stored = down_ref.shape[0]
    values_copy = pltpu.make_async_copy(values_hbm_ref, values_ref, value_sem)
    values_copy.start()
    copies = []
    for s in range(slots_ref.shape[0]):
        spot, _ = slot_position(s, group_ref, store_ref, stored)
        copies.append(pltpu.make_async_copy(down_ref.at[spot], slots_ref.at[s], sems.at[s]))
    for copy in copies:
        copy.start()

    rows, local, width = key_ref.shape
    heads = queries_ref.shape[1] // width
    grouped = heads // local
    positions = keys_ref.shape[1]
    scale = width ** (-0.5)
    queries = [queries_ref[:, h * width : (h + 1) * width].astype(F32) for h in range(heads)]
    queries = jnp.swapaxes(jnp.stack(queries), 0, 1)
    row_head = lax.broadcasted_iota(jnp.int32, (heads, positions), 0) // grouped
    place_head = lax.broadcasted_iota(jnp.int32, (heads, positions), 1) % local
    same = row_head == place_head

    def spread(ref, r):
        fresh = ref[r].astype(F32)
        parts = [jnp.broadcast_to(fresh[k : k + 1], (grouped, width)) for k in range(local)]
        return jnp.concatenate(parts, axis=0)

    weights, fresh_weights, denominators = [], [], []
    for r in range(rows):
        query = queries[r]
        scores = lax.dot_general(
            query.astype(BF16), keys_ref[r], (((1,), (1,)), ((), ())), preferred_element_type=F32
        )
        scores = jnp.where(same, scores * scale, -jnp.inf)
        fresh_score = jnp.sum(query * spread(key_ref, r), axis=1, keepdims=True) * scale
        overall = jnp.maximum(jnp.max(scores, axis=1, keepdims=True), fresh_score)
        weight = jnp.exp(scores - overall)
        fresh_weight = jnp.exp(fresh_score - overall)
        denominators.append(jnp.sum(weight, axis=1, keepdims=True) + fresh_weight)
        weights.append(weight.astype(BF16))
        fresh_weights.append(fresh_weight)
    values_copy.wait()
    mixed = []
    for r in range(rows):
        total = jnp.dot(weights[r], values_ref[r], preferred_element_type=F32)
        total = total + fresh_weights[r] * spread(value_ref, r)
        mixed.append(total / denominators[r])
    mixed = jnp.swapaxes(jnp.stack(mixed), 0, 1)

    half = width // 2
    low = lax.broadcasted_iota(jnp.int32, (rows, width), 1) < half
    for g in range(grouped):
        one, two = mixed[g], mixed[grouped + g]
        pair = (
            jnp.where(low, one, pltpu.roll(two, half, 1)),
            jnp.where(low, pltpu.roll(one, half, 1), two),
        )
        for i, part in enumerate(pair):
            part = part.astype(BF16)
            for o in range(out_ref.shape[0]):
                out_ref[o, 2 * g + i] = part
    for copy in copies:
        copy.wait()


def project_kernel(
    group_ref,
    store_ref,
    rows_ref,
    att_ref,
    w_ref,
    before_ref,
    after_ref,
    slots_ref,
    keep_ref,
    send_ref,
    acc,
):
    slots, _, _, rank = slots_ref.shape
    stored = store_ref.shape[0] // lax.axis_size("owner")
    owners, rows, feats = att_ref.shape
    owner = lax.axis_index("owner")
    mine = att_ref[owner]
    beside = jnp.concatenate(
        [att_ref[lax.rem(owner + owners - 1, owners)], att_ref[lax.rem(owner + 1, owners)]], axis=1
    )
    first = lax.rem(lax.axis_index("tensor"), 2) == 0
    block = keep_ref.shape[1]
    planes = before_ref.shape[1] // (2 * block)

    across = lax.rem(owner + 2, owners)

    def columns(z, target):
        at = [pl.multiple_of(((2 * z + c) * owners + target) * block, block) for c in range(2)]
        return jnp.concatenate([w_ref[:, pl.ds(a, block)] for a in at], axis=1)

    for z in range(planes):
        span = pl.ds(z * 2 * block, 2 * block)
        near_rows = jnp.concatenate([before_ref[:, span], after_ref[:, span]], axis=0)
        here = jnp.dot(beside, near_rows, preferred_element_type=F32)
        here = here + jnp.dot(mine, columns(z, owner), preferred_element_type=F32)
        there = jnp.dot(mine, columns(z, across), preferred_element_type=F32)
        for i, part in enumerate((here, there)):
            even, odd = part[:, :block], part[:, block:]
            rows_span = pl.ds((2 * z + i) * rows, rows)
            keep_ref[rows_span, :] = jnp.where(first, even, odd)
            send_ref[rows_span, :] = jnp.where(first, odd, even).astype(BF16)
    att = jnp.concatenate([att_ref[o] for o in range(owners)], axis=1)
    ids = row_adapters(rows_ref, rank)
    acc[...] = jnp.zeros_like(acc)
    for s in range(slots):
        _, here = slot_position(s, group_ref, store_ref, stored)

        @pl.when(here)
        def _(s=s):
            table = slots_ref[s].reshape(owners * feats, rank)
            code = jnp.dot(att, table, preferred_element_type=F32)
            acc[...] += jnp.where(ids == group_ref[0, s], code, 0.0)

    half = rows // 2
    code = jnp.concatenate([acc[:half, :], acc[half:, :]], axis=1)
    keep_ref[2 * planes * rows :, :] = code
    send_ref[2 * planes * rows :, :] = code.astype(BF16)


def pair_kernel(keep_ref, got_ref, own_ref, across_ref, codes_ref):
    planes, rows, _ = own_ref.shape
    for z in range(planes):
        span = pl.ds(2 * z * rows, rows)
        own_ref[z] = keep_ref[span, :] + got_ref[span, :].astype(F32)
        span = pl.ds((2 * z + 1) * rows, rows)
        across_ref[z] = (keep_ref[span, :] + got_ref[span, :].astype(F32)).astype(BF16)
    span = pl.ds(2 * planes * rows, codes_ref.shape[1])
    code = (keep_ref[span, :] + got_ref[span, :].astype(F32)).astype(BF16)
    for z in range(planes):
        codes_ref[z] = code


def add_kernel(one_ref, two_ref, out_ref):
    out_ref[...] = (one_ref[...] + two_ref[...].astype(F32)).astype(BF16)


def update_kernel(
    group_ref, store_ref, rows_ref, codes_ref, up_ref, own_ref, *rest
):
    send_refs, (ubuf, acc, sems) = rest[:-3], rest[-3:]
    slots, rank, _ = ubuf.shape
    stored = up_ref.shape[0]
    copies = []
    for s in range(slots):
        spot, _ = slot_position(s, group_ref, store_ref, stored)
        copy = pltpu.make_async_copy(up_ref.at[spot], ubuf.at[s], sems.at[s])
        copy.start()
        copies.append(copy)
    rows, block = own_ref.shape
    owners = lax.axis_size("owner")
    owner = lax.axis_index("owner")
    packed = codes_ref[0].astype(F32)
    for z in range(1, codes_ref.shape[0]):
        packed = packed + codes_ref[z].astype(F32)
    code = jnp.concatenate([packed[:, :rank], packed[:, rank:]], axis=0).astype(BF16).astype(F32)
    ids = row_adapters(rows_ref, rank)
    acc[...] = jnp.zeros_like(acc)
    for s in range(slots):
        copies[s].wait()
        _, here = slot_position(s, group_ref, store_ref, stored)

        @pl.when(here)
        def _(s=s):
            chosen = jnp.where(ids == group_ref[0, s], code, 0.0).astype(BF16)
            acc[...] += jnp.dot(chosen, ubuf[s], preferred_element_type=F32)

    def columns(target):
        return acc[:, pl.ds(pl.multiple_of(target * block, block), block)]

    own_ref[...] = columns(owner)
    for i, send_ref in enumerate(send_refs):
        send_ref[...] = columns(lax.rem(owner + i + 1, owners)).astype(BF16)


def final_kernel(parts_ref, own_ref, *rest):
    got_refs, out_ref = rest[:-1], rest[-1]
    base = parts_ref[0].astype(F32)
    for z in range(1, parts_ref.shape[0]):
        base = base + parts_ref[z].astype(F32)
    update = own_ref[...]
    for got_ref in got_refs:
        update = update + got_ref[...].astype(F32)
    out_ref[...] = (base + ADAPTER_SCALE * update).astype(BF16)


def shards(
    queries,
    cached_key_rows,
    cached_value_rows,
    newest_key,
    newest_value,
    output_weight,
    adapter_down_weight,
    adapter_up_weight,
    adapter_store_row,
    adapters_by_group,
    adapter_per_row,
):
    owners = lax.axis_size("owner")
    tensors = lax.axis_size("tensor")
    planes = tensors // 2
    slots = adapters_by_group.shape[1]
    row_count, local_heads, head_width = newest_key.shape
    rows = adapter_per_row.shape[0]
    feats = local_heads * output_weight.shape[1]
    columns = output_weight.shape[2]
    block = columns // (tensors * owners)
    rank = adapter_down_weight.shape[-1]
    row_ids = adapter_per_row.reshape(1, rows)

    slab = pltpu.VMEM((feats, columns // owners), BF16)
    weight, local_queries, right, left = pl.pallas_call(
        slab_kernel,
        name="slabs",
        out_shape=(
            pltpu.VMEM((feats, columns), BF16),
            pltpu.VMEM(queries.shape, BF16),
            slab,
            slab,
        ),
        in_specs=[HBM, HBM],
        out_specs=(VMEM, VMEM, VMEM, VMEM),
        scratch_shapes=[pltpu.SemaphoreType.DMA((5,))],
        compiler_params=LIMIT,
    )(far(output_weight.reshape(feats, columns)), far(queries))
    before = lax.ppermute(right, "owner", [(o, (o + 1) % owners) for o in range(owners)])
    after = lax.ppermute(left, "owner", [(o, (o - 1) % owners) for o in range(owners)])

    outgoing, tables = pl.pallas_call(
        attend_kernel,
        name="attend",
        out_shape=(
            pltpu.VMEM((owners, tensors, row_count, feats), BF16),
            pltpu.VMEM((slots,) + adapter_down_weight.shape[1:], BF16),
        ),
        in_specs=[SMEM, SMEM, VMEM, VMEM, HBM, VMEM, VMEM, HBM],
        out_specs=(VMEM, VMEM),
        scratch_shapes=[
            pltpu.VMEM((row_count, cached_value_rows.shape[1] * local_heads, head_width), BF16),
            pltpu.SemaphoreType.DMA,
            pltpu.SemaphoreType.DMA((slots,)),
        ],
        compiler_params=LIMIT,
    )(
        adapters_by_group,
        adapter_store_row,
        near(local_queries),
        near(cached_key_rows.reshape(row_count, -1, head_width)),
        far(cached_value_rows.reshape(row_count, -1, head_width)),
        newest_key,
        newest_value,
        far(adapter_down_weight),
    )
    outgoing = outgoing.reshape(owners * tensors, row_count, feats)
    attention = lax.all_to_all(
        outgoing, ("owner", "tensor"), split_axis=0, concat_axis=0, tiled=True
    )
    attention = attention.reshape(owners, rows, feats)

    tall = 2 * planes * rows + rows // 2
    keep, send = pl.pallas_call(
        project_kernel,
        name="project",
        out_shape=(pltpu.VMEM((tall, block), F32), pltpu.VMEM((tall, block), BF16)),
        in_specs=[SMEM, SMEM] + [VMEM] * 6,
        out_specs=(VMEM, VMEM),
        scratch_shapes=[pltpu.VMEM((rows, rank), F32)],
        compiler_params=LIMIT,
    )(
        adapters_by_group,
        adapter_store_row,
        row_ids,
        near(attention),
        near(weight),
        near(before),
        near(after),
        near(tables),
    )
    got = lax.ppermute(send, "tensor", [(t, t ^ 1) for t in range(tensors)])
    own_part, across, codes = pl.pallas_call(
        pair_kernel,
        name="pair",
        out_shape=(
            pltpu.VMEM((planes, rows, block), F32),
            pltpu.VMEM((planes, rows, block), BF16),
            pltpu.VMEM((planes, rows // 2, 2 * rank), BF16),
        ),
        in_specs=[VMEM, VMEM],
        out_specs=(VMEM, VMEM, VMEM),
        compiler_params=LIMIT,
    )(near(keep), near(got))
    groups = [[2 * z + c for z in range(planes)] for c in range(2)]

    def over_z(pieces):
        return lax.all_to_all(
            pieces, "tensor", split_axis=0, concat_axis=0, tiled=True, axis_index_groups=groups
        )

    across = lax.ppermute(across, "owner", [(o, (o + 2) % owners) for o in range(owners)])
    codes = over_z(codes)
    strip = pltpu.VMEM((rows, block), BF16)
    own_update, *updates = pl.pallas_call(
        update_kernel,
        name="update",
        out_shape=(pltpu.VMEM((rows, block), F32),) + (strip,) * (owners - 1),
        in_specs=[SMEM, SMEM] + [VMEM] * 2 + [HBM],
        out_specs=(VMEM,) * owners,
        scratch_shapes=[
            pltpu.VMEM((slots,) + adapter_up_weight.shape[1:], BF16),
            pltpu.VMEM((rows, owners * block), F32),
            pltpu.SemaphoreType.DMA((slots,)),
        ],
        compiler_params=LIMIT,
    )(adapters_by_group, adapter_store_row, row_ids, near(codes), far(adapter_up_weight))
    updates = [
        lax.ppermute(update, "owner", [(o, (o + i + 1) % owners) for o in range(owners)])
        for i, update in enumerate(updates)
    ]
    parts = over_z(
        pl.pallas_call(
            add_kernel,
            name="add",
            out_shape=pltpu.VMEM((planes, rows, block), BF16),
            in_specs=[VMEM, VMEM],
            out_specs=VMEM,
            compiler_params=LIMIT,
        )(near(own_part), near(across))
    )
    return pl.pallas_call(
        final_kernel,
        name="final",
        out_shape=jax.ShapeDtypeStruct((rows, block), BF16),
        in_specs=[VMEM] * (owners + 1),
        out_specs=VMEM,
        compiler_params=LIMIT,
    )(near(parts), near(own_update), *[near(update) for update in updates])


def solution(mesh):
    return jax.shard_map(
        shards,
        mesh=mesh,
        in_specs=(
            P(("dp", "tensor"), "owner"),
            P(("dp", "tensor"), None, "owner", None),
            P(("dp", "tensor"), None, "owner", None),
            P(("dp", "tensor"), "owner", None),
            P(("dp", "tensor"), "owner", None),
            P("owner", "tensor", None),
            P("owner", None, "tensor", None),
            P("owner", None, "tensor"),
            P(),
            P("dp", None),
            P("dp"),
        ),
        out_specs=P("dp", ("tensor", "owner")),
        check_vma=False,
    )
```

```python
import jax
import jax.numpy as jnp
from jax import lax
from jax.experimental import pallas as pl
from jax.experimental.pallas import tpu as pltpu
from jax.sharding import PartitionSpec as P

ADAPTER_SCALE = 2.0
BF16 = jnp.bfloat16
F32 = jnp.float32

VMEM = pl.BlockSpec(memory_space=pltpu.VMEM)
SMEM = pl.BlockSpec(memory_space=pltpu.SMEM)
HBM = pl.BlockSpec(memory_space=pltpu.HBM)
LIMIT = pltpu.CompilerParams(vmem_limit_bytes=16 * 1024 * 1024)


def near(array):
    return pltpu.with_memory_space_constraint(array, pltpu.VMEM)


def far(array):
    return pltpu.with_memory_space_constraint(array, pltpu.HBM)


def slot_position(slot, group_ref, store_ref, stored):
    spot = store_ref[group_ref[0, slot]] - lax.axis_index("owner") * stored
    here = jnp.logical_and(spot >= 0, spot < stored)
    return jnp.clip(spot, 0, stored - 1), here


def row_adapters(rows_ref, width):
    rows = rows_ref.shape[1]
    return jnp.transpose(jnp.broadcast_to(rows_ref[...], (rows, rows)))[:, :width]


def slab_kernel(w_hbm_ref, queries_hbm_ref, w_ref, queries_ref, right_ref, left_ref, sems):
    chunks = sems.shape[0] - 1
    step = w_ref.shape[0] // chunks
    copies = [
        pltpu.make_async_copy(
            w_hbm_ref.at[pl.ds(i * step, step)], w_ref.at[pl.ds(i * step, step)], sems.at[i]
        )
        for i in range(chunks)
    ]
    copies.append(pltpu.make_async_copy(queries_hbm_ref, queries_ref, sems.at[chunks]))
    for copy in copies:
        copy.start()
    owner, owners = lax.axis_index("owner"), lax.axis_size("owner")
    targets = [lax.rem(owner + 1, owners), lax.rem(owner + owners - 1, owners)]
    for i in range(chunks):
        copies[i].wait()
        rows = pl.ds(i * step, step)
        for out_ref, target in zip((right_ref, left_ref), targets):
            for block in range(out_ref.shape[1] // 128):
                at = pl.multiple_of((block * owners + target) * 128, 128)
                out_ref[rows, block * 128 : (block + 1) * 128] = w_ref[rows, pl.ds(at, 128)]
    copies[chunks].wait()


def attend_kernel(
    group_ref,
    store_ref,
    queries_ref,
    keys_ref,
    values_hbm_ref,
    key_ref,
    value_ref,
    down_ref,
    out_ref,
    slots_ref,
    values_ref,
    value_sems,
    sems,
):
    stored = down_ref.shape[0]
    part = values_ref.shape[1] // 2
    value_copies = [
        pltpu.make_async_copy(
            values_hbm_ref.at[r, pl.ds(i * part, part)],
            values_ref.at[r, pl.ds(i * part, part)],
            value_sems.at[2 * r + i],
        )
        for r in range(values_ref.shape[0])
        for i in range(2)
    ]
    for copy in value_copies:
        copy.start()
    copies = []
    for s in range(slots_ref.shape[0]):
        spot, _ = slot_position(s, group_ref, store_ref, stored)
        copies.append(pltpu.make_async_copy(down_ref.at[spot], slots_ref.at[s], sems.at[s]))
    for copy in copies:
        copy.start()

    rows, local, width = key_ref.shape
    heads = queries_ref.shape[1] // width
    grouped = heads // local
    positions = keys_ref.shape[1]
    scale = width ** (-0.5)
    queries = [queries_ref[:, h * width : (h + 1) * width].astype(F32) for h in range(heads)]
    queries = jnp.swapaxes(jnp.stack(queries), 0, 1)
    row_head = lax.broadcasted_iota(jnp.int32, (heads, positions), 0) // grouped
    place_head = lax.broadcasted_iota(jnp.int32, (heads, positions), 1) % local
    same = row_head == place_head

    def spread(ref, r):
        fresh = ref[r].astype(F32)
        parts = [jnp.broadcast_to(fresh[k : k + 1], (grouped, width)) for k in range(local)]
        return jnp.concatenate(parts, axis=0)

    weights, fresh_weights, denominators = [], [], []
    for r in range(rows):
        query = queries[r]
        scores = lax.dot_general(
            query.astype(BF16), keys_ref[r], (((1,), (1,)), ((), ())), preferred_element_type=F32
        )
        scores = jnp.where(same, scores * scale, -jnp.inf)
        fresh_score = jnp.sum(query * spread(key_ref, r), axis=1, keepdims=True) * scale
        overall = jnp.maximum(jnp.max(scores, axis=1, keepdims=True), fresh_score)
        weight = jnp.exp(scores - overall)
        fresh_weight = jnp.exp(fresh_score - overall)
        denominators.append(jnp.sum(weight, axis=1, keepdims=True) + fresh_weight)
        weights.append(weight.astype(BF16))
        fresh_weights.append(fresh_weight)
    for copy in value_copies:
        copy.wait()
    mixed = []
    for r in range(rows):
        total = jnp.dot(weights[r], values_ref[r], preferred_element_type=F32)
        total = total + fresh_weights[r] * spread(value_ref, r)
        mixed.append(total / denominators[r])
    mixed = jnp.swapaxes(jnp.stack(mixed), 0, 1)

    half = width // 2
    low = lax.broadcasted_iota(jnp.int32, (rows, width), 1) < half
    for g in range(grouped):
        one, two = mixed[g], mixed[grouped + g]
        pair = (
            jnp.where(low, one, pltpu.roll(two, half, 1)),
            jnp.where(low, pltpu.roll(one, half, 1), two),
        )
        for i, part in enumerate(pair):
            part = part.astype(BF16)
            for o in range(out_ref.shape[0]):
                out_ref[o, 2 * g + i] = part
    for copy in copies:
        copy.wait()


def project_kernel(
    group_ref,
    store_ref,
    rows_ref,
    att_ref,
    w_ref,
    before_ref,
    after_ref,
    slots_ref,
    keep_ref,
    send_ref,
    acc,
):
    slots, _, _, rank = slots_ref.shape
    stored = store_ref.shape[0] // lax.axis_size("owner")
    owners, rows, feats = att_ref.shape
    owner = lax.axis_index("owner")
    mine = att_ref[owner]
    beside = jnp.concatenate(
        [att_ref[lax.rem(owner + owners - 1, owners)], att_ref[lax.rem(owner + 1, owners)]], axis=1
    )
    first = lax.rem(lax.axis_index("tensor"), 2) == 0
    block = keep_ref.shape[1]
    planes = before_ref.shape[1] // (2 * block)

    across = lax.rem(owner + 2, owners)

    def columns(z, target):
        at = [pl.multiple_of(((2 * z + c) * owners + target) * block, block) for c in range(2)]
        return jnp.concatenate([w_ref[:, pl.ds(a, block)] for a in at], axis=1)

    for z in range(planes):
        span = pl.ds(z * 2 * block, 2 * block)
        near_rows = jnp.concatenate([before_ref[:, span], after_ref[:, span]], axis=0)
        here = jnp.dot(beside, near_rows, preferred_element_type=F32)
        here = here + jnp.dot(mine, columns(z, owner), preferred_element_type=F32)
        there = jnp.dot(mine, columns(z, across), preferred_element_type=F32)
        for i, part in enumerate((here, there)):
            even, odd = part[:, :block], part[:, block:]
            rows_span = pl.ds((2 * z + i) * rows, rows)
            keep_ref[rows_span, :] = jnp.where(first, even, odd)
            send_ref[rows_span, :] = jnp.where(first, odd, even).astype(BF16)
    att = jnp.concatenate([att_ref[o] for o in range(owners)], axis=1)
    ids = row_adapters(rows_ref, rank)
    acc[...] = jnp.zeros_like(acc)
    for s in range(slots):
        _, here = slot_position(s, group_ref, store_ref, stored)

        @pl.when(here)
        def _(s=s):
            table = slots_ref[s].reshape(owners * feats, rank)
            code = jnp.dot(att, table, preferred_element_type=F32)
            acc[...] += jnp.where(ids == group_ref[0, s], code, 0.0)

    half = rows // 2
    code = jnp.concatenate([acc[:half, :], acc[half:, :]], axis=1)
    keep_ref[2 * planes * rows :, :] = code
    send_ref[2 * planes * rows :, :] = code.astype(BF16)


def pair_kernel(keep_ref, got_ref, own_ref, across_ref, codes_ref):
    planes, rows, _ = own_ref.shape
    for z in range(planes):
        span = pl.ds(2 * z * rows, rows)
        own_ref[z] = keep_ref[span, :] + got_ref[span, :].astype(F32)
        span = pl.ds((2 * z + 1) * rows, rows)
        across_ref[z] = (keep_ref[span, :] + got_ref[span, :].astype(F32)).astype(BF16)
    span = pl.ds(2 * planes * rows, codes_ref.shape[1])
    code = (keep_ref[span, :] + got_ref[span, :].astype(F32)).astype(BF16)
    for z in range(planes):
        codes_ref[z] = code


def add_kernel(one_ref, two_ref, out_ref):
    out_ref[...] = (one_ref[...] + two_ref[...].astype(F32)).astype(BF16)


def update_kernel(group_ref, store_ref, rows_ref, codes_ref, up_ref, own_ref, *rest):
    send_refs, acc = rest[:-1], rest[-1]
    slots = group_ref.shape[1]
    stored, rank, _ = up_ref.shape
    rows, block = own_ref.shape
    owners = lax.axis_size("owner")
    owner = lax.axis_index("owner")
    packed = codes_ref[0].astype(F32)
    for z in range(1, codes_ref.shape[0]):
        packed = packed + codes_ref[z].astype(F32)
    code = jnp.concatenate([packed[:, :rank], packed[:, rank:]], axis=0).astype(BF16).astype(F32)
    ids = row_adapters(rows_ref, rank)
    acc[...] = jnp.zeros_like(acc)
    for s in range(slots):
        spot, here = slot_position(s, group_ref, store_ref, stored)

        @pl.when(here)
        def _(s=s, spot=spot):
            chosen = jnp.where(ids == group_ref[0, s], code, 0.0).astype(BF16)
            acc[...] += jnp.dot(chosen, up_ref[spot], preferred_element_type=F32)

    def columns(target):
        return acc[:, pl.ds(pl.multiple_of(target * block, block), block)]

    own_ref[...] = columns(owner)
    for i, send_ref in enumerate(send_refs):
        send_ref[...] = columns(lax.rem(owner + i + 1, owners)).astype(BF16)


def final_kernel(parts_ref, own_ref, *rest):
    got_refs, out_ref = rest[:-1], rest[-1]
    base = parts_ref[0].astype(F32)
    for z in range(1, parts_ref.shape[0]):
        base = base + parts_ref[z].astype(F32)
    update = own_ref[...]
    for got_ref in got_refs:
        update = update + got_ref[...].astype(F32)
    out_ref[...] = (base + ADAPTER_SCALE * update).astype(BF16)


def shards(
    queries,
    cached_key_rows,
    cached_value_rows,
    newest_key,
    newest_value,
    output_weight,
    adapter_down_weight,
    adapter_up_weight,
    adapter_store_row,
    adapters_by_group,
    adapter_per_row,
):
    owners = lax.axis_size("owner")
    tensors = lax.axis_size("tensor")
    planes = tensors // 2
    slots = adapters_by_group.shape[1]
    row_count, local_heads, head_width = newest_key.shape
    rows = adapter_per_row.shape[0]
    feats = local_heads * output_weight.shape[1]
    columns = output_weight.shape[2]
    block = columns // (tensors * owners)
    rank = adapter_down_weight.shape[-1]
    row_ids = adapter_per_row.reshape(1, rows)

    slab = pltpu.VMEM((feats, columns // owners), BF16)
    weight, local_queries, right, left = pl.pallas_call(
        slab_kernel,
        name="slabs",
        out_shape=(
            pltpu.VMEM((feats, columns), BF16),
            pltpu.VMEM(queries.shape, BF16),
            slab,
            slab,
        ),
        in_specs=[HBM, HBM],
        out_specs=(VMEM, VMEM, VMEM, VMEM),
        scratch_shapes=[pltpu.SemaphoreType.DMA((feats // 8 + 1,))],
        compiler_params=LIMIT,
    )(far(output_weight.reshape(feats, columns)), far(queries))
    before = lax.ppermute(right, "owner", [(o, (o + 1) % owners) for o in range(owners)])
    after = lax.ppermute(left, "owner", [(o, (o - 1) % owners) for o in range(owners)])

    outgoing, tables = pl.pallas_call(
        attend_kernel,
        name="attend",
        out_shape=(
            pltpu.VMEM((owners, tensors, row_count, feats), BF16),
            pltpu.VMEM((slots,) + adapter_down_weight.shape[1:], BF16),
        ),
        in_specs=[SMEM, SMEM, VMEM, VMEM, HBM, VMEM, VMEM, HBM],
        out_specs=(VMEM, VMEM),
        scratch_shapes=[
            pltpu.VMEM((row_count, cached_value_rows.shape[1] * local_heads, head_width), BF16),
            pltpu.SemaphoreType.DMA((2 * row_count,)),
            pltpu.SemaphoreType.DMA((slots,)),
        ],
        compiler_params=LIMIT,
    )(
        adapters_by_group,
        adapter_store_row,
        near(local_queries),
        near(cached_key_rows.reshape(row_count, -1, head_width)),
        far(cached_value_rows.reshape(row_count, -1, head_width)),
        newest_key,
        newest_value,
        far(adapter_down_weight),
    )
    outgoing = outgoing.reshape(owners * tensors, row_count, feats)
    attention = lax.all_to_all(
        outgoing, ("owner", "tensor"), split_axis=0, concat_axis=0, tiled=True
    )
    attention = attention.reshape(owners, rows, feats)

    tall = 2 * planes * rows + rows // 2
    keep, send = pl.pallas_call(
        project_kernel,
        name="project",
        out_shape=(pltpu.VMEM((tall, block), F32), pltpu.VMEM((tall, block), BF16)),
        in_specs=[SMEM, SMEM] + [VMEM] * 6,
        out_specs=(VMEM, VMEM),
        scratch_shapes=[pltpu.VMEM((rows, rank), F32)],
        compiler_params=LIMIT,
    )(
        adapters_by_group,
        adapter_store_row,
        row_ids,
        near(attention),
        near(weight),
        near(before),
        near(after),
        near(tables),
    )
    got = lax.ppermute(send, "tensor", [(t, t ^ 1) for t in range(tensors)])
    own_part, across, codes = pl.pallas_call(
        pair_kernel,
        name="pair",
        out_shape=(
            pltpu.VMEM((planes, rows, block), F32),
            pltpu.VMEM((planes, rows, block), BF16),
            pltpu.VMEM((planes, rows // 2, 2 * rank), BF16),
        ),
        in_specs=[VMEM, VMEM],
        out_specs=(VMEM, VMEM, VMEM),
        compiler_params=LIMIT,
    )(near(keep), near(got))
    groups = [[2 * z + c for z in range(planes)] for c in range(2)]

    def over_z(pieces):
        return lax.all_to_all(
            pieces, "tensor", split_axis=0, concat_axis=0, tiled=True, axis_index_groups=groups
        )

    across = lax.ppermute(across, "owner", [(o, (o + 2) % owners) for o in range(owners)])
    codes = over_z(codes)
    strip = pltpu.VMEM((rows, block), BF16)
    own_update, *updates = pl.pallas_call(
        update_kernel,
        name="update",
        out_shape=(pltpu.VMEM((rows, block), F32),) + (strip,) * (owners - 1),
        in_specs=[SMEM, SMEM] + [VMEM] * 3,
        out_specs=(VMEM,) * owners,
        scratch_shapes=[pltpu.VMEM((rows, owners * block), F32)],
        compiler_params=LIMIT,
    )(adapters_by_group, adapter_store_row, row_ids, near(codes), near(adapter_up_weight))
    updates = [
        lax.ppermute(update, "owner", [(o, (o + i + 1) % owners) for o in range(owners)])
        for i, update in enumerate(updates)
    ]
    parts = over_z(
        pl.pallas_call(
            add_kernel,
            name="add",
            out_shape=pltpu.VMEM((planes, rows, block), BF16),
            in_specs=[VMEM, VMEM],
            out_specs=VMEM,
            compiler_params=LIMIT,
        )(near(own_part), near(across))
    )
    return pl.pallas_call(
        final_kernel,
        name="final",
        out_shape=jax.ShapeDtypeStruct((rows, block), BF16),
        in_specs=[VMEM] * (owners + 1),
        out_specs=VMEM,
        compiler_params=LIMIT,
    )(near(parts), near(own_update), *[near(update) for update in updates])


def solution(mesh):
    return jax.shard_map(
        shards,
        mesh=mesh,
        in_specs=(
            P(("dp", "tensor"), "owner"),
            P(("dp", "tensor"), None, "owner", None),
            P(("dp", "tensor"), None, "owner", None),
            P(("dp", "tensor"), "owner", None),
            P(("dp", "tensor"), "owner", None),
            P("owner", "tensor", None),
            P("owner", None, "tensor", None),
            P("owner", None, "tensor"),
            P(),
            P("dp", None),
            P("dp"),
        ),
        out_specs=P("dp", ("tensor", "owner")),
        check_vma=False,
    )
```

```python
import jax
import jax.numpy as jnp
from jax import lax
from jax.experimental import pallas as pl
from jax.experimental.pallas import tpu as pltpu
from jax.sharding import PartitionSpec as P

ADAPTER_SCALE = 2.0
BF16 = jnp.bfloat16
F32 = jnp.float32

VMEM = pl.BlockSpec(memory_space=pltpu.VMEM)
HBM = pl.BlockSpec(memory_space=pltpu.HBM)
LIMIT = pltpu.CompilerParams(vmem_limit_bytes=16 * 1024 * 1024)


def near(array):
    return pltpu.with_memory_space_constraint(array, pltpu.VMEM)


def far(array):
    return pltpu.with_memory_space_constraint(array, pltpu.HBM)


def slot_position(slot, group_ref, store_ref, stored):
    spot = store_ref[0, group_ref[0, slot]] - lax.axis_index("owner") * stored
    here = jnp.logical_and(spot >= 0, spot < stored)
    return jnp.clip(spot, 0, stored - 1), here


def index_copies(group_ref, store_ref, group, store, sems):
    copies = (
        pltpu.make_async_copy(group_ref, group, sems.at[0]),
        pltpu.make_async_copy(store_ref, store, sems.at[1]),
    )
    for copy in copies:
        copy.start()
    return copies


def row_adapters(rows_ref, width):
    rows = rows_ref.shape[1]
    return jnp.transpose(jnp.broadcast_to(rows_ref[...], (rows, rows)))[:, :width]


def slab_kernel(
    w_hbm_ref,
    queries_hbm_ref,
    values_hbm_ref,
    w_ref,
    queries_ref,
    values_ref,
    right_ref,
    left_ref,
    sems,
    value_sems,
):
    chunks = sems.shape[0] - 1
    step = w_ref.shape[0] // chunks
    copies = [
        pltpu.make_async_copy(
            w_hbm_ref.at[pl.ds(i * step, step)], w_ref.at[pl.ds(i * step, step)], sems.at[i]
        )
        for i in range(chunks)
    ]
    rest = [pltpu.make_async_copy(queries_hbm_ref, queries_ref, sems.at[chunks])]
    rest += [
        pltpu.make_async_copy(values_hbm_ref.at[r], values_ref.at[r], value_sems.at[r])
        for r in range(values_ref.shape[0])
    ]
    for copy in copies + rest:
        copy.start()
    owner, owners = lax.axis_index("owner"), lax.axis_size("owner")
    targets = [lax.rem(owner + 1, owners), lax.rem(owner + owners - 1, owners)]
    for i in range(chunks):
        copies[i].wait()
        rows = pl.ds(i * step, step)
        for out_ref, target in zip((right_ref, left_ref), targets):
            for block in range(out_ref.shape[1] // 128):
                at = pl.multiple_of((block * owners + target) * 128, 128)
                out_ref[rows, block * 128 : (block + 1) * 128] = w_ref[rows, pl.ds(at, 128)]
    for copy in rest:
        copy.wait()


def attend_kernel(
    group_ref,
    store_ref,
    queries_ref,
    keys_ref,
    values_ref,
    key_ref,
    value_ref,
    down_ref,
    out_ref,
    slots_ref,
    group,
    store,
    index_sems,
    sems,
):
    stored = down_ref.shape[0]
    indices = index_copies(group_ref, store_ref, group, store, index_sems)

    rows, local, width = key_ref.shape
    heads = queries_ref.shape[1] // width
    grouped = heads // local
    positions = keys_ref.shape[1]
    scale = width ** (-0.5)
    queries = [queries_ref[:, h * width : (h + 1) * width].astype(F32) for h in range(heads)]
    queries = jnp.swapaxes(jnp.stack(queries), 0, 1)
    row_head = lax.broadcasted_iota(jnp.int32, (heads, positions), 0) // grouped
    place_head = lax.broadcasted_iota(jnp.int32, (heads, positions), 1) % local
    same = row_head == place_head

    def spread(ref, r):
        fresh = ref[r].astype(F32)
        parts = [jnp.broadcast_to(fresh[k : k + 1], (grouped, width)) for k in range(local)]
        return jnp.concatenate(parts, axis=0)

    weights, fresh_weights, denominators = [], [], []
    for r in range(rows):
        query = queries[r]
        scores = lax.dot_general(
            query.astype(BF16), keys_ref[r], (((1,), (1,)), ((), ())), preferred_element_type=F32
        )
        scores = jnp.where(same, scores * scale, -jnp.inf)
        fresh_score = jnp.sum(query * spread(key_ref, r), axis=1, keepdims=True) * scale
        overall = jnp.maximum(jnp.max(scores, axis=1, keepdims=True), fresh_score)
        weight = jnp.exp(scores - overall)
        fresh_weight = jnp.exp(fresh_score - overall)
        denominators.append(jnp.sum(weight, axis=1, keepdims=True) + fresh_weight)
        weights.append(weight.astype(BF16))
        fresh_weights.append(fresh_weight)
    for copy in indices:
        copy.wait()
    copies = []
    for s in range(slots_ref.shape[0]):
        spot, _ = slot_position(s, group, store, stored)
        copies.append(pltpu.make_async_copy(down_ref.at[spot], slots_ref.at[s], sems.at[s]))
        copies[s].start()
    mixed = []
    for r in range(rows):
        total = jnp.dot(weights[r], values_ref[r], preferred_element_type=F32)
        total = total + fresh_weights[r] * spread(value_ref, r)
        mixed.append(total / denominators[r])
    mixed = jnp.swapaxes(jnp.stack(mixed), 0, 1)

    half = width // 2
    low = lax.broadcasted_iota(jnp.int32, (rows, width), 1) < half
    for g in range(grouped):
        one, two = mixed[g], mixed[grouped + g]
        pair = (
            jnp.where(low, one, pltpu.roll(two, half, 1)),
            jnp.where(low, pltpu.roll(one, half, 1), two),
        )
        for i, part in enumerate(pair):
            part = part.astype(BF16)
            for o in range(out_ref.shape[0]):
                out_ref[o, 2 * g + i] = part
    for copy in copies:
        copy.wait()


def project_kernel(
    group_ref,
    store_ref,
    rows_ref,
    att_ref,
    w_ref,
    before_ref,
    after_ref,
    slots_ref,
    keep_ref,
    send_ref,
    acc,
    group,
    store,
    index_sems,
):
    indices = index_copies(group_ref, store_ref, group, store, index_sems)
    slots, _, _, rank = slots_ref.shape
    stored = store_ref.shape[1] // lax.axis_size("owner")
    owners, rows, feats = att_ref.shape
    owner = lax.axis_index("owner")
    mine = att_ref[owner]
    beside = jnp.concatenate(
        [att_ref[lax.rem(owner + owners - 1, owners)], att_ref[lax.rem(owner + 1, owners)]], axis=1
    )
    first = lax.rem(lax.axis_index("tensor"), 2) == 0
    block = keep_ref.shape[1]
    planes = before_ref.shape[1] // (2 * block)

    across = lax.rem(owner + 2, owners)

    def columns(z, target):
        at = [pl.multiple_of(((2 * z + c) * owners + target) * block, block) for c in range(2)]
        return jnp.concatenate([w_ref[:, pl.ds(a, block)] for a in at], axis=1)

    for z in range(planes):
        span = pl.ds(z * 2 * block, 2 * block)
        near_rows = jnp.concatenate([before_ref[:, span], after_ref[:, span]], axis=0)
        here = jnp.dot(beside, near_rows, preferred_element_type=F32)
        here = here + jnp.dot(mine, columns(z, owner), preferred_element_type=F32)
        there = jnp.dot(mine, columns(z, across), preferred_element_type=F32)
        for i, part in enumerate((here, there)):
            even, odd = part[:, :block], part[:, block:]
            rows_span = pl.ds((2 * z + i) * rows, rows)
            keep_ref[rows_span, :] = jnp.where(first, even, odd)
            send_ref[rows_span, :] = jnp.where(first, odd, even).astype(BF16)
    att = jnp.concatenate([att_ref[o] for o in range(owners)], axis=1)
    ids = row_adapters(rows_ref, rank)
    acc[...] = jnp.zeros_like(acc)
    for copy in indices:
        copy.wait()
    for s in range(slots):
        _, here = slot_position(s, group, store, stored)

        @pl.when(here)
        def _(s=s):
            table = slots_ref[s].reshape(owners * feats, rank)
            code = jnp.dot(att, table, preferred_element_type=F32)
            acc[...] += jnp.where(ids == group[0, s], code, 0.0)

    half = rows // 2
    code = jnp.concatenate([acc[:half, :], acc[half:, :]], axis=1)
    keep_ref[2 * planes * rows :, :] = code
    send_ref[2 * planes * rows :, :] = code.astype(BF16)


def pair_kernel(keep_ref, got_ref, own_ref, across_ref, codes_ref):
    planes, rows, _ = own_ref.shape
    for z in range(planes):
        span = pl.ds(2 * z * rows, rows)
        own_ref[z] = keep_ref[span, :] + got_ref[span, :].astype(F32)
        span = pl.ds((2 * z + 1) * rows, rows)
        across_ref[z] = (keep_ref[span, :] + got_ref[span, :].astype(F32)).astype(BF16)
    span = pl.ds(2 * planes * rows, codes_ref.shape[1])
    code = (keep_ref[span, :] + got_ref[span, :].astype(F32)).astype(BF16)
    for z in range(planes):
        codes_ref[z] = code


def add_kernel(one_ref, two_ref, out_ref):
    out_ref[...] = (one_ref[...] + two_ref[...].astype(F32)).astype(BF16)


def update_kernel(group_ref, store_ref, rows_ref, codes_ref, up_ref, own_ref, *rest):
    send_refs, (acc, group, store, index_sems) = rest[:-4], rest[-4:]
    indices = index_copies(group_ref, store_ref, group, store, index_sems)
    slots = group.shape[1]
    stored, rank, _ = up_ref.shape
    rows, block = own_ref.shape
    owners = lax.axis_size("owner")
    owner = lax.axis_index("owner")
    packed = codes_ref[0].astype(F32)
    for z in range(1, codes_ref.shape[0]):
        packed = packed + codes_ref[z].astype(F32)
    code = jnp.concatenate([packed[:, :rank], packed[:, rank:]], axis=0).astype(BF16).astype(F32)
    ids = row_adapters(rows_ref, rank)
    acc[...] = jnp.zeros_like(acc)
    for copy in indices:
        copy.wait()
    for s in range(slots):
        spot, here = slot_position(s, group, store, stored)

        @pl.when(here)
        def _(s=s, spot=spot):
            chosen = jnp.where(ids == group[0, s], code, 0.0).astype(BF16)
            acc[...] += jnp.dot(chosen, up_ref[spot], preferred_element_type=F32)

    def columns(target):
        return acc[:, pl.ds(pl.multiple_of(target * block, block), block)]

    own_ref[...] = columns(owner)
    for i, send_ref in enumerate(send_refs):
        send_ref[...] = columns(lax.rem(owner + i + 1, owners)).astype(BF16)


def final_kernel(parts_ref, own_ref, *rest):
    got_refs, out_ref = rest[:-1], rest[-1]
    base = parts_ref[0].astype(F32)
    for z in range(1, parts_ref.shape[0]):
        base = base + parts_ref[z].astype(F32)
    update = own_ref[...]
    for got_ref in got_refs:
        update = update + got_ref[...].astype(F32)
    out_ref[...] = (base + ADAPTER_SCALE * update).astype(BF16)


def shards(
    queries,
    cached_key_rows,
    cached_value_rows,
    newest_key,
    newest_value,
    output_weight,
    adapter_down_weight,
    adapter_up_weight,
    adapter_store_row,
    adapters_by_group,
    adapter_per_row,
):
    owners = lax.axis_size("owner")
    tensors = lax.axis_size("tensor")
    planes = tensors // 2
    slots = adapters_by_group.shape[1]
    row_count, local_heads, head_width = newest_key.shape
    rows = adapter_per_row.shape[0]
    feats = local_heads * output_weight.shape[1]
    columns = output_weight.shape[2]
    block = columns // (tensors * owners)
    rank = adapter_down_weight.shape[-1]
    row_ids = adapter_per_row.reshape(1, rows)
    group, store = far(adapters_by_group), far(adapter_store_row.reshape(1, -1))
    indices = [
        pltpu.SMEM(group.shape, jnp.int32),
        pltpu.SMEM(store.shape, jnp.int32),
        pltpu.SemaphoreType.DMA((2,)),
    ]

    slab = pltpu.VMEM((feats, columns // owners), BF16)
    positions = cached_value_rows.shape[1] * local_heads
    weight, local_queries, values, right, left = pl.pallas_call(
        slab_kernel,
        name="slabs",
        out_shape=(
            pltpu.VMEM((feats, columns), BF16),
            pltpu.VMEM(queries.shape, BF16),
            pltpu.VMEM((row_count, positions, head_width), BF16),
            slab,
            slab,
        ),
        in_specs=[HBM, HBM, HBM],
        out_specs=(VMEM,) * 5,
        scratch_shapes=[
            pltpu.SemaphoreType.DMA((feats // 16 + 1,)),
            pltpu.SemaphoreType.DMA((row_count,)),
        ],
        compiler_params=LIMIT,
    )(
        far(output_weight.reshape(feats, columns)),
        far(queries),
        far(cached_value_rows.reshape(row_count, positions, head_width)),
    )
    before = lax.ppermute(right, "owner", [(o, (o + 1) % owners) for o in range(owners)])
    after = lax.ppermute(left, "owner", [(o, (o - 1) % owners) for o in range(owners)])

    outgoing, tables = pl.pallas_call(
        attend_kernel,
        name="attend",
        out_shape=(
            pltpu.VMEM((owners, tensors, row_count, feats), BF16),
            pltpu.VMEM((slots,) + adapter_down_weight.shape[1:], BF16),
        ),
        in_specs=[HBM, HBM] + [VMEM] * 5 + [HBM],
        out_specs=(VMEM, VMEM),
        scratch_shapes=indices + [pltpu.SemaphoreType.DMA((slots,))],
        compiler_params=LIMIT,
    )(
        group,
        store,
        near(local_queries),
        near(cached_key_rows.reshape(row_count, -1, head_width)),
        near(values),
        newest_key,
        newest_value,
        far(adapter_down_weight),
    )
    outgoing = outgoing.reshape(owners * tensors, row_count, feats)
    attention = lax.all_to_all(
        outgoing, ("owner", "tensor"), split_axis=0, concat_axis=0, tiled=True
    )
    attention = attention.reshape(owners, rows, feats)

    tall = 2 * planes * rows + rows // 2
    keep, send = pl.pallas_call(
        project_kernel,
        name="project",
        out_shape=(pltpu.VMEM((tall, block), F32), pltpu.VMEM((tall, block), BF16)),
        in_specs=[HBM, HBM] + [VMEM] * 6,
        out_specs=(VMEM, VMEM),
        scratch_shapes=[pltpu.VMEM((rows, rank), F32)] + indices,
        compiler_params=LIMIT,
    )(
        group,
        store,
        row_ids,
        near(attention),
        near(weight),
        near(before),
        near(after),
        near(tables),
    )
    got = lax.ppermute(send, "tensor", [(t, t ^ 1) for t in range(tensors)])
    own_part, across, codes = pl.pallas_call(
        pair_kernel,
        name="pair",
        out_shape=(
            pltpu.VMEM((planes, rows, block), F32),
            pltpu.VMEM((planes, rows, block), BF16),
            pltpu.VMEM((planes, rows // 2, 2 * rank), BF16),
        ),
        in_specs=[VMEM, VMEM],
        out_specs=(VMEM, VMEM, VMEM),
        compiler_params=LIMIT,
    )(near(keep), near(got))
    groups = [[2 * z + c for z in range(planes)] for c in range(2)]

    def over_z(pieces):
        return lax.all_to_all(
            pieces, "tensor", split_axis=0, concat_axis=0, tiled=True, axis_index_groups=groups
        )

    across = lax.ppermute(across, "owner", [(o, (o + 2) % owners) for o in range(owners)])
    codes = over_z(codes)
    strip = pltpu.VMEM((rows, block), BF16)
    own_update, *updates = pl.pallas_call(
        update_kernel,
        name="update",
        out_shape=(pltpu.VMEM((rows, block), F32),) + (strip,) * (owners - 1),
        in_specs=[HBM, HBM] + [VMEM] * 3,
        out_specs=(VMEM,) * owners,
        scratch_shapes=[pltpu.VMEM((rows, owners * block), F32)] + indices,
        compiler_params=LIMIT,
    )(group, store, row_ids, near(codes), near(adapter_up_weight))
    updates = [
        lax.ppermute(update, "owner", [(o, (o + i + 1) % owners) for o in range(owners)])
        for i, update in enumerate(updates)
    ]
    parts = over_z(
        pl.pallas_call(
            add_kernel,
            name="add",
            out_shape=pltpu.VMEM((planes, rows, block), BF16),
            in_specs=[VMEM, VMEM],
            out_specs=VMEM,
            compiler_params=LIMIT,
        )(near(own_part), near(across))
    )
    return pl.pallas_call(
        final_kernel,
        name="final",
        out_shape=jax.ShapeDtypeStruct((rows, block), BF16),
        in_specs=[VMEM] * (owners + 1),
        out_specs=VMEM,
        compiler_params=LIMIT,
    )(near(parts), near(own_update), *[near(update) for update in updates])


def solution(mesh):
    return jax.shard_map(
        shards,
        mesh=mesh,
        in_specs=(
            P(("dp", "tensor"), "owner"),
            P(("dp", "tensor"), None, "owner", None),
            P(("dp", "tensor"), None, "owner", None),
            P(("dp", "tensor"), "owner", None),
            P(("dp", "tensor"), "owner", None),
            P("owner", "tensor", None),
            P("owner", None, "tensor", None),
            P("owner", None, "tensor"),
            P(),
            P("dp", None),
            P("dp"),
        ),
        out_specs=P("dp", ("tensor", "owner")),
        check_vma=False,
    )
```

```python
import jax
import jax.numpy as jnp
from jax import lax
from jax.experimental import pallas as pl
from jax.experimental.pallas import tpu as pltpu
from jax.sharding import PartitionSpec as P

ADAPTER_SCALE = 2.0
BF16 = jnp.bfloat16
F32 = jnp.float32

VMEM = pl.BlockSpec(memory_space=pltpu.VMEM)
HBM = pl.BlockSpec(memory_space=pltpu.HBM)
LIMIT = pltpu.CompilerParams(vmem_limit_bytes=16 * 1024 * 1024)


def near(array):
    return pltpu.with_memory_space_constraint(array, pltpu.VMEM)


def far(array):
    return pltpu.with_memory_space_constraint(array, pltpu.HBM)


def slot_position(slot, group_ref, store_ref, stored):
    spot = store_ref[0, group_ref[0, slot]] - lax.axis_index("owner") * stored
    here = jnp.logical_and(spot >= 0, spot < stored)
    return jnp.clip(spot, 0, stored - 1), here


def index_copies(group_ref, store_ref, group, store, sems):
    copies = (
        pltpu.make_async_copy(group_ref, group, sems.at[0]),
        pltpu.make_async_copy(store_ref, store, sems.at[1]),
    )
    for copy in copies:
        copy.start()
    return copies


def row_adapters(rows_ref, width):
    rows = rows_ref.shape[1]
    return jnp.transpose(jnp.broadcast_to(rows_ref[...], (rows, rows)))[:, :width]


def slab_kernel(
    w_hbm_ref,
    queries_hbm_ref,
    values_hbm_ref,
    w_ref,
    queries_ref,
    values_ref,
    right_ref,
    left_ref,
    sems,
    value_sems,
):
    chunks = sems.shape[0] - 1
    step = w_ref.shape[0] // chunks
    copies = [
        pltpu.make_async_copy(
            w_hbm_ref.at[pl.ds(i * step, step)], w_ref.at[pl.ds(i * step, step)], sems.at[i]
        )
        for i in range(chunks)
    ]
    rest = [pltpu.make_async_copy(queries_hbm_ref, queries_ref, sems.at[chunks])]
    rest += [
        pltpu.make_async_copy(values_hbm_ref.at[r], values_ref.at[r], value_sems.at[r])
        for r in range(values_ref.shape[0])
    ]
    for copy in copies + rest:
        copy.start()
    owner, owners = lax.axis_index("owner"), lax.axis_size("owner")
    targets = [lax.rem(owner + 1, owners), lax.rem(owner + owners - 1, owners)]
    for i in range(chunks):
        copies[i].wait()
        rows = pl.ds(i * step, step)
        for out_ref, target in zip((right_ref, left_ref), targets):
            for block in range(out_ref.shape[1] // 128):
                at = pl.multiple_of((block * owners + target) * 128, 128)
                out_ref[rows, block * 128 : (block + 1) * 128] = w_ref[rows, pl.ds(at, 128)]
    for copy in rest:
        copy.wait()


def attend_kernel(queries_ref, keys_ref, values_ref, key_ref, value_ref, out_ref):
    rows, local, width = key_ref.shape
    heads = queries_ref.shape[1] // width
    grouped = heads // local
    positions = keys_ref.shape[1]
    scale = width ** (-0.5)
    queries = [queries_ref[:, h * width : (h + 1) * width].astype(F32) for h in range(heads)]
    queries = jnp.swapaxes(jnp.stack(queries), 0, 1)
    row_head = lax.broadcasted_iota(jnp.int32, (heads, positions), 0) // grouped
    place_head = lax.broadcasted_iota(jnp.int32, (heads, positions), 1) % local
    same = row_head == place_head

    def spread(ref, r):
        fresh = ref[r].astype(F32)
        parts = [jnp.broadcast_to(fresh[k : k + 1], (grouped, width)) for k in range(local)]
        return jnp.concatenate(parts, axis=0)

    weights, fresh_weights, denominators = [], [], []
    for r in range(rows):
        query = queries[r]
        scores = lax.dot_general(
            query.astype(BF16), keys_ref[r], (((1,), (1,)), ((), ())), preferred_element_type=F32
        )
        scores = jnp.where(same, scores * scale, -jnp.inf)
        fresh_score = jnp.sum(query * spread(key_ref, r), axis=1, keepdims=True) * scale
        overall = jnp.maximum(jnp.max(scores, axis=1, keepdims=True), fresh_score)
        weight = jnp.exp(scores - overall)
        fresh_weight = jnp.exp(fresh_score - overall)
        denominators.append(jnp.sum(weight, axis=1, keepdims=True) + fresh_weight)
        weights.append(weight.astype(BF16))
        fresh_weights.append(fresh_weight)
    mixed = []
    for r in range(rows):
        total = jnp.dot(weights[r], values_ref[r], preferred_element_type=F32)
        total = total + fresh_weights[r] * spread(value_ref, r)
        mixed.append(total / denominators[r])
    mixed = jnp.swapaxes(jnp.stack(mixed), 0, 1)

    half = width // 2
    low = lax.broadcasted_iota(jnp.int32, (rows, width), 1) < half
    for g in range(grouped):
        one, two = mixed[g], mixed[grouped + g]
        pair = (
            jnp.where(low, one, pltpu.roll(two, half, 1)),
            jnp.where(low, pltpu.roll(one, half, 1), two),
        )
        for i, part in enumerate(pair):
            part = part.astype(BF16)
            for o in range(out_ref.shape[0]):
                out_ref[o, 2 * g + i] = part


def project_kernel(
    group_ref,
    store_ref,
    rows_ref,
    att_ref,
    w_ref,
    before_ref,
    after_ref,
    down_ref,
    keep_ref,
    send_ref,
    acc,
    group,
    store,
    index_sems,
):
    indices = index_copies(group_ref, store_ref, group, store, index_sems)
    slots = group.shape[1]
    stored, _, _, rank = down_ref.shape
    owners, rows, feats = att_ref.shape
    owner = lax.axis_index("owner")
    mine = att_ref[owner]
    beside = jnp.concatenate(
        [att_ref[lax.rem(owner + owners - 1, owners)], att_ref[lax.rem(owner + 1, owners)]], axis=1
    )
    first = lax.rem(lax.axis_index("tensor"), 2) == 0
    block = keep_ref.shape[1]
    planes = before_ref.shape[1] // (2 * block)

    across = lax.rem(owner + 2, owners)

    def columns(z, target):
        at = [pl.multiple_of(((2 * z + c) * owners + target) * block, block) for c in range(2)]
        return jnp.concatenate([w_ref[:, pl.ds(a, block)] for a in at], axis=1)

    for z in range(planes):
        span = pl.ds(z * 2 * block, 2 * block)
        near_rows = jnp.concatenate([before_ref[:, span], after_ref[:, span]], axis=0)
        here = jnp.dot(beside, near_rows, preferred_element_type=F32)
        here = here + jnp.dot(mine, columns(z, owner), preferred_element_type=F32)
        there = jnp.dot(mine, columns(z, across), preferred_element_type=F32)
        for i, part in enumerate((here, there)):
            even, odd = part[:, :block], part[:, block:]
            rows_span = pl.ds((2 * z + i) * rows, rows)
            keep_ref[rows_span, :] = jnp.where(first, even, odd)
            send_ref[rows_span, :] = jnp.where(first, odd, even).astype(BF16)
    att = jnp.concatenate([att_ref[o] for o in range(owners)], axis=1)
    ids = row_adapters(rows_ref, rank)
    acc[...] = jnp.zeros_like(acc)
    for copy in indices:
        copy.wait()
    for s in range(slots):
        spot, here = slot_position(s, group, store, stored)

        @pl.when(here)
        def _(s=s, spot=spot):
            table = down_ref[spot].reshape(owners * feats, rank)
            code = jnp.dot(att, table, preferred_element_type=F32)
            acc[...] += jnp.where(ids == group[0, s], code, 0.0)

    half = rows // 2
    code = jnp.concatenate([acc[:half, :], acc[half:, :]], axis=1)
    keep_ref[2 * planes * rows :, :] = code
    send_ref[2 * planes * rows :, :] = code.astype(BF16)


def pair_kernel(keep_ref, got_ref, own_ref, across_ref, codes_ref):
    planes, rows, _ = own_ref.shape
    for z in range(planes):
        span = pl.ds(2 * z * rows, rows)
        own_ref[z] = keep_ref[span, :] + got_ref[span, :].astype(F32)
        span = pl.ds((2 * z + 1) * rows, rows)
        across_ref[z] = (keep_ref[span, :] + got_ref[span, :].astype(F32)).astype(BF16)
    span = pl.ds(2 * planes * rows, codes_ref.shape[1])
    code = (keep_ref[span, :] + got_ref[span, :].astype(F32)).astype(BF16)
    for z in range(planes):
        codes_ref[z] = code


def add_kernel(one_ref, two_ref, out_ref):
    out_ref[...] = (one_ref[...] + two_ref[...].astype(F32)).astype(BF16)


def update_kernel(group_ref, store_ref, rows_ref, codes_ref, up_ref, own_ref, *rest):
    send_refs, (acc, group, store, index_sems) = rest[:-4], rest[-4:]
    indices = index_copies(group_ref, store_ref, group, store, index_sems)
    slots = group.shape[1]
    stored, rank, _ = up_ref.shape
    rows, block = own_ref.shape
    owners = lax.axis_size("owner")
    owner = lax.axis_index("owner")
    packed = codes_ref[0].astype(F32)
    for z in range(1, codes_ref.shape[0]):
        packed = packed + codes_ref[z].astype(F32)
    code = jnp.concatenate([packed[:, :rank], packed[:, rank:]], axis=0).astype(BF16).astype(F32)
    ids = row_adapters(rows_ref, rank)
    acc[...] = jnp.zeros_like(acc)
    for copy in indices:
        copy.wait()
    for s in range(slots):
        spot, here = slot_position(s, group, store, stored)

        @pl.when(here)
        def _(s=s, spot=spot):
            chosen = jnp.where(ids == group[0, s], code, 0.0).astype(BF16)
            acc[...] += jnp.dot(chosen, up_ref[spot], preferred_element_type=F32)

    def columns(target):
        return acc[:, pl.ds(pl.multiple_of(target * block, block), block)]

    own_ref[...] = columns(owner)
    for i, send_ref in enumerate(send_refs):
        send_ref[...] = columns(lax.rem(owner + i + 1, owners)).astype(BF16)


def final_kernel(parts_ref, own_ref, *rest):
    got_refs, out_ref = rest[:-1], rest[-1]
    base = parts_ref[0].astype(F32)
    for z in range(1, parts_ref.shape[0]):
        base = base + parts_ref[z].astype(F32)
    update = own_ref[...]
    for got_ref in got_refs:
        update = update + got_ref[...].astype(F32)
    out_ref[...] = (base + ADAPTER_SCALE * update).astype(BF16)


def shards(
    queries,
    cached_key_rows,
    cached_value_rows,
    newest_key,
    newest_value,
    output_weight,
    adapter_down_weight,
    adapter_up_weight,
    adapter_store_row,
    adapters_by_group,
    adapter_per_row,
):
    owners = lax.axis_size("owner")
    tensors = lax.axis_size("tensor")
    planes = tensors // 2
    slots = adapters_by_group.shape[1]
    row_count, local_heads, head_width = newest_key.shape
    rows = adapter_per_row.shape[0]
    feats = local_heads * output_weight.shape[1]
    columns = output_weight.shape[2]
    block = columns // (tensors * owners)
    rank = adapter_down_weight.shape[-1]
    row_ids = adapter_per_row.reshape(1, rows)
    group, store = far(adapters_by_group), far(adapter_store_row.reshape(1, -1))
    indices = [
        pltpu.SMEM(group.shape, jnp.int32),
        pltpu.SMEM(store.shape, jnp.int32),
        pltpu.SemaphoreType.DMA((2,)),
    ]

    slab = pltpu.VMEM((feats, columns // owners), BF16)
    positions = cached_value_rows.shape[1] * local_heads
    weight, local_queries, values, right, left = pl.pallas_call(
        slab_kernel,
        name="slabs",
        out_shape=(
            pltpu.VMEM((feats, columns), BF16),
            pltpu.VMEM(queries.shape, BF16),
            pltpu.VMEM((row_count, positions, head_width), BF16),
            slab,
            slab,
        ),
        in_specs=[HBM, HBM, HBM],
        out_specs=(VMEM,) * 5,
        scratch_shapes=[
            pltpu.SemaphoreType.DMA((feats // 16 + 1,)),
            pltpu.SemaphoreType.DMA((row_count,)),
        ],
        compiler_params=LIMIT,
    )(
        far(output_weight.reshape(feats, columns)),
        far(queries),
        far(cached_value_rows.reshape(row_count, positions, head_width)),
    )
    before = lax.ppermute(right, "owner", [(o, (o + 1) % owners) for o in range(owners)])
    after = lax.ppermute(left, "owner", [(o, (o - 1) % owners) for o in range(owners)])

    outgoing = pl.pallas_call(
        attend_kernel,
        name="attend",
        out_shape=pltpu.VMEM((owners, tensors, row_count, feats), BF16),
        in_specs=[VMEM] * 5,
        out_specs=VMEM,
        compiler_params=LIMIT,
    )(
        near(local_queries),
        near(cached_key_rows.reshape(row_count, positions, head_width)),
        near(values),
        newest_key,
        newest_value,
    )
    outgoing = outgoing.reshape(owners * tensors, row_count, feats)
    attention = lax.all_to_all(
        outgoing, ("owner", "tensor"), split_axis=0, concat_axis=0, tiled=True
    )
    attention = attention.reshape(owners, rows, feats)

    tall = 2 * planes * rows + rows // 2
    keep, send = pl.pallas_call(
        project_kernel,
        name="project",
        out_shape=(pltpu.VMEM((tall, block), F32), pltpu.VMEM((tall, block), BF16)),
        in_specs=[HBM, HBM] + [VMEM] * 6,
        out_specs=(VMEM, VMEM),
        scratch_shapes=[pltpu.VMEM((rows, rank), F32)] + indices,
        compiler_params=LIMIT,
    )(
        group,
        store,
        row_ids,
        near(attention),
        near(weight),
        near(before),
        near(after),
        near(adapter_down_weight),
    )
    got = lax.ppermute(send, "tensor", [(t, t ^ 1) for t in range(tensors)])
    own_part, across, codes = pl.pallas_call(
        pair_kernel,
        name="pair",
        out_shape=(
            pltpu.VMEM((planes, rows, block), F32),
            pltpu.VMEM((planes, rows, block), BF16),
            pltpu.VMEM((planes, rows // 2, 2 * rank), BF16),
        ),
        in_specs=[VMEM, VMEM],
        out_specs=(VMEM, VMEM, VMEM),
        compiler_params=LIMIT,
    )(near(keep), near(got))
    groups = [[2 * z + c for z in range(planes)] for c in range(2)]

    def over_z(pieces):
        return lax.all_to_all(
            pieces, "tensor", split_axis=0, concat_axis=0, tiled=True, axis_index_groups=groups
        )

    across = lax.ppermute(across, "owner", [(o, (o + 2) % owners) for o in range(owners)])
    codes = over_z(codes)
    strip = pltpu.VMEM((rows, block), BF16)
    own_update, *updates = pl.pallas_call(
        update_kernel,
        name="update",
        out_shape=(pltpu.VMEM((rows, block), F32),) + (strip,) * (owners - 1),
        in_specs=[HBM, HBM] + [VMEM] * 3,
        out_specs=(VMEM,) * owners,
        scratch_shapes=[pltpu.VMEM((rows, owners * block), F32)] + indices,
        compiler_params=LIMIT,
    )(group, store, row_ids, near(codes), near(adapter_up_weight))
    updates = [
        lax.ppermute(update, "owner", [(o, (o + i + 1) % owners) for o in range(owners)])
        for i, update in enumerate(updates)
    ]
    parts = over_z(
        pl.pallas_call(
            add_kernel,
            name="add",
            out_shape=pltpu.VMEM((planes, rows, block), BF16),
            in_specs=[VMEM, VMEM],
            out_specs=VMEM,
            compiler_params=LIMIT,
        )(near(own_part), near(across))
    )
    return pl.pallas_call(
        final_kernel,
        name="final",
        out_shape=jax.ShapeDtypeStruct((rows, block), BF16),
        in_specs=[VMEM] * (owners + 1),
        out_specs=VMEM,
        compiler_params=LIMIT,
    )(near(parts), near(own_update), *[near(update) for update in updates])


def solution(mesh):
    return jax.shard_map(
        shards,
        mesh=mesh,
        in_specs=(
            P(("dp", "tensor"), "owner"),
            P(("dp", "tensor"), None, "owner", None),
            P(("dp", "tensor"), None, "owner", None),
            P(("dp", "tensor"), "owner", None),
            P(("dp", "tensor"), "owner", None),
            P("owner", "tensor", None),
            P("owner", None, "tensor", None),
            P("owner", None, "tensor"),
            P(),
            P("dp", None),
            P("dp"),
        ),
        out_specs=P("dp", ("tensor", "owner")),
        check_vma=False,
    )
```

```python
import jax
import jax.numpy as jnp
from jax import lax
from jax.experimental import pallas as pl
from jax.experimental.pallas import tpu as pltpu
from jax.sharding import PartitionSpec as P

ADAPTER_SCALE = 2.0
BF16 = jnp.bfloat16
F32 = jnp.float32

VMEM = pl.BlockSpec(memory_space=pltpu.VMEM)
HBM = pl.BlockSpec(memory_space=pltpu.HBM)
LIMIT = pltpu.CompilerParams(vmem_limit_bytes=16 * 1024 * 1024)


def near(array):
    return pltpu.with_memory_space_constraint(array, pltpu.VMEM)


def far(array):
    return pltpu.with_memory_space_constraint(array, pltpu.HBM)


def slot_position(slot, group_ref, store_ref, stored):
    spot = store_ref[0, group_ref[0, slot]] - lax.axis_index("owner") * stored
    here = jnp.logical_and(spot >= 0, spot < stored)
    return jnp.clip(spot, 0, stored - 1), here


def index_copies(group_ref, store_ref, group, store, sems):
    copies = (
        pltpu.make_async_copy(group_ref, group, sems.at[0]),
        pltpu.make_async_copy(store_ref, store, sems.at[1]),
    )
    for copy in copies:
        copy.start()
    return copies


def row_adapters(rows_ref, width):
    rows = rows_ref.shape[1]
    return jnp.transpose(jnp.broadcast_to(rows_ref[...], (rows, rows)))[:, :width]


def slab_kernel(
    w_hbm_ref,
    queries_hbm_ref,
    values_hbm_ref,
    w_ref,
    queries_ref,
    values_ref,
    right_ref,
    left_ref,
    sems,
    value_sems,
):
    chunks = sems.shape[0] - 1
    step = w_ref.shape[0] // chunks
    copies = [
        pltpu.make_async_copy(
            w_hbm_ref.at[pl.ds(i * step, step)], w_ref.at[pl.ds(i * step, step)], sems.at[i]
        )
        for i in range(chunks)
    ]
    rest = [pltpu.make_async_copy(queries_hbm_ref, queries_ref, sems.at[chunks])]
    rest += [
        pltpu.make_async_copy(values_hbm_ref.at[r], values_ref.at[r], value_sems.at[r])
        for r in range(values_ref.shape[0])
    ]
    for copy in copies + rest:
        copy.start()
    owner, owners = lax.axis_index("owner"), lax.axis_size("owner")
    targets = [lax.rem(owner + 1, owners), lax.rem(owner + owners - 1, owners)]
    for i in range(chunks):
        copies[i].wait()
        rows = pl.ds(i * step, step)
        for out_ref, target in zip((right_ref, left_ref), targets):
            for block in range(out_ref.shape[1] // 128):
                at = pl.multiple_of((block * owners + target) * 128, 128)
                out_ref[rows, block * 128 : (block + 1) * 128] = w_ref[rows, pl.ds(at, 128)]
    for copy in rest:
        copy.wait()


def attend_kernel(queries_ref, keys_ref, values_ref, key_ref, value_ref, out_ref):
    rows, local, width = key_ref.shape
    heads = queries_ref.shape[1] // width
    grouped = heads // local
    positions = keys_ref.shape[1]
    scale = width ** (-0.5)
    queries = [queries_ref[:, h * width : (h + 1) * width].astype(F32) for h in range(heads)]
    queries = jnp.swapaxes(jnp.stack(queries), 0, 1)
    row_head = lax.broadcasted_iota(jnp.int32, (heads, positions), 0) // grouped
    place_head = lax.broadcasted_iota(jnp.int32, (heads, positions), 1) % local
    same = row_head == place_head

    def spread(ref, r):
        fresh = ref[r].astype(F32)
        parts = [jnp.broadcast_to(fresh[k : k + 1], (grouped, width)) for k in range(local)]
        return jnp.concatenate(parts, axis=0)

    weights, fresh_weights, denominators = [], [], []
    for r in range(rows):
        query = queries[r]
        scores = lax.dot_general(
            query.astype(BF16), keys_ref[r], (((1,), (1,)), ((), ())), preferred_element_type=F32
        )
        scores = jnp.where(same, scores * scale, -jnp.inf)
        fresh_score = jnp.sum(query * spread(key_ref, r), axis=1, keepdims=True) * scale
        overall = jnp.maximum(jnp.max(scores, axis=1, keepdims=True), fresh_score)
        weight = jnp.exp(scores - overall)
        fresh_weight = jnp.exp(fresh_score - overall)
        denominators.append(jnp.sum(weight, axis=1, keepdims=True) + fresh_weight)
        weights.append(weight.astype(BF16))
        fresh_weights.append(fresh_weight)
    mixed = []
    for r in range(rows):
        total = jnp.dot(weights[r], values_ref[r], preferred_element_type=F32)
        total = total + fresh_weights[r] * spread(value_ref, r)
        mixed.append(total / denominators[r])
    mixed = jnp.swapaxes(jnp.stack(mixed), 0, 1)

    half = width // 2
    low = lax.broadcasted_iota(jnp.int32, (rows, width), 1) < half
    for g in range(grouped):
        one, two = mixed[g], mixed[grouped + g]
        pair = (
            jnp.where(low, one, pltpu.roll(two, half, 1)),
            jnp.where(low, pltpu.roll(one, half, 1), two),
        )
        for i, part in enumerate(pair):
            part = part.astype(BF16)
            for o in range(out_ref.shape[0]):
                out_ref[o, 2 * g + i] = part


def project_kernel(
    order_ref,
    att_ref,
    w_ref,
    before_ref,
    after_ref,
    own_ref,
    send_own_ref,
    across_ref,
    send_across_ref,
):
    del order_ref
    owners, rows, _ = att_ref.shape
    owner = lax.axis_index("owner")
    mine = att_ref[owner]
    beside = jnp.concatenate(
        [att_ref[lax.rem(owner + owners - 1, owners)], att_ref[lax.rem(owner + 1, owners)]], axis=1
    )
    first = lax.rem(lax.axis_index("tensor"), 2) == 0
    planes, _, block = own_ref.shape
    opposite = lax.rem(owner + 2, owners)

    def columns(z, target):
        at = [pl.multiple_of(((2 * z + c) * owners + target) * block, block) for c in range(2)]
        return jnp.concatenate([w_ref[:, pl.ds(a, block)] for a in at], axis=1)

    for z in range(planes):
        span = pl.ds(z * 2 * block, 2 * block)
        near_rows = jnp.concatenate([before_ref[:, span], after_ref[:, span]], axis=0)
        here = jnp.dot(beside, near_rows, preferred_element_type=F32)
        here = here + jnp.dot(mine, columns(z, owner), preferred_element_type=F32)
        there = jnp.dot(mine, columns(z, opposite), preferred_element_type=F32)
        for part, keep, send in (
            (here, own_ref, send_own_ref),
            (there, across_ref, send_across_ref),
        ):
            even, odd = part[:, :block], part[:, block:]
            keep[z] = jnp.where(first, even, odd)
            send[z] = jnp.where(first, odd, even).astype(BF16)


def rank_kernel(
    group_ref,
    store_ref,
    rows_ref,
    order_ref,
    att_ref,
    down_ref,
    codes_ref,
    acc,
    group,
    store,
    index_sems,
):
    del order_ref
    indices = index_copies(group_ref, store_ref, group, store, index_sems)
    slots = group.shape[1]
    stored, _, _, rank = down_ref.shape
    owners, rows, feats = att_ref.shape
    att = jnp.concatenate([att_ref[o] for o in range(owners)], axis=1)
    ids = row_adapters(rows_ref, rank)
    acc[...] = jnp.zeros_like(acc)
    for copy in indices:
        copy.wait()
    for s in range(slots):
        spot, here = slot_position(s, group, store, stored)

        @pl.when(here)
        def _(s=s, spot=spot):
            table = down_ref[spot].reshape(owners * feats, rank)
            code = jnp.dot(att, table, preferred_element_type=F32)
            acc[...] += jnp.where(ids == group[0, s], code, 0.0)

    half = rows // 2
    code = jnp.concatenate([acc[:half, :], acc[half:, :]], axis=1).astype(BF16)
    for z in range(codes_ref.shape[0]):
        codes_ref[z] = code


def pair_kernel(order_ref, keep_ref, got_ref, out_ref):
    del order_ref
    out_ref[...] = (keep_ref[...] + got_ref[...].astype(F32)).astype(BF16)


def add_kernel(keep_ref, got_ref, across_ref, out_ref):
    total = keep_ref[...] + got_ref[...].astype(F32) + across_ref[...].astype(F32)
    out_ref[...] = total.astype(BF16)


def update_kernel(
    group_ref, store_ref, rows_ref, codes_ref, others_ref, up_ref, own_ref, *rest
):
    send_refs, (acc, group, store, index_sems) = rest[:-4], rest[-4:]
    indices = index_copies(group_ref, store_ref, group, store, index_sems)
    slots = group.shape[1]
    stored, rank, _ = up_ref.shape
    rows, block = own_ref.shape
    owners = lax.axis_size("owner")
    owner = lax.axis_index("owner")
    packed = codes_ref[0].astype(F32) + others_ref[0].astype(F32)
    for z in range(1, codes_ref.shape[0]):
        packed = packed + codes_ref[z].astype(F32) + others_ref[z].astype(F32)
    code = jnp.concatenate([packed[:, :rank], packed[:, rank:]], axis=0).astype(BF16).astype(F32)
    ids = row_adapters(rows_ref, rank)
    acc[...] = jnp.zeros_like(acc)
    for copy in indices:
        copy.wait()
    for s in range(slots):
        spot, here = slot_position(s, group, store, stored)

        @pl.when(here)
        def _(s=s, spot=spot):
            chosen = jnp.where(ids == group[0, s], code, 0.0).astype(BF16)
            acc[...] += jnp.dot(chosen, up_ref[spot], preferred_element_type=F32)

    def columns(target):
        return acc[:, pl.ds(pl.multiple_of(target * block, block), block)]

    own_ref[...] = columns(owner)
    for i, send_ref in enumerate(send_refs):
        send_ref[...] = columns(lax.rem(owner + i + 1, owners)).astype(BF16)


def final_kernel(parts_ref, own_ref, *rest):
    got_refs, out_ref = rest[:-1], rest[-1]
    base = parts_ref[0].astype(F32)
    for z in range(1, parts_ref.shape[0]):
        base = base + parts_ref[z].astype(F32)
    update = own_ref[...]
    for got_ref in got_refs:
        update = update + got_ref[...].astype(F32)
    out_ref[...] = (base + ADAPTER_SCALE * update).astype(BF16)


def shards(
    queries,
    cached_key_rows,
    cached_value_rows,
    newest_key,
    newest_value,
    output_weight,
    adapter_down_weight,
    adapter_up_weight,
    adapter_store_row,
    adapters_by_group,
    adapter_per_row,
):
    owners = lax.axis_size("owner")
    tensors = lax.axis_size("tensor")
    planes = tensors // 2
    slots = adapters_by_group.shape[1]
    row_count, local_heads, head_width = newest_key.shape
    rows = adapter_per_row.shape[0]
    feats = local_heads * output_weight.shape[1]
    columns = output_weight.shape[2]
    block = columns // (tensors * owners)
    rank = adapter_down_weight.shape[-1]
    row_ids = adapter_per_row.reshape(1, rows)
    group, store = far(adapters_by_group), far(adapter_store_row.reshape(1, -1))
    indices = [
        pltpu.SMEM(group.shape, jnp.int32),
        pltpu.SMEM(store.shape, jnp.int32),
        pltpu.SemaphoreType.DMA((2,)),
    ]

    slab = pltpu.VMEM((feats, columns // owners), BF16)
    positions = cached_value_rows.shape[1] * local_heads
    weight, local_queries, values, right, left = pl.pallas_call(
        slab_kernel,
        name="slabs",
        out_shape=(
            pltpu.VMEM((feats, columns), BF16),
            pltpu.VMEM(queries.shape, BF16),
            pltpu.VMEM((row_count, positions, head_width), BF16),
            slab,
            slab,
        ),
        in_specs=[HBM, HBM, HBM],
        out_specs=(VMEM,) * 5,
        scratch_shapes=[
            pltpu.SemaphoreType.DMA((feats // 16 + 1,)),
            pltpu.SemaphoreType.DMA((row_count,)),
        ],
        compiler_params=LIMIT,
    )(
        far(output_weight.reshape(feats, columns)),
        far(queries),
        far(cached_value_rows.reshape(row_count, positions, head_width)),
    )
    before = lax.ppermute(right, "owner", [(o, (o + 1) % owners) for o in range(owners)])
    after = lax.ppermute(left, "owner", [(o, (o - 1) % owners) for o in range(owners)])

    outgoing = pl.pallas_call(
        attend_kernel,
        name="attend",
        out_shape=pltpu.VMEM((owners, tensors, row_count, feats), BF16),
        in_specs=[VMEM] * 5,
        out_specs=VMEM,
        compiler_params=LIMIT,
    )(
        near(local_queries),
        near(cached_key_rows.reshape(row_count, positions, head_width)),
        near(values),
        newest_key,
        newest_value,
    )
    outgoing = outgoing.reshape(owners * tensors, row_count, feats)
    attention = lax.all_to_all(
        outgoing, ("owner", "tensor"), split_axis=0, concat_axis=0, tiled=True
    )
    attention = attention.reshape(owners, rows, feats)

    attention, down = near(attention), near(adapter_down_weight)
    swap = [(t, t ^ 1) for t in range(tensors)]
    kept, sent = pltpu.VMEM((planes, rows, block), F32), pltpu.VMEM((planes, rows, block), BF16)
    own_part, send_own, across_part, send_across = pl.pallas_call(
        project_kernel,
        name="project",
        out_shape=(kept, sent, kept, sent),
        in_specs=[VMEM] * 5,
        out_specs=(VMEM,) * 4,
        compiler_params=LIMIT,
    )(down, attention, near(weight), near(before), near(after))
    got_across = lax.ppermute(send_across, "tensor", swap)
    codes = pl.pallas_call(
        rank_kernel,
        name="rank",
        out_shape=pltpu.VMEM((planes, rows // 2, 2 * rank), BF16),
        in_specs=[HBM, HBM] + [VMEM] * 4,
        out_specs=VMEM,
        scratch_shapes=[pltpu.VMEM((rows, rank), F32)] + indices,
        compiler_params=LIMIT,
    )(group, store, row_ids, near(send_across), attention, down)
    across = pl.pallas_call(
        pair_kernel,
        name="pair",
        out_shape=sent,
        in_specs=[HBM, VMEM, VMEM],
        out_specs=VMEM,
        compiler_params=LIMIT,
    )(codes, near(across_part), near(got_across))
    across, send_own = lax.optimization_barrier((across, send_own))
    across = lax.ppermute(across, "owner", [(o, (o + 2) % owners) for o in range(owners)])
    got_own = lax.ppermute(send_own, "tensor", swap)
    groups = [[2 * z + c for z in range(planes)] for c in range(2)]

    def over_z(pieces):
        return lax.all_to_all(
            pieces, "tensor", split_axis=0, concat_axis=0, tiled=True, axis_index_groups=groups
        )

    codes = over_z(codes)
    other_codes = lax.ppermute(codes, "tensor", swap)
    strip = pltpu.VMEM((rows, block), BF16)
    own_update, *updates = pl.pallas_call(
        update_kernel,
        name="update",
        out_shape=(pltpu.VMEM((rows, block), F32),) + (strip,) * (owners - 1),
        in_specs=[HBM, HBM] + [VMEM] * 4,
        out_specs=(VMEM,) * owners,
        scratch_shapes=[pltpu.VMEM((rows, owners * block), F32)] + indices,
        compiler_params=LIMIT,
    )(group, store, row_ids, near(codes), near(other_codes), near(adapter_up_weight))
    updates = [
        lax.ppermute(update, "owner", [(o, (o + i + 1) % owners) for o in range(owners)])
        for i, update in enumerate(updates)
    ]
    parts = over_z(
        pl.pallas_call(
            add_kernel,
            name="add",
            out_shape=pltpu.VMEM((planes, rows, block), BF16),
            in_specs=[VMEM] * 3,
            out_specs=VMEM,
            compiler_params=LIMIT,
        )(near(own_part), near(got_own), near(across))
    )
    return pl.pallas_call(
        final_kernel,
        name="final",
        out_shape=jax.ShapeDtypeStruct((rows, block), BF16),
        in_specs=[VMEM] * (owners + 1),
        out_specs=VMEM,
        compiler_params=LIMIT,
    )(near(parts), near(own_update), *[near(update) for update in updates])


def solution(mesh):
    return jax.shard_map(
        shards,
        mesh=mesh,
        in_specs=(
            P(("dp", "tensor"), "owner"),
            P(("dp", "tensor"), None, "owner", None),
            P(("dp", "tensor"), None, "owner", None),
            P(("dp", "tensor"), "owner", None),
            P(("dp", "tensor"), "owner", None),
            P("owner", "tensor", None),
            P("owner", None, "tensor", None),
            P("owner", None, "tensor"),
            P(),
            P("dp", None),
            P("dp"),
        ),
        out_specs=P("dp", ("tensor", "owner")),
        check_vma=False,
    )
```

```python
import jax
import jax.numpy as jnp
from jax import lax
from jax.experimental import pallas as pl
from jax.experimental.pallas import tpu as pltpu
from jax.sharding import PartitionSpec as P

ADAPTER_SCALE = 2.0
BF16 = jnp.bfloat16
F32 = jnp.float32

VMEM = pl.BlockSpec(memory_space=pltpu.VMEM)
HBM = pl.BlockSpec(memory_space=pltpu.HBM)
LIMIT = pltpu.CompilerParams(vmem_limit_bytes=16 * 1024 * 1024)


def near(array):
    return pltpu.with_memory_space_constraint(array, pltpu.VMEM)


def far(array):
    return pltpu.with_memory_space_constraint(array, pltpu.HBM)


def slot_position(slot, group_ref, store_ref, stored):
    spot = store_ref[0, group_ref[0, slot]] - lax.axis_index("owner") * stored
    here = jnp.logical_and(spot >= 0, spot < stored)
    return jnp.clip(spot, 0, stored - 1), here


def index_copies(group_ref, store_ref, group, store, sems):
    copies = (
        pltpu.make_async_copy(group_ref, group, sems.at[0]),
        pltpu.make_async_copy(store_ref, store, sems.at[1]),
    )
    for copy in copies:
        copy.start()
    return copies


def row_adapters(rows_ref, width):
    rows = rows_ref.shape[1]
    return jnp.transpose(jnp.broadcast_to(rows_ref[...], (rows, rows)))[:, :width]


def column_copies(w_ref, out_ref, step, sems):
    owners = lax.axis_size("owner")
    target = lax.rem(lax.axis_index("owner") + step, owners)
    copies = []
    for block in range(out_ref.shape[1] // 128):
        at = pl.multiple_of((block * owners + target) * 128, 128)
        copies.append(
            pltpu.make_async_copy(
                w_ref.at[:, pl.ds(at, 128)],
                out_ref.at[:, pl.ds(block * 128, 128)],
                sems.at[block],
            )
        )
    return copies


def front_kernel(
    queries_hbm_ref,
    keys_hbm_ref,
    values_hbm_ref,
    w_ref,
    key_hbm_ref,
    value_hbm_ref,
    out_ref,
    right_ref,
    left_ref,
    queries_ref,
    keys_ref,
    values_ref,
    key_ref,
    value_ref,
    small_sems,
    key_sems,
    value_sems,
    right_sems,
    left_sems,
):
    copies = [
        pltpu.make_async_copy(queries_hbm_ref, queries_ref, small_sems.at[0]),
        pltpu.make_async_copy(key_hbm_ref, key_ref, small_sems.at[1]),
        pltpu.make_async_copy(value_hbm_ref, value_ref, small_sems.at[2]),
    ]
    for r in range(keys_ref.shape[0]):
        copies.append(pltpu.make_async_copy(keys_hbm_ref.at[r], keys_ref.at[r], key_sems.at[r]))
    later = [
        pltpu.make_async_copy(values_hbm_ref.at[r], values_ref.at[r], value_sems.at[r])
        for r in range(values_ref.shape[0])
    ]
    last = column_copies(w_ref, right_ref, 1, right_sems)
    last += column_copies(w_ref, left_ref, lax.axis_size("owner") - 1, left_sems)
    for copy in copies + later + last:
        copy.start()
    for copy in copies:
        copy.wait()
    rows, local, width = key_ref.shape
    heads = queries_ref.shape[1] // width
    grouped = heads // local
    positions = keys_ref.shape[1]
    scale = width ** (-0.5)
    queries = [queries_ref[:, h * width : (h + 1) * width].astype(F32) for h in range(heads)]
    queries = jnp.swapaxes(jnp.stack(queries), 0, 1)
    row_head = lax.broadcasted_iota(jnp.int32, (heads, positions), 0) // grouped
    place_head = lax.broadcasted_iota(jnp.int32, (heads, positions), 1) % local
    same = row_head == place_head

    def spread(ref, r):
        fresh = ref[r].astype(F32)
        parts = [jnp.broadcast_to(fresh[k : k + 1], (grouped, width)) for k in range(local)]
        return jnp.concatenate(parts, axis=0)

    weights, fresh_weights, denominators = [], [], []
    for r in range(rows):
        query = queries[r]
        scores = lax.dot_general(
            query.astype(BF16), keys_ref[r], (((1,), (1,)), ((), ())), preferred_element_type=F32
        )
        scores = jnp.where(same, scores * scale, -jnp.inf)
        fresh_score = jnp.sum(query * spread(key_ref, r), axis=1, keepdims=True) * scale
        overall = jnp.maximum(jnp.max(scores, axis=1, keepdims=True), fresh_score)
        weight = jnp.exp(scores - overall)
        fresh_weight = jnp.exp(fresh_score - overall)
        denominators.append(jnp.sum(weight, axis=1, keepdims=True) + fresh_weight)
        weights.append(weight.astype(BF16))
        fresh_weights.append(fresh_weight)
    for copy in later:
        copy.wait()
    mixed = []
    for r in range(rows):
        total = jnp.dot(weights[r], values_ref[r], preferred_element_type=F32)
        total = total + fresh_weights[r] * spread(value_ref, r)
        mixed.append(total / denominators[r])
    mixed = jnp.swapaxes(jnp.stack(mixed), 0, 1)

    half = width // 2
    low = lax.broadcasted_iota(jnp.int32, (rows, width), 1) < half
    for g in range(grouped):
        one, two = mixed[g], mixed[grouped + g]
        pair = (
            jnp.where(low, one, pltpu.roll(two, half, 1)),
            jnp.where(low, pltpu.roll(one, half, 1), two),
        )
        for i, part in enumerate(pair):
            part = part.astype(BF16)
            for o in range(out_ref.shape[0]):
                out_ref[o, 2 * g + i] = part
    for copy in last:
        copy.wait()


def project_kernel(
    group_ref,
    store_ref,
    rows_ref,
    att_ref,
    w_ref,
    before_ref,
    after_ref,
    down_ref,
    keep_ref,
    send_ref,
    acc,
    group,
    store,
    index_sems,
):
    indices = index_copies(group_ref, store_ref, group, store, index_sems)
    slots = group.shape[1]
    stored, _, _, rank = down_ref.shape
    owners, rows, feats = att_ref.shape
    owner = lax.axis_index("owner")
    mine = att_ref[owner]
    beside = jnp.concatenate(
        [att_ref[lax.rem(owner + owners - 1, owners)], att_ref[lax.rem(owner + 1, owners)]], axis=1
    )
    first = lax.rem(lax.axis_index("tensor"), 2) == 0
    block = keep_ref.shape[1]
    planes = before_ref.shape[1] // (2 * block)

    across = lax.rem(owner + 2, owners)

    def columns(z, target):
        at = [pl.multiple_of(((2 * z + c) * owners + target) * block, block) for c in range(2)]
        return jnp.concatenate([w_ref[:, pl.ds(a, block)] for a in at], axis=1)

    for z in range(planes):
        span = pl.ds(z * 2 * block, 2 * block)
        near_rows = jnp.concatenate([before_ref[:, span], after_ref[:, span]], axis=0)
        here = jnp.dot(beside, near_rows, preferred_element_type=F32)
        here = here + jnp.dot(mine, columns(z, owner), preferred_element_type=F32)
        there = jnp.dot(mine, columns(z, across), preferred_element_type=F32)
        for i, part in enumerate((here, there)):
            even, odd = part[:, :block], part[:, block:]
            rows_span = pl.ds((2 * z + i) * rows, rows)
            keep_ref[rows_span, :] = jnp.where(first, even, odd)
            send_ref[rows_span, :] = jnp.where(first, odd, even).astype(BF16)
    att = jnp.concatenate([att_ref[o] for o in range(owners)], axis=1)
    ids = row_adapters(rows_ref, rank)
    acc[...] = jnp.zeros_like(acc)
    for copy in indices:
        copy.wait()
    for s in range(slots):
        spot, here = slot_position(s, group, store, stored)

        @pl.when(here)
        def _(s=s, spot=spot):
            table = down_ref[spot].reshape(owners * feats, rank)
            code = jnp.dot(att, table, preferred_element_type=F32)
            acc[...] += jnp.where(ids == group[0, s], code, 0.0)

    half = rows // 2
    code = jnp.concatenate([acc[:half, :], acc[half:, :]], axis=1)
    keep_ref[2 * planes * rows :, :] = code
    send_ref[2 * planes * rows :, :] = code.astype(BF16)


def pair_kernel(keep_ref, got_ref, own_ref, across_ref, codes_ref):
    planes, rows, _ = own_ref.shape
    for z in range(planes):
        span = pl.ds(2 * z * rows, rows)
        own_ref[z] = keep_ref[span, :] + got_ref[span, :].astype(F32)
        span = pl.ds((2 * z + 1) * rows, rows)
        across_ref[z] = (keep_ref[span, :] + got_ref[span, :].astype(F32)).astype(BF16)
    span = pl.ds(2 * planes * rows, codes_ref.shape[1])
    code = (keep_ref[span, :] + got_ref[span, :].astype(F32)).astype(BF16)
    for z in range(planes):
        codes_ref[z] = code


def add_kernel(one_ref, two_ref, out_ref):
    out_ref[...] = (one_ref[...] + two_ref[...].astype(F32)).astype(BF16)


def update_kernel(group_ref, store_ref, rows_ref, codes_ref, up_ref, own_ref, *rest):
    send_refs, (acc, group, store, index_sems) = rest[:-4], rest[-4:]
    indices = index_copies(group_ref, store_ref, group, store, index_sems)
    slots = group.shape[1]
    stored, rank, _ = up_ref.shape
    rows, block = own_ref.shape
    owners = lax.axis_size("owner")
    owner = lax.axis_index("owner")
    packed = codes_ref[0].astype(F32)
    for z in range(1, codes_ref.shape[0]):
        packed = packed + codes_ref[z].astype(F32)
    code = jnp.concatenate([packed[:, :rank], packed[:, rank:]], axis=0).astype(BF16).astype(F32)
    ids = row_adapters(rows_ref, rank)
    acc[...] = jnp.zeros_like(acc)
    for copy in indices:
        copy.wait()
    for s in range(slots):
        spot, here = slot_position(s, group, store, stored)

        @pl.when(here)
        def _(s=s, spot=spot):
            chosen = jnp.where(ids == group[0, s], code, 0.0).astype(BF16)
            acc[...] += jnp.dot(chosen, up_ref[spot], preferred_element_type=F32)

    def columns(target):
        return acc[:, pl.ds(pl.multiple_of(target * block, block), block)]

    own_ref[...] = columns(owner)
    for i, send_ref in enumerate(send_refs):
        send_ref[...] = columns(lax.rem(owner + i + 1, owners)).astype(BF16)


def final_kernel(parts_ref, own_ref, *rest):
    got_refs, out_ref = rest[:-1], rest[-1]
    base = parts_ref[0].astype(F32)
    for z in range(1, parts_ref.shape[0]):
        base = base + parts_ref[z].astype(F32)
    update = own_ref[...]
    for got_ref in got_refs:
        update = update + got_ref[...].astype(F32)
    out_ref[...] = (base + ADAPTER_SCALE * update).astype(BF16)


def shards(
    queries,
    cached_key_rows,
    cached_value_rows,
    newest_key,
    newest_value,
    output_weight,
    adapter_down_weight,
    adapter_up_weight,
    adapter_store_row,
    adapters_by_group,
    adapter_per_row,
):
    owners = lax.axis_size("owner")
    tensors = lax.axis_size("tensor")
    planes = tensors // 2
    slots = adapters_by_group.shape[1]
    row_count, local_heads, head_width = newest_key.shape
    rows = adapter_per_row.shape[0]
    feats = local_heads * output_weight.shape[1]
    columns = output_weight.shape[2]
    block = columns // (tensors * owners)
    rank = adapter_down_weight.shape[-1]
    row_ids = adapter_per_row.reshape(1, rows)
    group, store = far(adapters_by_group), far(adapter_store_row.reshape(1, -1))
    indices = [
        pltpu.SMEM(group.shape, jnp.int32),
        pltpu.SMEM(store.shape, jnp.int32),
        pltpu.SemaphoreType.DMA((2,)),
    ]

    slab = pltpu.VMEM((feats, columns // owners), BF16)
    blocks = columns // owners // 128
    positions = cached_value_rows.shape[1] * local_heads
    cache = (row_count, positions, head_width)
    weight = output_weight.reshape(feats, columns)
    outgoing, right, left = pl.pallas_call(
        front_kernel,
        name="front",
        out_shape=(pltpu.VMEM((owners, tensors, row_count, feats), BF16), slab, slab),
        in_specs=[HBM] * 6,
        out_specs=(VMEM,) * 3,
        scratch_shapes=[
            pltpu.VMEM(queries.shape, BF16),
            pltpu.VMEM(cache, BF16),
            pltpu.VMEM(cache, BF16),
            pltpu.VMEM(newest_key.shape, BF16),
            pltpu.VMEM(newest_value.shape, BF16),
            pltpu.SemaphoreType.DMA((3,)),
            pltpu.SemaphoreType.DMA((row_count,)),
            pltpu.SemaphoreType.DMA((row_count,)),
            pltpu.SemaphoreType.DMA((blocks,)),
            pltpu.SemaphoreType.DMA((blocks,)),
        ],
        compiler_params=LIMIT,
    )(
        far(queries),
        far(cached_key_rows.reshape(cache)),
        far(cached_value_rows.reshape(cache)),
        far(weight),
        far(newest_key),
        far(newest_value),
    )
    before = lax.ppermute(right, "owner", [(o, (o + 1) % owners) for o in range(owners)])
    after = lax.ppermute(left, "owner", [(o, (o - 1) % owners) for o in range(owners)])
    outgoing = outgoing.reshape(owners * tensors, row_count, feats)
    attention = lax.all_to_all(
        outgoing, ("owner", "tensor"), split_axis=0, concat_axis=0, tiled=True
    )
    attention = attention.reshape(owners, rows, feats)

    tall = 2 * planes * rows + rows // 2
    keep, send = pl.pallas_call(
        project_kernel,
        name="project",
        out_shape=(pltpu.VMEM((tall, block), F32), pltpu.VMEM((tall, block), BF16)),
        in_specs=[HBM, HBM] + [VMEM] * 6,
        out_specs=(VMEM, VMEM),
        scratch_shapes=[pltpu.VMEM((rows, rank), F32)] + indices,
        compiler_params=LIMIT,
    )(
        group,
        store,
        row_ids,
        near(attention),
        weight,
        near(before),
        near(after),
        near(adapter_down_weight),
    )
    got = lax.ppermute(send, "tensor", [(t, t ^ 1) for t in range(tensors)])
    own_part, across, codes = pl.pallas_call(
        pair_kernel,
        name="pair",
        out_shape=(
            pltpu.VMEM((planes, rows, block), F32),
            pltpu.VMEM((planes, rows, block), BF16),
            pltpu.VMEM((planes, rows // 2, 2 * rank), BF16),
        ),
        in_specs=[VMEM, VMEM],
        out_specs=(VMEM, VMEM, VMEM),
        compiler_params=LIMIT,
    )(near(keep), near(got))
    groups = [[2 * z + c for z in range(planes)] for c in range(2)]

    def over_z(pieces):
        return lax.all_to_all(
            pieces, "tensor", split_axis=0, concat_axis=0, tiled=True, axis_index_groups=groups
        )

    across = lax.ppermute(across, "owner", [(o, (o + 2) % owners) for o in range(owners)])
    codes = over_z(codes)
    strip = pltpu.VMEM((rows, block), BF16)
    own_update, *updates = pl.pallas_call(
        update_kernel,
        name="update",
        out_shape=(pltpu.VMEM((rows, block), F32),) + (strip,) * (owners - 1),
        in_specs=[HBM, HBM] + [VMEM] * 3,
        out_specs=(VMEM,) * owners,
        scratch_shapes=[pltpu.VMEM((rows, owners * block), F32)] + indices,
        compiler_params=LIMIT,
    )(group, store, row_ids, near(codes), near(adapter_up_weight))
    updates = [
        lax.ppermute(update, "owner", [(o, (o + i + 1) % owners) for o in range(owners)])
        for i, update in enumerate(updates)
    ]
    parts = over_z(
        pl.pallas_call(
            add_kernel,
            name="add",
            out_shape=pltpu.VMEM((planes, rows, block), BF16),
            in_specs=[VMEM, VMEM],
            out_specs=VMEM,
            compiler_params=LIMIT,
        )(near(own_part), near(across))
    )
    return pl.pallas_call(
        final_kernel,
        name="final",
        out_shape=jax.ShapeDtypeStruct((rows, block), BF16),
        in_specs=[VMEM] * (owners + 1),
        out_specs=VMEM,
        compiler_params=LIMIT,
    )(near(parts), near(own_update), *[near(update) for update in updates])


def solution(mesh):
    return jax.shard_map(
        shards,
        mesh=mesh,
        in_specs=(
            P(("dp", "tensor"), "owner"),
            P(("dp", "tensor"), None, "owner", None),
            P(("dp", "tensor"), None, "owner", None),
            P(("dp", "tensor"), "owner", None),
            P(("dp", "tensor"), "owner", None),
            P("owner", "tensor", None),
            P("owner", None, "tensor", None),
            P("owner", None, "tensor"),
            P(),
            P("dp", None),
            P("dp"),
        ),
        out_specs=P("dp", ("tensor", "owner")),
        check_vma=False,
    )
```

```python
import jax
import jax.numpy as jnp
from jax import lax
from jax.experimental import pallas as pl
from jax.experimental.pallas import tpu as pltpu
from jax.sharding import PartitionSpec as P

ADAPTER_SCALE = 2.0
BF16 = jnp.bfloat16
F32 = jnp.float32

VMEM = pl.BlockSpec(memory_space=pltpu.VMEM)
HBM = pl.BlockSpec(memory_space=pltpu.HBM)
LIMIT = pltpu.CompilerParams(vmem_limit_bytes=16 * 1024 * 1024)


def near(array):
    return pltpu.with_memory_space_constraint(array, pltpu.VMEM)


def far(array):
    return pltpu.with_memory_space_constraint(array, pltpu.HBM)


def slot_position(slot, group_ref, store_ref, stored):
    spot = store_ref[0, group_ref[0, slot]] - lax.axis_index("owner") * stored
    here = jnp.logical_and(spot >= 0, spot < stored)
    return jnp.clip(spot, 0, stored - 1), here


def index_copies(group_ref, store_ref, group, store, sems):
    copies = (
        pltpu.make_async_copy(group_ref, group, sems.at[0]),
        pltpu.make_async_copy(store_ref, store, sems.at[1]),
    )
    for copy in copies:
        copy.start()
    return copies


def row_adapters(rows_ref, width):
    rows = rows_ref.shape[1]
    return jnp.transpose(jnp.broadcast_to(rows_ref[...], (rows, rows)))[:, :width]


def slab_kernel(
    w_hbm_ref,
    queries_hbm_ref,
    values_hbm_ref,
    w_ref,
    queries_ref,
    values_ref,
    right_ref,
    left_ref,
    sems,
    value_sems,
):
    chunks = sems.shape[0] - 1
    step = w_ref.shape[0] // chunks
    copies = [
        pltpu.make_async_copy(
            w_hbm_ref.at[pl.ds(i * step, step)], w_ref.at[pl.ds(i * step, step)], sems.at[i]
        )
        for i in range(chunks)
    ]
    rest = [pltpu.make_async_copy(queries_hbm_ref, queries_ref, sems.at[chunks])]
    rest += [
        pltpu.make_async_copy(values_hbm_ref.at[r], values_ref.at[r], value_sems.at[r])
        for r in range(values_ref.shape[0])
    ]
    for copy in copies + rest:
        copy.start()
    owner, owners = lax.axis_index("owner"), lax.axis_size("owner")
    targets = [lax.rem(owner + 1, owners), lax.rem(owner + owners - 1, owners)]
    for i in range(chunks):
        copies[i].wait()
        rows = pl.ds(i * step, step)
        for out_ref, target in zip((right_ref, left_ref), targets):
            for block in range(out_ref.shape[1] // 128):
                at = pl.multiple_of((block * owners + target) * 128, 128)
                out_ref[rows, block * 128 : (block + 1) * 128] = w_ref[rows, pl.ds(at, 128)]
    for copy in rest:
        copy.wait()


def attend_kernel(queries_ref, keys_ref, values_ref, key_ref, value_ref, out_ref):
    rows, local, width = key_ref.shape
    heads = queries_ref.shape[1] // width
    grouped = heads // local
    positions = keys_ref.shape[1]
    scale = width ** (-0.5)
    queries = [queries_ref[:, h * width : (h + 1) * width].astype(F32) for h in range(heads)]
    queries = jnp.swapaxes(jnp.stack(queries), 0, 1)
    row_head = lax.broadcasted_iota(jnp.int32, (heads, positions), 0) // grouped
    place_head = lax.broadcasted_iota(jnp.int32, (heads, positions), 1) % local
    same = row_head == place_head

    def spread(ref, r):
        fresh = ref[r].astype(F32)
        parts = [jnp.broadcast_to(fresh[k : k + 1], (grouped, width)) for k in range(local)]
        return jnp.concatenate(parts, axis=0)

    weights, fresh_weights, denominators = [], [], []
    for r in range(rows):
        query = queries[r]
        scores = lax.dot_general(
            query.astype(BF16), keys_ref[r], (((1,), (1,)), ((), ())), preferred_element_type=F32
        )
        scores = jnp.where(same, scores * scale, -jnp.inf)
        fresh_score = jnp.sum(query * spread(key_ref, r), axis=1, keepdims=True) * scale
        overall = jnp.maximum(jnp.max(scores, axis=1, keepdims=True), fresh_score)
        weight = jnp.exp(scores - overall)
        fresh_weight = jnp.exp(fresh_score - overall)
        denominators.append(jnp.sum(weight, axis=1, keepdims=True) + fresh_weight)
        weights.append(weight.astype(BF16))
        fresh_weights.append(fresh_weight)
    mixed = []
    for r in range(rows):
        total = jnp.dot(weights[r], values_ref[r], preferred_element_type=F32)
        total = total + fresh_weights[r] * spread(value_ref, r)
        mixed.append(total / denominators[r])
    mixed = jnp.swapaxes(jnp.stack(mixed), 0, 1)

    half = width // 2
    low = lax.broadcasted_iota(jnp.int32, (rows, width), 1) < half
    for g in range(grouped):
        one, two = mixed[g], mixed[grouped + g]
        pair = (
            jnp.where(low, one, pltpu.roll(two, half, 1)),
            jnp.where(low, pltpu.roll(one, half, 1), two),
        )
        for i, part in enumerate(pair):
            part = part.astype(BF16)
            for o in range(out_ref.shape[0]):
                out_ref[o, 2 * g + i] = part


def project_kernel(
    group_ref,
    store_ref,
    rows_ref,
    att_ref,
    w_ref,
    before_ref,
    after_ref,
    down_ref,
    own_ref,
    send_own_ref,
    keep_ref,
    send_ref,
    acc,
    group,
    store,
    index_sems,
):
    indices = index_copies(group_ref, store_ref, group, store, index_sems)
    slots = group.shape[1]
    stored, _, _, rank = down_ref.shape
    owners, rows, feats = att_ref.shape
    owner = lax.axis_index("owner")
    mine = att_ref[owner]
    beside = jnp.concatenate(
        [att_ref[lax.rem(owner + owners - 1, owners)], att_ref[lax.rem(owner + 1, owners)]], axis=1
    )
    first = lax.rem(lax.axis_index("tensor"), 2) == 0
    block = keep_ref.shape[1]
    planes = before_ref.shape[1] // (2 * block)

    across = lax.rem(owner + 2, owners)

    def columns(z, target):
        at = [pl.multiple_of(((2 * z + c) * owners + target) * block, block) for c in range(2)]
        return jnp.concatenate([w_ref[:, pl.ds(a, block)] for a in at], axis=1)

    for z in range(planes):
        span = pl.ds(z * 2 * block, 2 * block)
        near_rows = jnp.concatenate([before_ref[:, span], after_ref[:, span]], axis=0)
        here = jnp.dot(beside, near_rows, preferred_element_type=F32)
        here = here + jnp.dot(mine, columns(z, owner), preferred_element_type=F32)
        there = jnp.dot(mine, columns(z, across), preferred_element_type=F32)
        span = pl.ds(z * rows, rows)
        even, odd = here[:, :block], here[:, block:]
        own_ref[z] = jnp.where(first, even, odd).astype(BF16)
        send_own_ref[z] = jnp.where(first, odd, even).astype(BF16)
        even, odd = there[:, :block], there[:, block:]
        keep_ref[span, :] = jnp.where(first, even, odd)
        send_ref[span, :] = jnp.where(first, odd, even).astype(BF16)
    att = jnp.concatenate([att_ref[o] for o in range(owners)], axis=1)
    ids = row_adapters(rows_ref, rank)
    acc[...] = jnp.zeros_like(acc)
    for copy in indices:
        copy.wait()
    for s in range(slots):
        spot, here = slot_position(s, group, store, stored)

        @pl.when(here)
        def _(s=s, spot=spot):
            table = down_ref[spot].reshape(owners * feats, rank)
            code = jnp.dot(att, table, preferred_element_type=F32)
            acc[...] += jnp.where(ids == group[0, s], code, 0.0)

    half = rows // 2
    code = jnp.concatenate([acc[:half, :], acc[half:, :]], axis=1)
    keep_ref[planes * rows :, :] = code
    send_ref[planes * rows :, :] = code.astype(BF16)


def pair_kernel(keep_ref, got_ref, across_ref, codes_ref, code_ref, sems):
    planes, rows, _ = across_ref.shape
    span = pl.ds(planes * rows, code_ref.shape[0])
    code_ref[...] = (keep_ref[span, :] + got_ref[span, :].astype(F32)).astype(BF16)
    copies = [
        pltpu.make_async_copy(code_ref, codes_ref.at[z], sems.at[z]) for z in range(planes)
    ]
    for copy in copies:
        copy.start()
    for z in range(planes):
        span = pl.ds(z * rows, rows)
        across_ref[z] = (keep_ref[span, :] + got_ref[span, :].astype(F32)).astype(BF16)
    for copy in copies:
        copy.wait()


def add_kernel(keep_ref, got_ref, across_ref, out_ref):
    total = keep_ref[...].astype(F32) + got_ref[...].astype(F32)
    total = total + across_ref[...].astype(F32)
    out_ref[...] = total.astype(BF16)


def update_kernel(group_ref, store_ref, rows_ref, codes_ref, up_ref, own_ref, *rest):
    send_refs, (acc, group, store, index_sems) = rest[:-4], rest[-4:]
    indices = index_copies(group_ref, store_ref, group, store, index_sems)
    slots = group.shape[1]
    stored, rank, _ = up_ref.shape
    rows, block = own_ref.shape
    owners = lax.axis_size("owner")
    owner = lax.axis_index("owner")
    packed = codes_ref[0].astype(F32)
    for z in range(1, codes_ref.shape[0]):
        packed = packed + codes_ref[z].astype(F32)
    code = jnp.concatenate([packed[:, :rank], packed[:, rank:]], axis=0).astype(BF16).astype(F32)
    ids = row_adapters(rows_ref, rank)
    acc[...] = jnp.zeros_like(acc)
    for copy in indices:
        copy.wait()
    for s in range(slots):
        spot, here = slot_position(s, group, store, stored)

        @pl.when(here)
        def _(s=s, spot=spot):
            chosen = jnp.where(ids == group[0, s], code, 0.0).astype(BF16)
            acc[...] += jnp.dot(chosen, up_ref[spot], preferred_element_type=F32)

    def columns(target):
        return acc[:, pl.ds(pl.multiple_of(target * block, block), block)]

    own_ref[...] = columns(owner)
    for i, send_ref in enumerate(send_refs):
        send_ref[...] = columns(lax.rem(owner + i + 1, owners)).astype(BF16)


def final_kernel(parts_ref, own_ref, *rest):
    got_refs, out_ref = rest[:-1], rest[-1]
    base = parts_ref[0].astype(F32)
    for z in range(1, parts_ref.shape[0]):
        base = base + parts_ref[z].astype(F32)
    update = own_ref[...]
    for got_ref in got_refs:
        update = update + got_ref[...].astype(F32)
    out_ref[...] = (base + ADAPTER_SCALE * update).astype(BF16)


def shards(
    queries,
    cached_key_rows,
    cached_value_rows,
    newest_key,
    newest_value,
    output_weight,
    adapter_down_weight,
    adapter_up_weight,
    adapter_store_row,
    adapters_by_group,
    adapter_per_row,
):
    owners = lax.axis_size("owner")
    tensors = lax.axis_size("tensor")
    planes = tensors // 2
    slots = adapters_by_group.shape[1]
    row_count, local_heads, head_width = newest_key.shape
    rows = adapter_per_row.shape[0]
    feats = local_heads * output_weight.shape[1]
    columns = output_weight.shape[2]
    block = columns // (tensors * owners)
    rank = adapter_down_weight.shape[-1]
    row_ids = adapter_per_row.reshape(1, rows)
    group, store = far(adapters_by_group), far(adapter_store_row.reshape(1, -1))
    indices = [
        pltpu.SMEM(group.shape, jnp.int32),
        pltpu.SMEM(store.shape, jnp.int32),
        pltpu.SemaphoreType.DMA((2,)),
    ]

    slab = pltpu.VMEM((feats, columns // owners), BF16)
    positions = cached_value_rows.shape[1] * local_heads
    weight, local_queries, values, right, left = pl.pallas_call(
        slab_kernel,
        name="slabs",
        out_shape=(
            pltpu.VMEM((feats, columns), BF16),
            pltpu.VMEM(queries.shape, BF16),
            pltpu.VMEM((row_count, positions, head_width), BF16),
            slab,
            slab,
        ),
        in_specs=[HBM, HBM, HBM],
        out_specs=(VMEM,) * 5,
        scratch_shapes=[
            pltpu.SemaphoreType.DMA((feats // 16 + 1,)),
            pltpu.SemaphoreType.DMA((row_count,)),
        ],
        compiler_params=LIMIT,
    )(
        far(output_weight.reshape(feats, columns)),
        far(queries),
        far(cached_value_rows.reshape(row_count, positions, head_width)),
    )
    before = lax.ppermute(right, "owner", [(o, (o + 1) % owners) for o in range(owners)])
    after = lax.ppermute(left, "owner", [(o, (o - 1) % owners) for o in range(owners)])

    outgoing = pl.pallas_call(
        attend_kernel,
        name="attend",
        out_shape=pltpu.VMEM((owners, tensors, row_count, feats), BF16),
        in_specs=[VMEM] * 5,
        out_specs=VMEM,
        compiler_params=LIMIT,
    )(
        near(local_queries),
        near(cached_key_rows.reshape(row_count, positions, head_width)),
        near(values),
        newest_key,
        newest_value,
    )
    outgoing = outgoing.reshape(owners * tensors, row_count, feats)
    attention = lax.all_to_all(
        outgoing, ("owner", "tensor"), split_axis=0, concat_axis=0, tiled=True
    )
    attention = attention.reshape(owners, rows, feats)

    tall = planes * rows + rows // 2
    sent = pltpu.VMEM((planes, rows, block), BF16)
    own_part, send_own, keep, send = pl.pallas_call(
        project_kernel,
        name="project",
        out_shape=(
            sent,
            sent,
            pltpu.VMEM((tall, block), F32),
            pltpu.VMEM((tall, block), BF16),
        ),
        in_specs=[HBM, HBM] + [VMEM] * 6,
        out_specs=(VMEM,) * 4,
        scratch_shapes=[pltpu.VMEM((rows, rank), F32)] + indices,
        compiler_params=LIMIT,
    )(
        group,
        store,
        row_ids,
        near(attention),
        near(weight),
        near(before),
        near(after),
        near(adapter_down_weight),
    )
    swap = [(t, t ^ 1) for t in range(tensors)]
    got = lax.ppermute(send, "tensor", swap)
    lines = (rows // 2, 2 * rank)
    across, codes = pl.pallas_call(
        pair_kernel,
        name="pair",
        out_shape=(sent, pltpu.HBM((planes,) + lines, BF16)),
        in_specs=[VMEM, VMEM],
        out_specs=(VMEM, HBM),
        scratch_shapes=[pltpu.VMEM(lines, BF16), pltpu.SemaphoreType.DMA((planes,))],
        compiler_params=LIMIT,
    )(near(keep), near(got))
    groups = [[2 * z + c for z in range(planes)] for c in range(2)]

    def over_z(pieces):
        return lax.all_to_all(
            pieces, "tensor", split_axis=0, concat_axis=0, tiled=True, axis_index_groups=groups
        )

    across, send_own = lax.optimization_barrier((across, send_own))
    across = lax.ppermute(across, "owner", [(o, (o + 2) % owners) for o in range(owners)])
    codes = over_z(codes)
    got_own = lax.ppermute(send_own, "tensor", swap)
    strip = pltpu.VMEM((rows, block), BF16)
    own_update, *updates = pl.pallas_call(
        update_kernel,
        name="update",
        out_shape=(pltpu.VMEM((rows, block), F32),) + (strip,) * (owners - 1),
        in_specs=[HBM, HBM] + [VMEM] * 3,
        out_specs=(VMEM,) * owners,
        scratch_shapes=[pltpu.VMEM((rows, owners * block), F32)] + indices,
        compiler_params=LIMIT,
    )(group, store, row_ids, near(codes), near(adapter_up_weight))
    updates = [
        lax.ppermute(update, "owner", [(o, (o + i + 1) % owners) for o in range(owners)])
        for i, update in enumerate(updates)
    ]
    parts = over_z(
        pl.pallas_call(
            add_kernel,
            name="add",
            out_shape=pltpu.VMEM((planes, rows, block), BF16),
            in_specs=[VMEM] * 3,
            out_specs=VMEM,
            compiler_params=LIMIT,
        )(near(own_part), near(got_own), near(across))
    )
    return pl.pallas_call(
        final_kernel,
        name="final",
        out_shape=jax.ShapeDtypeStruct((rows, block), BF16),
        in_specs=[VMEM] * (owners + 1),
        out_specs=VMEM,
        compiler_params=LIMIT,
    )(near(parts), near(own_update), *[near(update) for update in updates])


def solution(mesh):
    return jax.shard_map(
        shards,
        mesh=mesh,
        in_specs=(
            P(("dp", "tensor"), "owner"),
            P(("dp", "tensor"), None, "owner", None),
            P(("dp", "tensor"), None, "owner", None),
            P(("dp", "tensor"), "owner", None),
            P(("dp", "tensor"), "owner", None),
            P("owner", "tensor", None),
            P("owner", None, "tensor", None),
            P("owner", None, "tensor"),
            P(),
            P("dp", None),
            P("dp"),
        ),
        out_specs=P("dp", ("tensor", "owner")),
        check_vma=False,
    )
```

```python
import jax
import jax.numpy as jnp
from jax import lax
from jax.experimental import pallas as pl
from jax.experimental.pallas import tpu as pltpu
from jax.sharding import PartitionSpec as P

ADAPTER_SCALE = 2.0
BF16 = jnp.bfloat16
F32 = jnp.float32

VMEM = pl.BlockSpec(memory_space=pltpu.VMEM)
HBM = pl.BlockSpec(memory_space=pltpu.HBM)
LIMIT = pltpu.CompilerParams(vmem_limit_bytes=16 * 1024 * 1024)


def near(array):
    return pltpu.with_memory_space_constraint(array, pltpu.VMEM)


def far(array):
    return pltpu.with_memory_space_constraint(array, pltpu.HBM)


def slot_position(slot, group_ref, store_ref, stored):
    spot = store_ref[0, group_ref[0, slot]] - lax.axis_index("owner") * stored
    here = jnp.logical_and(spot >= 0, spot < stored)
    return jnp.clip(spot, 0, stored - 1), here


def index_copies(group_ref, store_ref, group, store, sems):
    copies = (
        pltpu.make_async_copy(group_ref, group, sems.at[0]),
        pltpu.make_async_copy(store_ref, store, sems.at[1]),
    )
    for copy in copies:
        copy.start()
    return copies


def row_adapters(rows_ref, width):
    rows = rows_ref.shape[1]
    return jnp.transpose(jnp.broadcast_to(rows_ref[...], (rows, rows)))[:, :width]


def slab_kernel(
    w_hbm_ref,
    queries_hbm_ref,
    values_hbm_ref,
    w_ref,
    queries_ref,
    values_ref,
    right_ref,
    left_ref,
    sems,
    value_sems,
):
    chunks = sems.shape[0] - 1
    step = w_ref.shape[0] // chunks
    copies = [
        pltpu.make_async_copy(
            w_hbm_ref.at[pl.ds(i * step, step)], w_ref.at[pl.ds(i * step, step)], sems.at[i]
        )
        for i in range(chunks)
    ]
    rest = [pltpu.make_async_copy(queries_hbm_ref, queries_ref, sems.at[chunks])]
    rest += [
        pltpu.make_async_copy(values_hbm_ref.at[r], values_ref.at[r], value_sems.at[r])
        for r in range(values_ref.shape[0])
    ]
    for copy in copies + rest:
        copy.start()
    owner, owners = lax.axis_index("owner"), lax.axis_size("owner")
    targets = [lax.rem(owner + 1, owners), lax.rem(owner + owners - 1, owners)]
    for i in range(chunks):
        copies[i].wait()
        rows = pl.ds(i * step, step)
        for out_ref, target in zip((right_ref, left_ref), targets):
            for block in range(out_ref.shape[1] // 128):
                at = pl.multiple_of((block * owners + target) * 128, 128)
                out_ref[rows, block * 128 : (block + 1) * 128] = w_ref[rows, pl.ds(at, 128)]
    for copy in rest:
        copy.wait()


def attend_kernel(queries_ref, keys_ref, values_ref, key_ref, value_ref, out_ref):
    rows, local, width = key_ref.shape
    heads = queries_ref.shape[1] // width
    grouped = heads // local
    positions = keys_ref.shape[1]
    scale = width ** (-0.5)
    queries = [queries_ref[:, h * width : (h + 1) * width].astype(F32) for h in range(heads)]
    queries = jnp.swapaxes(jnp.stack(queries), 0, 1)
    row_head = lax.broadcasted_iota(jnp.int32, (heads, positions), 0) // grouped
    place_head = lax.broadcasted_iota(jnp.int32, (heads, positions), 1) % local
    same = row_head == place_head

    def spread(ref, r):
        fresh = ref[r].astype(F32)
        parts = [jnp.broadcast_to(fresh[k : k + 1], (grouped, width)) for k in range(local)]
        return jnp.concatenate(parts, axis=0)

    weights, fresh_weights, denominators = [], [], []
    for r in range(rows):
        query = queries[r]
        scores = lax.dot_general(
            query.astype(BF16), keys_ref[r], (((1,), (1,)), ((), ())), preferred_element_type=F32
        )
        scores = jnp.where(same, scores * scale, -jnp.inf)
        fresh_score = jnp.sum(query * spread(key_ref, r), axis=1, keepdims=True) * scale
        overall = jnp.maximum(jnp.max(scores, axis=1, keepdims=True), fresh_score)
        weight = jnp.exp(scores - overall)
        fresh_weight = jnp.exp(fresh_score - overall)
        denominators.append(jnp.sum(weight, axis=1, keepdims=True) + fresh_weight)
        weights.append(weight.astype(BF16))
        fresh_weights.append(fresh_weight)
    mixed = []
    for r in range(rows):
        total = jnp.dot(weights[r], values_ref[r], preferred_element_type=F32)
        total = total + fresh_weights[r] * spread(value_ref, r)
        mixed.append(total / denominators[r])
    mixed = jnp.swapaxes(jnp.stack(mixed), 0, 1)

    half = width // 2
    low = lax.broadcasted_iota(jnp.int32, (rows, width), 1) < half
    for g in range(grouped):
        one, two = mixed[g], mixed[grouped + g]
        pair = (
            jnp.where(low, one, pltpu.roll(two, half, 1)),
            jnp.where(low, pltpu.roll(one, half, 1), two),
        )
        for i, part in enumerate(pair):
            part = part.astype(BF16)
            for o in range(out_ref.shape[0]):
                out_ref[o, 2 * g + i] = part


def across_kernel(att_ref, w_ref, keep_ref, send_ref):
    owners = att_ref.shape[0]
    owner = lax.axis_index("owner")
    target = lax.rem(owner + 2, owners)
    mine = att_ref[owner]
    first = lax.rem(lax.axis_index("tensor"), 2) == 0
    planes, _, block = keep_ref.shape
    for z in range(planes):
        at = [pl.multiple_of(((2 * z + c) * owners + target) * block, block) for c in range(2)]
        columns = jnp.concatenate([w_ref[:, pl.ds(a, block)] for a in at], axis=1)
        part = jnp.dot(mine, columns, preferred_element_type=F32)
        even, odd = part[:, :block], part[:, block:]
        keep_ref[z] = jnp.where(first, even, odd)
        send_ref[z] = jnp.where(first, odd, even).astype(BF16)


def project_kernel(
    group_ref,
    store_ref,
    rows_ref,
    order_ref,
    att_ref,
    w_ref,
    before_ref,
    after_ref,
    down_ref,
    keep_ref,
    send_ref,
    acc,
    group,
    store,
    index_sems,
):
    del order_ref
    indices = index_copies(group_ref, store_ref, group, store, index_sems)
    slots = group.shape[1]
    stored, _, _, rank = down_ref.shape
    owners, rows, feats = att_ref.shape
    owner = lax.axis_index("owner")
    mine = att_ref[owner]
    beside = jnp.concatenate(
        [att_ref[lax.rem(owner + owners - 1, owners)], att_ref[lax.rem(owner + 1, owners)]], axis=1
    )
    first = lax.rem(lax.axis_index("tensor"), 2) == 0
    block = keep_ref.shape[1]
    planes = before_ref.shape[1] // (2 * block)


    def columns(z, target):
        at = [pl.multiple_of(((2 * z + c) * owners + target) * block, block) for c in range(2)]
        return jnp.concatenate([w_ref[:, pl.ds(a, block)] for a in at], axis=1)

    for z in range(planes):
        span = pl.ds(z * 2 * block, 2 * block)
        near_rows = jnp.concatenate([before_ref[:, span], after_ref[:, span]], axis=0)
        here = jnp.dot(beside, near_rows, preferred_element_type=F32)
        here = here + jnp.dot(mine, columns(z, owner), preferred_element_type=F32)
        even, odd = here[:, :block], here[:, block:]
        span = pl.ds(z * rows, rows)
        keep_ref[span, :] = jnp.where(first, even, odd)
        send_ref[span, :] = jnp.where(first, odd, even).astype(BF16)
    att = jnp.concatenate([att_ref[o] for o in range(owners)], axis=1)
    ids = row_adapters(rows_ref, rank)
    acc[...] = jnp.zeros_like(acc)
    for copy in indices:
        copy.wait()
    for s in range(slots):
        spot, here = slot_position(s, group, store, stored)

        @pl.when(here)
        def _(s=s, spot=spot):
            table = down_ref[spot].reshape(owners * feats, rank)
            code = jnp.dot(att, table, preferred_element_type=F32)
            acc[...] += jnp.where(ids == group[0, s], code, 0.0)

    half = rows // 2
    code = jnp.concatenate([acc[:half, :], acc[half:, :]], axis=1)
    keep_ref[planes * rows :, :] = code
    send_ref[planes * rows :, :] = code.astype(BF16)


def pair_across_kernel(keep_ref, got_ref, out_ref):
    out_ref[...] = (keep_ref[...] + got_ref[...].astype(F32)).astype(BF16)


def pair_kernel(keep_ref, got_ref, own_ref, codes_ref):
    planes, rows, _ = own_ref.shape
    for z in range(planes):
        span = pl.ds(z * rows, rows)
        own_ref[z] = keep_ref[span, :] + got_ref[span, :].astype(F32)
    span = pl.ds(planes * rows, codes_ref.shape[1])
    code = (keep_ref[span, :] + got_ref[span, :].astype(F32)).astype(BF16)
    for z in range(planes):
        codes_ref[z] = code


def add_kernel(one_ref, two_ref, out_ref):
    out_ref[...] = (one_ref[...] + two_ref[...].astype(F32)).astype(BF16)


def update_kernel(group_ref, store_ref, rows_ref, codes_ref, up_ref, own_ref, *rest):
    send_refs, (acc, group, store, index_sems) = rest[:-4], rest[-4:]
    indices = index_copies(group_ref, store_ref, group, store, index_sems)
    slots = group.shape[1]
    stored, rank, _ = up_ref.shape
    rows, block = own_ref.shape
    owners = lax.axis_size("owner")
    owner = lax.axis_index("owner")
    packed = codes_ref[0].astype(F32)
    for z in range(1, codes_ref.shape[0]):
        packed = packed + codes_ref[z].astype(F32)
    code = jnp.concatenate([packed[:, :rank], packed[:, rank:]], axis=0).astype(BF16).astype(F32)
    ids = row_adapters(rows_ref, rank)
    acc[...] = jnp.zeros_like(acc)
    for copy in indices:
        copy.wait()
    for s in range(slots):
        spot, here = slot_position(s, group, store, stored)

        @pl.when(here)
        def _(s=s, spot=spot):
            chosen = jnp.where(ids == group[0, s], code, 0.0).astype(BF16)
            acc[...] += jnp.dot(chosen, up_ref[spot], preferred_element_type=F32)

    def columns(target):
        return acc[:, pl.ds(pl.multiple_of(target * block, block), block)]

    own_ref[...] = columns(owner)
    for i, send_ref in enumerate(send_refs):
        send_ref[...] = columns(lax.rem(owner + i + 1, owners)).astype(BF16)


def final_kernel(parts_ref, own_ref, *rest):
    got_refs, out_ref = rest[:-1], rest[-1]
    base = parts_ref[0].astype(F32)
    for z in range(1, parts_ref.shape[0]):
        base = base + parts_ref[z].astype(F32)
    update = own_ref[...]
    for got_ref in got_refs:
        update = update + got_ref[...].astype(F32)
    out_ref[...] = (base + ADAPTER_SCALE * update).astype(BF16)


def shards(
    queries,
    cached_key_rows,
    cached_value_rows,
    newest_key,
    newest_value,
    output_weight,
    adapter_down_weight,
    adapter_up_weight,
    adapter_store_row,
    adapters_by_group,
    adapter_per_row,
):
    owners = lax.axis_size("owner")
    tensors = lax.axis_size("tensor")
    planes = tensors // 2
    slots = adapters_by_group.shape[1]
    row_count, local_heads, head_width = newest_key.shape
    rows = adapter_per_row.shape[0]
    feats = local_heads * output_weight.shape[1]
    columns = output_weight.shape[2]
    block = columns // (tensors * owners)
    rank = adapter_down_weight.shape[-1]
    row_ids = adapter_per_row.reshape(1, rows)
    group, store = far(adapters_by_group), far(adapter_store_row.reshape(1, -1))
    indices = [
        pltpu.SMEM(group.shape, jnp.int32),
        pltpu.SMEM(store.shape, jnp.int32),
        pltpu.SemaphoreType.DMA((2,)),
    ]

    slab = pltpu.VMEM((feats, columns // owners), BF16)
    positions = cached_value_rows.shape[1] * local_heads
    weight, local_queries, values, right, left = pl.pallas_call(
        slab_kernel,
        name="slabs",
        out_shape=(
            pltpu.VMEM((feats, columns), BF16),
            pltpu.VMEM(queries.shape, BF16),
            pltpu.VMEM((row_count, positions, head_width), BF16),
            slab,
            slab,
        ),
        in_specs=[HBM, HBM, HBM],
        out_specs=(VMEM,) * 5,
        scratch_shapes=[
            pltpu.SemaphoreType.DMA((feats // 16 + 1,)),
            pltpu.SemaphoreType.DMA((row_count,)),
        ],
        compiler_params=LIMIT,
    )(
        far(output_weight.reshape(feats, columns)),
        far(queries),
        far(cached_value_rows.reshape(row_count, positions, head_width)),
    )
    before = lax.ppermute(right, "owner", [(o, (o + 1) % owners) for o in range(owners)])
    after = lax.ppermute(left, "owner", [(o, (o - 1) % owners) for o in range(owners)])

    outgoing = pl.pallas_call(
        attend_kernel,
        name="attend",
        out_shape=pltpu.VMEM((owners, tensors, row_count, feats), BF16),
        in_specs=[VMEM] * 5,
        out_specs=VMEM,
        compiler_params=LIMIT,
    )(
        near(local_queries),
        near(cached_key_rows.reshape(row_count, positions, head_width)),
        near(values),
        newest_key,
        newest_value,
    )
    outgoing = outgoing.reshape(owners * tensors, row_count, feats)
    attention = lax.all_to_all(
        outgoing, ("owner", "tensor"), split_axis=0, concat_axis=0, tiled=True
    )
    attention = attention.reshape(owners, rows, feats)

    swap = [(t, t ^ 1) for t in range(tensors)]
    attention = near(attention)
    kept, sent = pltpu.VMEM((planes, rows, block), F32), pltpu.VMEM((planes, rows, block), BF16)
    keep_across, send_across = pl.pallas_call(
        across_kernel,
        name="across",
        out_shape=(kept, sent),
        in_specs=[VMEM, VMEM],
        out_specs=(VMEM, VMEM),
        compiler_params=LIMIT,
    )(attention, near(weight))
    got_across = lax.ppermute(send_across, "tensor", swap)
    tall = planes * rows + rows // 2
    keep, send = pl.pallas_call(
        project_kernel,
        name="project",
        out_shape=(pltpu.VMEM((tall, block), F32), pltpu.VMEM((tall, block), BF16)),
        in_specs=[HBM, HBM] + [VMEM] * 7,
        out_specs=(VMEM, VMEM),
        scratch_shapes=[pltpu.VMEM((rows, rank), F32)] + indices,
        compiler_params=LIMIT,
    )(
        group,
        store,
        row_ids,
        near(send_across),
        attention,
        near(weight),
        near(before),
        near(after),
        near(adapter_down_weight),
    )
    got = lax.ppermute(send, "tensor", swap)
    across = pl.pallas_call(
        pair_across_kernel,
        name="pair_across",
        out_shape=sent,
        in_specs=[VMEM, VMEM],
        out_specs=VMEM,
        compiler_params=LIMIT,
    )(near(keep_across), near(got_across))
    own_part, codes = pl.pallas_call(
        pair_kernel,
        name="pair",
        out_shape=(kept, pltpu.VMEM((planes, rows // 2, 2 * rank), BF16)),
        in_specs=[VMEM, VMEM],
        out_specs=(VMEM, VMEM),
        compiler_params=LIMIT,
    )(near(keep), near(got))
    groups = [[2 * z + c for z in range(planes)] for c in range(2)]

    def over_z(pieces):
        return lax.all_to_all(
            pieces, "tensor", split_axis=0, concat_axis=0, tiled=True, axis_index_groups=groups
        )

    across = lax.ppermute(across, "owner", [(o, (o + 2) % owners) for o in range(owners)])
    codes = over_z(codes)
    strip = pltpu.VMEM((rows, block), BF16)
    own_update, *updates = pl.pallas_call(
        update_kernel,
        name="update",
        out_shape=(pltpu.VMEM((rows, block), F32),) + (strip,) * (owners - 1),
        in_specs=[HBM, HBM] + [VMEM] * 3,
        out_specs=(VMEM,) * owners,
        scratch_shapes=[pltpu.VMEM((rows, owners * block), F32)] + indices,
        compiler_params=LIMIT,
    )(group, store, row_ids, near(codes), near(adapter_up_weight))
    updates = [
        lax.ppermute(update, "owner", [(o, (o + i + 1) % owners) for o in range(owners)])
        for i, update in enumerate(updates)
    ]
    parts = over_z(
        pl.pallas_call(
            add_kernel,
            name="add",
            out_shape=pltpu.VMEM((planes, rows, block), BF16),
            in_specs=[VMEM, VMEM],
            out_specs=VMEM,
            compiler_params=LIMIT,
        )(near(own_part), near(across))
    )
    return pl.pallas_call(
        final_kernel,
        name="final",
        out_shape=jax.ShapeDtypeStruct((rows, block), BF16),
        in_specs=[VMEM] * (owners + 1),
        out_specs=VMEM,
        compiler_params=LIMIT,
    )(near(parts), near(own_update), *[near(update) for update in updates])


def solution(mesh):
    return jax.shard_map(
        shards,
        mesh=mesh,
        in_specs=(
            P(("dp", "tensor"), "owner"),
            P(("dp", "tensor"), None, "owner", None),
            P(("dp", "tensor"), None, "owner", None),
            P(("dp", "tensor"), "owner", None),
            P(("dp", "tensor"), "owner", None),
            P("owner", "tensor", None),
            P("owner", None, "tensor", None),
            P("owner", None, "tensor"),
            P(),
            P("dp", None),
            P("dp"),
        ),
        out_specs=P("dp", ("tensor", "owner")),
        check_vma=False,
    )
```

```python
import jax
import jax.numpy as jnp
from jax import lax
from jax.experimental import pallas as pl
from jax.experimental.pallas import tpu as pltpu
from jax.sharding import PartitionSpec as P

ADAPTER_SCALE = 2.0
BF16 = jnp.bfloat16
F32 = jnp.float32

VMEM = pl.BlockSpec(memory_space=pltpu.VMEM)
HBM = pl.BlockSpec(memory_space=pltpu.HBM)
LIMIT = pltpu.CompilerParams(vmem_limit_bytes=16 * 1024 * 1024)


def near(array):
    return pltpu.with_memory_space_constraint(array, pltpu.VMEM)


def far(array):
    return pltpu.with_memory_space_constraint(array, pltpu.HBM)


def slot_position(slot, group_ref, store_ref, stored):
    spot = store_ref[0, group_ref[0, slot]] - lax.axis_index("owner") * stored
    here = jnp.logical_and(spot >= 0, spot < stored)
    return jnp.clip(spot, 0, stored - 1), here


def index_copies(group_ref, store_ref, group, store, sems):
    copies = (
        pltpu.make_async_copy(group_ref, group, sems.at[0]),
        pltpu.make_async_copy(store_ref, store, sems.at[1]),
    )
    for copy in copies:
        copy.start()
    return copies


def row_adapters(rows_ref, width):
    rows = rows_ref.shape[1]
    return jnp.transpose(jnp.broadcast_to(rows_ref[...], (rows, rows)))[:, :width]


def slab_kernel(
    w_hbm_ref,
    queries_hbm_ref,
    values_hbm_ref,
    w_ref,
    queries_ref,
    values_ref,
    right_ref,
    left_ref,
    sems,
    value_sems,
):
    chunks = sems.shape[0] - 1
    step = w_ref.shape[0] // chunks
    copies = [
        pltpu.make_async_copy(
            w_hbm_ref.at[pl.ds(i * step, step)], w_ref.at[pl.ds(i * step, step)], sems.at[i]
        )
        for i in range(chunks)
    ]
    rest = [pltpu.make_async_copy(queries_hbm_ref, queries_ref, sems.at[chunks])]
    rest += [
        pltpu.make_async_copy(values_hbm_ref.at[r], values_ref.at[r], value_sems.at[r])
        for r in range(values_ref.shape[0])
    ]
    for copy in copies + rest:
        copy.start()
    owner, owners = lax.axis_index("owner"), lax.axis_size("owner")
    targets = [lax.rem(owner + 1, owners), lax.rem(owner + owners - 1, owners)]
    for i in range(chunks):
        copies[i].wait()
        rows = pl.ds(i * step, step)
        for out_ref, target in zip((right_ref, left_ref), targets):
            for block in range(out_ref.shape[1] // 128):
                at = pl.multiple_of((block * owners + target) * 128, 128)
                out_ref[rows, block * 128 : (block + 1) * 128] = w_ref[rows, pl.ds(at, 128)]
    for copy in rest:
        copy.wait()


def attend_kernel(queries_ref, keys_ref, values_ref, key_ref, value_ref, out_ref):
    rows, local, width = key_ref.shape
    heads = queries_ref.shape[1] // width
    grouped = heads // local
    positions = keys_ref.shape[1]
    scale = width ** (-0.5)
    queries = [queries_ref[:, h * width : (h + 1) * width].astype(F32) for h in range(heads)]
    queries = jnp.swapaxes(jnp.stack(queries), 0, 1)
    row_head = lax.broadcasted_iota(jnp.int32, (heads, positions), 0) // grouped
    place_head = lax.broadcasted_iota(jnp.int32, (heads, positions), 1) % local
    same = row_head == place_head

    def spread(ref, r):
        fresh = ref[r].astype(F32)
        parts = [jnp.broadcast_to(fresh[k : k + 1], (grouped, width)) for k in range(local)]
        return jnp.concatenate(parts, axis=0)

    weights, fresh_weights, denominators = [], [], []
    for r in range(rows):
        query = queries[r]
        scores = lax.dot_general(
            query.astype(BF16), keys_ref[r], (((1,), (1,)), ((), ())), preferred_element_type=F32
        )
        scores = jnp.where(same, scores * scale, -jnp.inf)
        fresh_score = jnp.sum(query * spread(key_ref, r), axis=1, keepdims=True) * scale
        overall = jnp.maximum(jnp.max(scores, axis=1, keepdims=True), fresh_score)
        weight = jnp.exp(scores - overall)
        fresh_weight = jnp.exp(fresh_score - overall)
        denominators.append(jnp.sum(weight, axis=1, keepdims=True) + fresh_weight)
        weights.append(weight.astype(BF16))
        fresh_weights.append(fresh_weight)
    mixed = []
    for r in range(rows):
        total = jnp.dot(weights[r], values_ref[r], preferred_element_type=F32)
        total = total + fresh_weights[r] * spread(value_ref, r)
        mixed.append(total / denominators[r])
    mixed = jnp.swapaxes(jnp.stack(mixed), 0, 1)

    half = width // 2
    low = lax.broadcasted_iota(jnp.int32, (rows, width), 1) < half
    for g in range(grouped):
        one, two = mixed[g], mixed[grouped + g]
        pair = (
            jnp.where(low, one, pltpu.roll(two, half, 1)),
            jnp.where(low, pltpu.roll(one, half, 1), two),
        )
        for i, part in enumerate(pair):
            part = part.astype(BF16)
            for o in range(out_ref.shape[0]):
                out_ref[o, 2 * g + i] = part


def across_kernel(att_ref, w_ref, keep_ref, send_ref):
    owners = att_ref.shape[0]
    owner = lax.axis_index("owner")
    target = lax.rem(owner + 2, owners)
    mine = att_ref[owner]
    first = lax.rem(lax.axis_index("tensor"), 2) == 0
    planes, _, block = keep_ref.shape
    for z in range(planes):
        at = [pl.multiple_of(((2 * z + c) * owners + target) * block, block) for c in range(2)]
        columns = jnp.concatenate([w_ref[:, pl.ds(a, block)] for a in at], axis=1)
        part = jnp.dot(mine, columns, preferred_element_type=F32)
        even, odd = part[:, :block], part[:, block:]
        keep_ref[z] = jnp.where(first, even, odd)
        send_ref[z] = jnp.where(first, odd, even).astype(BF16)


def project_kernel(
    group_ref,
    store_ref,
    rows_ref,
    order_ref,
    att_ref,
    w_ref,
    before_ref,
    after_ref,
    down_ref,
    keep_ref,
    send_ref,
    acc,
    group,
    store,
    index_sems,
):
    del order_ref
    indices = index_copies(group_ref, store_ref, group, store, index_sems)
    slots = group.shape[1]
    stored, _, _, rank = down_ref.shape
    owners, rows, feats = att_ref.shape
    owner = lax.axis_index("owner")
    mine = att_ref[owner]
    beside = jnp.concatenate(
        [att_ref[lax.rem(owner + owners - 1, owners)], att_ref[lax.rem(owner + 1, owners)]], axis=1
    )
    first = lax.rem(lax.axis_index("tensor"), 2) == 0
    block = keep_ref.shape[1]
    planes = before_ref.shape[1] // (2 * block)


    def columns(z, target):
        at = [pl.multiple_of(((2 * z + c) * owners + target) * block, block) for c in range(2)]
        return jnp.concatenate([w_ref[:, pl.ds(a, block)] for a in at], axis=1)

    for z in range(planes):
        span = pl.ds(z * 2 * block, 2 * block)
        near_rows = jnp.concatenate([before_ref[:, span], after_ref[:, span]], axis=0)
        here = jnp.dot(beside, near_rows, preferred_element_type=F32)
        here = here + jnp.dot(mine, columns(z, owner), preferred_element_type=F32)
        even, odd = here[:, :block], here[:, block:]
        span = pl.ds(z * rows, rows)
        keep_ref[span, :] = jnp.where(first, even, odd).astype(BF16)
        send_ref[span, :] = jnp.where(first, odd, even).astype(BF16)
    att = jnp.concatenate([att_ref[o] for o in range(owners)], axis=1)
    ids = row_adapters(rows_ref, rank)
    acc[...] = jnp.zeros_like(acc)
    for copy in indices:
        copy.wait()
    for s in range(slots):
        spot, here = slot_position(s, group, store, stored)

        @pl.when(here)
        def _(s=s, spot=spot):
            table = down_ref[spot].reshape(owners * feats, rank)
            code = jnp.dot(att, table, preferred_element_type=F32)
            acc[...] += jnp.where(ids == group[0, s], code, 0.0)

    half = rows // 2
    code = jnp.concatenate([acc[:half, :], acc[half:, :]], axis=1)
    keep_ref[planes * rows :, :] = code.astype(BF16)
    send_ref[planes * rows :, :] = code.astype(BF16)


def pair_across_kernel(keep_ref, got_ref, out_ref):
    out_ref[...] = (keep_ref[...] + got_ref[...].astype(F32)).astype(BF16)


def pair_kernel(keep_ref, got_ref, codes_ref):
    span = pl.ds(keep_ref.shape[0] - codes_ref.shape[1], codes_ref.shape[1])
    code = (keep_ref[span, :].astype(F32) + got_ref[span, :].astype(F32)).astype(BF16)
    for z in range(codes_ref.shape[0]):
        codes_ref[z] = code


def add_kernel(keep_ref, got_ref, across_ref, out_ref):
    planes, rows, _ = out_ref.shape
    for z in range(planes):
        span = pl.ds(z * rows, rows)
        total = keep_ref[span, :].astype(F32) + got_ref[span, :].astype(F32)
        out_ref[z] = (total + across_ref[z].astype(F32)).astype(BF16)


def update_kernel(group_ref, store_ref, rows_ref, codes_ref, up_ref, own_ref, *rest):
    send_refs, (acc, group, store, index_sems) = rest[:-4], rest[-4:]
    indices = index_copies(group_ref, store_ref, group, store, index_sems)
    slots = group.shape[1]
    stored, rank, _ = up_ref.shape
    rows, block = own_ref.shape
    owners = lax.axis_size("owner")
    owner = lax.axis_index("owner")
    packed = codes_ref[0].astype(F32)
    for z in range(1, codes_ref.shape[0]):
        packed = packed + codes_ref[z].astype(F32)
    code = jnp.concatenate([packed[:, :rank], packed[:, rank:]], axis=0).astype(BF16).astype(F32)
    ids = row_adapters(rows_ref, rank)
    acc[...] = jnp.zeros_like(acc)
    for copy in indices:
        copy.wait()
    for s in range(slots):
        spot, here = slot_position(s, group, store, stored)

        @pl.when(here)
        def _(s=s, spot=spot):
            chosen = jnp.where(ids == group[0, s], code, 0.0).astype(BF16)
            acc[...] += jnp.dot(chosen, up_ref[spot], preferred_element_type=F32)

    def columns(target):
        return acc[:, pl.ds(pl.multiple_of(target * block, block), block)]

    own_ref[...] = columns(owner)
    for i, send_ref in enumerate(send_refs):
        send_ref[...] = columns(lax.rem(owner + i + 1, owners)).astype(BF16)


def final_kernel(parts_ref, own_ref, *rest):
    got_refs, out_ref = rest[:-1], rest[-1]
    base = parts_ref[0].astype(F32)
    for z in range(1, parts_ref.shape[0]):
        base = base + parts_ref[z].astype(F32)
    update = own_ref[...]
    for got_ref in got_refs:
        update = update + got_ref[...].astype(F32)
    out_ref[...] = (base + ADAPTER_SCALE * update).astype(BF16)


def shards(
    queries,
    cached_key_rows,
    cached_value_rows,
    newest_key,
    newest_value,
    output_weight,
    adapter_down_weight,
    adapter_up_weight,
    adapter_store_row,
    adapters_by_group,
    adapter_per_row,
):
    owners = lax.axis_size("owner")
    tensors = lax.axis_size("tensor")
    planes = tensors // 2
    slots = adapters_by_group.shape[1]
    row_count, local_heads, head_width = newest_key.shape
    rows = adapter_per_row.shape[0]
    feats = local_heads * output_weight.shape[1]
    columns = output_weight.shape[2]
    block = columns // (tensors * owners)
    rank = adapter_down_weight.shape[-1]
    row_ids = adapter_per_row.reshape(1, rows)
    group, store = far(adapters_by_group), far(adapter_store_row.reshape(1, -1))
    indices = [
        pltpu.SMEM(group.shape, jnp.int32),
        pltpu.SMEM(store.shape, jnp.int32),
        pltpu.SemaphoreType.DMA((2,)),
    ]

    slab = pltpu.VMEM((feats, columns // owners), BF16)
    positions = cached_value_rows.shape[1] * local_heads
    weight, local_queries, values, right, left = pl.pallas_call(
        slab_kernel,
        name="slabs",
        out_shape=(
            pltpu.VMEM((feats, columns), BF16),
            pltpu.VMEM(queries.shape, BF16),
            pltpu.VMEM((row_count, positions, head_width), BF16),
            slab,
            slab,
        ),
        in_specs=[HBM, HBM, HBM],
        out_specs=(VMEM,) * 5,
        scratch_shapes=[
            pltpu.SemaphoreType.DMA((feats // 16 + 1,)),
            pltpu.SemaphoreType.DMA((row_count,)),
        ],
        compiler_params=LIMIT,
    )(
        far(output_weight.reshape(feats, columns)),
        far(queries),
        far(cached_value_rows.reshape(row_count, positions, head_width)),
    )
    before = lax.ppermute(right, "owner", [(o, (o + 1) % owners) for o in range(owners)])
    after = lax.ppermute(left, "owner", [(o, (o - 1) % owners) for o in range(owners)])

    outgoing = pl.pallas_call(
        attend_kernel,
        name="attend",
        out_shape=pltpu.VMEM((owners, tensors, row_count, feats), BF16),
        in_specs=[VMEM] * 5,
        out_specs=VMEM,
        compiler_params=LIMIT,
    )(
        near(local_queries),
        near(cached_key_rows.reshape(row_count, positions, head_width)),
        near(values),
        newest_key,
        newest_value,
    )
    outgoing = outgoing.reshape(owners * tensors, row_count, feats)
    attention = lax.all_to_all(
        outgoing, ("owner", "tensor"), split_axis=0, concat_axis=0, tiled=True
    )
    attention = attention.reshape(owners, rows, feats)

    swap = [(t, t ^ 1) for t in range(tensors)]
    attention = near(attention)
    kept, sent = pltpu.VMEM((planes, rows, block), F32), pltpu.VMEM((planes, rows, block), BF16)
    keep_across, send_across = pl.pallas_call(
        across_kernel,
        name="across",
        out_shape=(kept, sent),
        in_specs=[VMEM, VMEM],
        out_specs=(VMEM, VMEM),
        compiler_params=LIMIT,
    )(attention, near(weight))
    got_across = lax.ppermute(send_across, "tensor", swap)
    tall = planes * rows + rows // 2
    keep, send = pl.pallas_call(
        project_kernel,
        name="project",
        out_shape=(pltpu.VMEM((tall, block), BF16), pltpu.VMEM((tall, block), BF16)),
        in_specs=[HBM, HBM] + [VMEM] * 7,
        out_specs=(VMEM, VMEM),
        scratch_shapes=[pltpu.VMEM((rows, rank), F32)] + indices,
        compiler_params=LIMIT,
    )(
        group,
        store,
        row_ids,
        near(send_across),
        attention,
        near(weight),
        near(before),
        near(after),
        near(adapter_down_weight),
    )
    got = lax.ppermute(send, "tensor", swap)
    across = pl.pallas_call(
        pair_across_kernel,
        name="pair_across",
        out_shape=sent,
        in_specs=[VMEM, VMEM],
        out_specs=VMEM,
        compiler_params=LIMIT,
    )(near(keep_across), near(got_across))
    codes = pl.pallas_call(
        pair_kernel,
        name="pair",
        out_shape=pltpu.VMEM((planes, rows // 2, 2 * rank), BF16),
        in_specs=[VMEM, VMEM],
        out_specs=VMEM,
        compiler_params=LIMIT,
    )(near(keep), near(got))
    groups = [[2 * z + c for z in range(planes)] for c in range(2)]

    def over_z(pieces):
        return lax.all_to_all(
            pieces, "tensor", split_axis=0, concat_axis=0, tiled=True, axis_index_groups=groups
        )

    across = lax.ppermute(across, "owner", [(o, (o + 2) % owners) for o in range(owners)])
    codes = over_z(codes)
    strip = pltpu.VMEM((rows, block), BF16)
    own_update, *updates = pl.pallas_call(
        update_kernel,
        name="update",
        out_shape=(pltpu.VMEM((rows, block), F32),) + (strip,) * (owners - 1),
        in_specs=[HBM, HBM] + [VMEM] * 3,
        out_specs=(VMEM,) * owners,
        scratch_shapes=[pltpu.VMEM((rows, owners * block), F32)] + indices,
        compiler_params=LIMIT,
    )(group, store, row_ids, near(codes), near(adapter_up_weight))
    updates = [
        lax.ppermute(update, "owner", [(o, (o + i + 1) % owners) for o in range(owners)])
        for i, update in enumerate(updates)
    ]
    parts = over_z(
        pl.pallas_call(
            add_kernel,
            name="add",
            out_shape=pltpu.VMEM((planes, rows, block), BF16),
            in_specs=[VMEM] * 3,
            out_specs=VMEM,
            compiler_params=LIMIT,
        )(near(keep), near(got), near(across))
    )
    return pl.pallas_call(
        final_kernel,
        name="final",
        out_shape=jax.ShapeDtypeStruct((rows, block), BF16),
        in_specs=[VMEM] * (owners + 1),
        out_specs=VMEM,
        compiler_params=LIMIT,
    )(near(parts), near(own_update), *[near(update) for update in updates])


def solution(mesh):
    return jax.shard_map(
        shards,
        mesh=mesh,
        in_specs=(
            P(("dp", "tensor"), "owner"),
            P(("dp", "tensor"), None, "owner", None),
            P(("dp", "tensor"), None, "owner", None),
            P(("dp", "tensor"), "owner", None),
            P(("dp", "tensor"), "owner", None),
            P("owner", "tensor", None),
            P("owner", None, "tensor", None),
            P("owner", None, "tensor"),
            P(),
            P("dp", None),
            P("dp"),
        ),
        out_specs=P("dp", ("tensor", "owner")),
        check_vma=False,
    )
```

```python
import jax
import jax.numpy as jnp
from jax import lax
from jax.experimental import pallas as pl
from jax.experimental.pallas import tpu as pltpu
from jax.sharding import PartitionSpec as P

ADAPTER_SCALE = 2.0
STEPS = (2, 1, 3)
BF16 = jnp.bfloat16
F32 = jnp.float32

VMEM = pl.BlockSpec(memory_space=pltpu.VMEM)
HBM = pl.BlockSpec(memory_space=pltpu.HBM)
LIMIT = pltpu.CompilerParams(vmem_limit_bytes=16 * 1024 * 1024)


def near(array):
    return pltpu.with_memory_space_constraint(array, pltpu.VMEM)


def far(array):
    return pltpu.with_memory_space_constraint(array, pltpu.HBM)


def slot_position(slot, group_ref, store_ref, stored):
    spot = store_ref[0, group_ref[0, slot]] - lax.axis_index("owner") * stored
    here = jnp.logical_and(spot >= 0, spot < stored)
    return jnp.clip(spot, 0, stored - 1), here


def index_copies(group_ref, store_ref, group, store, sems):
    copies = (
        pltpu.make_async_copy(group_ref, group, sems.at[0]),
        pltpu.make_async_copy(store_ref, store, sems.at[1]),
    )
    for copy in copies:
        copy.start()
    return copies


def row_adapters(rows_ref, width):
    rows = rows_ref.shape[1]
    return jnp.transpose(jnp.broadcast_to(rows_ref[...], (rows, rows)))[:, :width]


def slab_kernel(
    w_hbm_ref,
    queries_hbm_ref,
    values_hbm_ref,
    w_ref,
    queries_ref,
    values_ref,
    right_ref,
    left_ref,
    sems,
    value_sems,
):
    chunks = sems.shape[0] - 1
    step = w_ref.shape[0] // chunks
    copies = [
        pltpu.make_async_copy(
            w_hbm_ref.at[pl.ds(i * step, step)], w_ref.at[pl.ds(i * step, step)], sems.at[i]
        )
        for i in range(chunks)
    ]
    rest = [pltpu.make_async_copy(queries_hbm_ref, queries_ref, sems.at[chunks])]
    rest += [
        pltpu.make_async_copy(values_hbm_ref.at[r], values_ref.at[r], value_sems.at[r])
        for r in range(values_ref.shape[0])
    ]
    for copy in copies + rest:
        copy.start()
    owner, owners = lax.axis_index("owner"), lax.axis_size("owner")
    targets = [lax.rem(owner + 1, owners), lax.rem(owner + owners - 1, owners)]
    for i in range(chunks):
        copies[i].wait()
        rows = pl.ds(i * step, step)
        for out_ref, target in zip((right_ref, left_ref), targets):
            for block in range(out_ref.shape[1] // 128):
                at = pl.multiple_of((block * owners + target) * 128, 128)
                out_ref[rows, block * 128 : (block + 1) * 128] = w_ref[rows, pl.ds(at, 128)]
    for copy in rest:
        copy.wait()


def attend_kernel(queries_ref, keys_ref, values_ref, key_ref, value_ref, out_ref):
    rows, local, width = key_ref.shape
    heads = queries_ref.shape[1] // width
    grouped = heads // local
    positions = keys_ref.shape[1]
    scale = width ** (-0.5)
    queries = [queries_ref[:, h * width : (h + 1) * width].astype(F32) for h in range(heads)]
    queries = jnp.swapaxes(jnp.stack(queries), 0, 1)
    row_head = lax.broadcasted_iota(jnp.int32, (heads, positions), 0) // grouped
    place_head = lax.broadcasted_iota(jnp.int32, (heads, positions), 1) % local
    same = row_head == place_head

    def spread(ref, r):
        fresh = ref[r].astype(F32)
        parts = [jnp.broadcast_to(fresh[k : k + 1], (grouped, width)) for k in range(local)]
        return jnp.concatenate(parts, axis=0)

    weights, fresh_weights, denominators = [], [], []
    for r in range(rows):
        query = queries[r]
        scores = lax.dot_general(
            query.astype(BF16), keys_ref[r], (((1,), (1,)), ((), ())), preferred_element_type=F32
        )
        scores = jnp.where(same, scores * scale, -jnp.inf)
        fresh_score = jnp.sum(query * spread(key_ref, r), axis=1, keepdims=True) * scale
        overall = jnp.maximum(jnp.max(scores, axis=1, keepdims=True), fresh_score)
        weight = jnp.exp(scores - overall)
        fresh_weight = jnp.exp(fresh_score - overall)
        denominators.append(jnp.sum(weight, axis=1, keepdims=True) + fresh_weight)
        weights.append(weight.astype(BF16))
        fresh_weights.append(fresh_weight)
    mixed = []
    for r in range(rows):
        total = jnp.dot(weights[r], values_ref[r], preferred_element_type=F32)
        total = total + fresh_weights[r] * spread(value_ref, r)
        mixed.append(total / denominators[r])
    mixed = jnp.swapaxes(jnp.stack(mixed), 0, 1)

    half = width // 2
    low = lax.broadcasted_iota(jnp.int32, (rows, width), 1) < half
    for g in range(grouped):
        one, two = mixed[g], mixed[grouped + g]
        pair = (
            jnp.where(low, one, pltpu.roll(two, half, 1)),
            jnp.where(low, pltpu.roll(one, half, 1), two),
        )
        for i, part in enumerate(pair):
            part = part.astype(BF16)
            for o in range(out_ref.shape[0]):
                out_ref[o, 2 * g + i] = part


def across_kernel(att_ref, w_ref, keep_ref, send_ref):
    owners = att_ref.shape[0]
    owner = lax.axis_index("owner")
    target = lax.rem(owner + 2, owners)
    mine = att_ref[owner]
    first = lax.rem(lax.axis_index("tensor"), 2) == 0
    planes, _, block = keep_ref.shape
    for z in range(planes):
        at = [pl.multiple_of(((2 * z + c) * owners + target) * block, block) for c in range(2)]
        columns = jnp.concatenate([w_ref[:, pl.ds(a, block)] for a in at], axis=1)
        part = jnp.dot(mine, columns, preferred_element_type=F32)
        even, odd = part[:, :block], part[:, block:]
        keep_ref[z] = jnp.where(first, even, odd)
        send_ref[z] = jnp.where(first, odd, even).astype(BF16)


def project_kernel(
    group_ref,
    store_ref,
    rows_ref,
    order_ref,
    att_ref,
    w_ref,
    before_ref,
    after_ref,
    down_ref,
    keep_ref,
    send_ref,
    acc,
    group,
    store,
    index_sems,
):
    del order_ref
    indices = index_copies(group_ref, store_ref, group, store, index_sems)
    slots = group.shape[1]
    stored, _, _, rank = down_ref.shape
    owners, rows, feats = att_ref.shape
    owner = lax.axis_index("owner")
    mine = att_ref[owner]
    beside = jnp.concatenate(
        [att_ref[lax.rem(owner + owners - 1, owners)], att_ref[lax.rem(owner + 1, owners)]], axis=1
    )
    first = lax.rem(lax.axis_index("tensor"), 2) == 0
    block = keep_ref.shape[1]
    planes = before_ref.shape[1] // (2 * block)


    def columns(z, target):
        at = [pl.multiple_of(((2 * z + c) * owners + target) * block, block) for c in range(2)]
        return jnp.concatenate([w_ref[:, pl.ds(a, block)] for a in at], axis=1)

    for z in range(planes):
        span = pl.ds(z * 2 * block, 2 * block)
        near_rows = jnp.concatenate([before_ref[:, span], after_ref[:, span]], axis=0)
        here = jnp.dot(beside, near_rows, preferred_element_type=F32)
        here = here + jnp.dot(mine, columns(z, owner), preferred_element_type=F32)
        even, odd = here[:, :block], here[:, block:]
        span = pl.ds(z * rows, rows)
        keep_ref[span, :] = jnp.where(first, even, odd)
        send_ref[span, :] = jnp.where(first, odd, even).astype(BF16)
    att = jnp.concatenate([att_ref[o] for o in range(owners)], axis=1)
    ids = row_adapters(rows_ref, rank)
    acc[...] = jnp.zeros_like(acc)
    for copy in indices:
        copy.wait()
    for s in range(slots):
        spot, here = slot_position(s, group, store, stored)

        @pl.when(here)
        def _(s=s, spot=spot):
            table = down_ref[spot].reshape(owners * feats, rank)
            code = jnp.dot(att, table, preferred_element_type=F32)
            acc[...] += jnp.where(ids == group[0, s], code, 0.0)

    half = rows // 2
    code = jnp.concatenate([acc[:half, :], acc[half:, :]], axis=1)
    keep_ref[planes * rows :, :] = code
    send_ref[planes * rows :, :] = code.astype(BF16)


def pair_across_kernel(keep_ref, got_ref, out_ref):
    out_ref[...] = (keep_ref[...] + got_ref[...].astype(F32)).astype(BF16)


def pair_kernel(keep_ref, got_ref, own_ref, codes_ref):
    planes, rows, _ = own_ref.shape
    for z in range(planes):
        span = pl.ds(z * rows, rows)
        own_ref[z] = keep_ref[span, :] + got_ref[span, :].astype(F32)
    span = pl.ds(planes * rows, codes_ref.shape[1])
    code = (keep_ref[span, :] + got_ref[span, :].astype(F32)).astype(BF16)
    for z in range(planes):
        codes_ref[z] = code


def add_kernel(one_ref, two_ref, out_ref):
    out_ref[...] = (one_ref[...] + two_ref[...].astype(F32)).astype(BF16)


def update_kernel(group_ref, store_ref, rows_ref, codes_ref, up_ref, own_ref, *rest):
    send_refs, (acc, group, store, index_sems) = rest[:-4], rest[-4:]
    indices = index_copies(group_ref, store_ref, group, store, index_sems)
    slots = group.shape[1]
    stored, rank, _ = up_ref.shape
    rows, block = own_ref.shape
    owners = lax.axis_size("owner")
    owner = lax.axis_index("owner")
    packed = codes_ref[0].astype(F32)
    for z in range(1, codes_ref.shape[0]):
        packed = packed + codes_ref[z].astype(F32)
    code = jnp.concatenate([packed[:, :rank], packed[:, rank:]], axis=0).astype(BF16).astype(F32)
    ids = row_adapters(rows_ref, rank)
    acc[...] = jnp.zeros_like(acc)
    for copy in indices:
        copy.wait()
    for s in range(slots):
        spot, here = slot_position(s, group, store, stored)

        @pl.when(here)
        def _(s=s, spot=spot):
            chosen = jnp.where(ids == group[0, s], code, 0.0).astype(BF16)
            acc[...] += jnp.dot(chosen, up_ref[spot], preferred_element_type=F32)

    def columns(target):
        return acc[:, pl.ds(pl.multiple_of(target * block, block), block)]

    own_ref[...] = columns(owner)
    for i, send_ref in enumerate(send_refs):
        send_ref[...] = columns(lax.rem(owner + STEPS[i], owners)).astype(BF16)


def final_kernel(parts_ref, own_ref, *rest):
    got_refs, out_ref = rest[:-1], rest[-1]
    base = parts_ref[0].astype(F32)
    for z in range(1, parts_ref.shape[0]):
        base = base + parts_ref[z].astype(F32)
    update = own_ref[...]
    for got_ref in got_refs:
        update = update + got_ref[...].astype(F32)
    out_ref[...] = (base + ADAPTER_SCALE * update).astype(BF16)


def shards(
    queries,
    cached_key_rows,
    cached_value_rows,
    newest_key,
    newest_value,
    output_weight,
    adapter_down_weight,
    adapter_up_weight,
    adapter_store_row,
    adapters_by_group,
    adapter_per_row,
):
    owners = lax.axis_size("owner")
    tensors = lax.axis_size("tensor")
    planes = tensors // 2
    slots = adapters_by_group.shape[1]
    row_count, local_heads, head_width = newest_key.shape
    rows = adapter_per_row.shape[0]
    feats = local_heads * output_weight.shape[1]
    columns = output_weight.shape[2]
    block = columns // (tensors * owners)
    rank = adapter_down_weight.shape[-1]
    row_ids = adapter_per_row.reshape(1, rows)
    group, store = far(adapters_by_group), far(adapter_store_row.reshape(1, -1))
    indices = [
        pltpu.SMEM(group.shape, jnp.int32),
        pltpu.SMEM(store.shape, jnp.int32),
        pltpu.SemaphoreType.DMA((2,)),
    ]

    slab = pltpu.VMEM((feats, columns // owners), BF16)
    positions = cached_value_rows.shape[1] * local_heads
    weight, local_queries, values, right, left = pl.pallas_call(
        slab_kernel,
        name="slabs",
        out_shape=(
            pltpu.VMEM((feats, columns), BF16),
            pltpu.VMEM(queries.shape, BF16),
            pltpu.VMEM((row_count, positions, head_width), BF16),
            slab,
            slab,
        ),
        in_specs=[HBM, HBM, HBM],
        out_specs=(VMEM,) * 5,
        scratch_shapes=[
            pltpu.SemaphoreType.DMA((feats // 16 + 1,)),
            pltpu.SemaphoreType.DMA((row_count,)),
        ],
        compiler_params=LIMIT,
    )(
        far(output_weight.reshape(feats, columns)),
        far(queries),
        far(cached_value_rows.reshape(row_count, positions, head_width)),
    )
    before = lax.ppermute(right, "owner", [(o, (o + 1) % owners) for o in range(owners)])
    after = lax.ppermute(left, "owner", [(o, (o - 1) % owners) for o in range(owners)])

    outgoing = pl.pallas_call(
        attend_kernel,
        name="attend",
        out_shape=pltpu.VMEM((owners, tensors, row_count, feats), BF16),
        in_specs=[VMEM] * 5,
        out_specs=VMEM,
        compiler_params=LIMIT,
    )(
        near(local_queries),
        near(cached_key_rows.reshape(row_count, positions, head_width)),
        near(values),
        newest_key,
        newest_value,
    )
    outgoing = outgoing.reshape(owners * tensors, row_count, feats)
    attention = lax.all_to_all(
        outgoing, ("owner", "tensor"), split_axis=0, concat_axis=0, tiled=True
    )
    attention = attention.reshape(owners, rows, feats)

    swap = [(t, t ^ 1) for t in range(tensors)]
    attention = near(attention)
    kept, sent = pltpu.VMEM((planes, rows, block), F32), pltpu.VMEM((planes, rows, block), BF16)
    keep_across, send_across = pl.pallas_call(
        across_kernel,
        name="across",
        out_shape=(kept, sent),
        in_specs=[VMEM, VMEM],
        out_specs=(VMEM, VMEM),
        compiler_params=LIMIT,
    )(attention, near(weight))
    got_across = lax.ppermute(send_across, "tensor", swap)
    tall = planes * rows + rows // 2
    keep, send = pl.pallas_call(
        project_kernel,
        name="project",
        out_shape=(pltpu.VMEM((tall, block), F32), pltpu.VMEM((tall, block), BF16)),
        in_specs=[HBM, HBM] + [VMEM] * 7,
        out_specs=(VMEM, VMEM),
        scratch_shapes=[pltpu.VMEM((rows, rank), F32)] + indices,
        compiler_params=LIMIT,
    )(
        group,
        store,
        row_ids,
        near(send_across),
        attention,
        near(weight),
        near(before),
        near(after),
        near(adapter_down_weight),
    )
    got = lax.ppermute(send, "tensor", swap)
    across = pl.pallas_call(
        pair_across_kernel,
        name="pair_across",
        out_shape=sent,
        in_specs=[VMEM, VMEM],
        out_specs=VMEM,
        compiler_params=LIMIT,
    )(near(keep_across), near(got_across))
    own_part, codes = pl.pallas_call(
        pair_kernel,
        name="pair",
        out_shape=(kept, pltpu.VMEM((planes, rows // 2, 2 * rank), BF16)),
        in_specs=[VMEM, VMEM],
        out_specs=(VMEM, VMEM),
        compiler_params=LIMIT,
    )(near(keep), near(got))
    groups = [[2 * z + c for z in range(planes)] for c in range(2)]

    def over_z(pieces):
        return lax.all_to_all(
            pieces, "tensor", split_axis=0, concat_axis=0, tiled=True, axis_index_groups=groups
        )

    across = lax.ppermute(across, "owner", [(o, (o + 2) % owners) for o in range(owners)])
    codes = over_z(codes)
    strip = pltpu.VMEM((rows, block), BF16)
    own_update, *updates = pl.pallas_call(
        update_kernel,
        name="update",
        out_shape=(pltpu.VMEM((rows, block), F32),) + (strip,) * (owners - 1),
        in_specs=[HBM, HBM] + [VMEM] * 3,
        out_specs=(VMEM,) * owners,
        scratch_shapes=[pltpu.VMEM((rows, owners * block), F32)] + indices,
        compiler_params=LIMIT,
    )(group, store, row_ids, near(codes), near(adapter_up_weight))
    updates = [
        lax.ppermute(update, "owner", [(o, (o + STEPS[i]) % owners) for o in range(owners)])
        for i, update in enumerate(updates)
    ]
    parts = over_z(
        pl.pallas_call(
            add_kernel,
            name="add",
            out_shape=pltpu.VMEM((planes, rows, block), BF16),
            in_specs=[VMEM, VMEM],
            out_specs=VMEM,
            compiler_params=LIMIT,
        )(near(own_part), near(across))
    )
    return pl.pallas_call(
        final_kernel,
        name="final",
        out_shape=jax.ShapeDtypeStruct((rows, block), BF16),
        in_specs=[VMEM] * (owners + 1),
        out_specs=VMEM,
        compiler_params=LIMIT,
    )(near(parts), near(own_update), *[near(update) for update in updates])


def solution(mesh):
    return jax.shard_map(
        shards,
        mesh=mesh,
        in_specs=(
            P(("dp", "tensor"), "owner"),
            P(("dp", "tensor"), None, "owner", None),
            P(("dp", "tensor"), None, "owner", None),
            P(("dp", "tensor"), "owner", None),
            P(("dp", "tensor"), "owner", None),
            P("owner", "tensor", None),
            P("owner", None, "tensor", None),
            P("owner", None, "tensor"),
            P(),
            P("dp", None),
            P("dp"),
        ),
        out_specs=P("dp", ("tensor", "owner")),
        check_vma=False,
    )
```
